32 devices in a mesh: dp: 8 (over z, y), section: 4 (over x, core).
Axes of the slice: x: 2, y: 2, z: 4, core: 2. Of those that a mesh axis runs over, the one named last changes fastest.
Arguments:
- tokens: bfloat16 [8192, 768], P(('dp', 'section')), may hold values from -6 to 6
- cotangent: bfloat16 [8192, 768], P(('dp', 'section')), may hold values from -6 to 6
- section_weight: bfloat16 [4, 768, 2304], P('section')
- norm_gain: float32 [4, 768], P('section'), may hold values from 0.1 to 1.9
- norm_bias: float32 [4, 768], P('section'), may hold values from -1.75 to 1.75
- mol_ids: int32 [32, 256], P(('dp', 'section')), may hold values from 0 to 2, never falling along the last dimension, each value on 1 to 128 neighbouring positions
- key_mask: int32 [32, 256], P(('dp', 'section')), may hold values 0 or 1
Outputs:
- final_out: bfloat16 [8192, 768], P(('dp', 'section'))
- input_grad: float32 [8192, 768], P(('dp', 'section'))
- weight_grad: float32 [4, 768, 2304], P('section', None, 'dp')
- gain_grad: float32 [4, 768], P('section', 'dp')
- bias_grad: float32 [4, 768], P('section', 'dp')
The draws below stay inside these ranges and needn't reach their ends.
Inputs may be any that keep to these rules, and one draw needn't show every extreme that they name: `mol_ids`: in every row (one micro-batch) the molecule numbers never fall, each molecule covers 1 to 128 consecutive slots, and in every row some molecule covers exactly 128.
All inputs are finite; a program needn't handle non-finite values. No bound on the sum of `key_mask` on one device may be relied on, other than what follows from the above.
Results may differ from the reference program's by a relative error of at most 0.02.
Values may be sent and summed in bfloat16 or wider, within the bound.
A program may use at most 256 MiB of HBM per device.

```python
import math
import jax
import jax.numpy as jnp
import numpy as np
from jax import lax

D = 768
HEADS = 32
HS = 24
ROWS = 256
BLOCKS = 32
TOKENS = 8192
MOST = 128
MOLS = 3
N_SECTION = 4


def draw_section_weight(key, part):
    full_shape = (N_SECTION, D, 3 * D)
    section_pos = lax.broadcasted_iota(jnp.int32, full_shape, 0)
    column_pos = lax.broadcasted_iota(jnp.int32, full_shape, 2)
    is_mixing = section_pos % 2 == 1
    factor = jnp.where(is_mixing & (column_pos < D), 6.0, jnp.where(is_mixing & (column_pos >= 2 * D), 2.0, 1.0))
    base_draw = jax.random.normal(key, full_shape, jnp.float32)
    return (base_draw * factor / math.sqrt(D)).astype(jnp.bfloat16)


def with_ends(drawn, key, least, top_value):
    extent = drawn.shape
    index_at = [jax.random.randint(jax.random.fold_in(key, axis), (), 0, extent[axis]) for axis in range(len(extent))]
    drawn = drawn.at[tuple(index_at)].set(least)
    longest = extent.index(max(extent))
    index_at[longest] = (index_at[longest] + 1) % extent[longest]
    return drawn.at[tuple(index_at)].set(top_value)


def steps_of(stream_key, extent, cuts, least, high):
    level = 1.0
    for dim, parts in cuts:
        draws = jax.random.uniform(jax.random.fold_in(jax.random.fold_in(stream_key, 6), dim), (parts,), jnp.float32, least / len(cuts), high / len(cuts))
        level = level * jnp.repeat(jnp.exp(draws), extent[dim] // parts).reshape((-1,) + (1,) * (len(extent) - 1 - dim))
    return level


def split_up(amount, total, limit, skew):
    portions = [(1 << 20) // math.isqrt(standing ** skew) + 1 for standing in range(2, amount + 1)]
    spare, counts = total - limit - (amount - 1), [1] * (amount - 1)
    while spare > 0:
        movable = [i for i in range(amount - 1) if counts[i] < limit]
        mass, budget = sum([portions[i] for i in movable]), spare
        for i in movable:
            extra = min(limit - counts[i], max(1, budget * portions[i] // mass), spare)
            counts[i] = counts[i] + extra
            spare = spare - extra
    return np.array([limit] + counts)


def uneven(rng, count, total, reach, skew):
    if count == 2:
        one = jax.random.randint(rng, (), max(1, total - reach), min(reach, total - 1) + 1)
        return jnp.stack([one, total - one])
    lengths = jnp.asarray(split_up(count, total, reach, skew), jnp.int32)
    couples = (count - 1) // 2
    source_of, receiver = lengths[1:1 + 2 * couples:2], lengths[2:2 + 2 * couples:2]
    slack = jnp.minimum(source_of - 1, reach - receiver)
    moved = jax.random.randint(jax.random.fold_in(rng, 1), (couples,), 0, 1 << 20) % (slack + 1)
    lengths = lengths.at[1:1 + 2 * couples:2].set(source_of - moved).at[2:2 + 2 * couples:2].set(receiver + moved)
    return lengths[jax.random.permutation(jax.random.fold_in(rng, 2), count)]


def gaussian(stream_key, extent, scale, bound, shards=(), held_as=jnp.bfloat16):
    level = steps_of(stream_key, extent, shards, -0.22, 0.18) if shards else 1.0
    drawn = jax.random.normal(stream_key, extent, jnp.float32) * scale * level
    return jnp.minimum(jnp.maximum(drawn, -bound), bound).astype(held_as)


def setup_inputs(seed: int = 0) -> dict:
    streams_of = jax.random.split(jax.random.key(seed), 8)
    return {
        "tokens": gaussian(streams_of[0], (TOKENS, D), 1.0, 6.0, ((0, 32),)),
        "cotangent": gaussian(streams_of[1], (TOKENS, D), 1.0, 6.0, ((0, 32),)),
        "section_weight": draw_section_weight(jax.random.fold_in(streams_of[7], 71), 0),
        "norm_gain": jnp.clip(1.0 + 0.18 * jax.random.normal(streams_of[3], (N_SECTION, D), jnp.float32), 0.1, 1.9),
        "norm_bias": gaussian(streams_of[4], (N_SECTION, D), 0.3, 1.75, ((0, 4),), jnp.float32),
        "mol_ids": jax.vmap(lambda own: jnp.searchsorted(jnp.cumsum(uneven(own, MOLS, ROWS, MOST, 1)), jnp.arange(ROWS), side="right"))(jax.random.split(streams_of[5], BLOCKS)).reshape((BLOCKS, ROWS)).astype(jnp.int32),
        "key_mask": with_ends((jax.random.randint(streams_of[6], (BLOCKS, ROWS), 0, 8) < 7).astype(jnp.int32), jax.random.fold_in(streams_of[6], 1), 0, 1),
    }


@jax.custom_vjp
def low(v):
    return lax.optimization_barrier(v.astype(jnp.bfloat16)).astype(jnp.float32)

@jax.custom_vjp
def low_back(v):
    return v

def low_keep(v):
    return (low(v), None)

def low_pass(kept, grad):
    return (grad,)

def back_keep(v):
    return (v, None)

def back_low(kept, grad):
    return (low(grad),)
low.defvjp(low_keep, low_pass)
low_back.defvjp(back_keep, back_low)
NORM_EPS = 1e-05
NEG_FILL = -1e+30
HIGHEST_PREC = lax.Precision.HIGHEST

def normalize(values, gain_row, bias_row):
    center = values - lax.optimization_barrier(jnp.mean(values, axis=-1, keepdims=True))
    spread = lax.optimization_barrier(jnp.mean(center * center, axis=-1, keepdims=True))
    return center * lax.rsqrt(spread + NORM_EPS) * gain_row + bias_row

def split_heads(matrix):
    return jnp.transpose(matrix.reshape(matrix.shape[0], HEADS, HS), (1, 0, 2))

def attention_section(xin, weight, gain_row, bias_row, allowed):
    normed = low(normalize(xin, gain_row, bias_row))
    qkv_all = low_back(low(jnp.dot(normed, weight, precision=HIGHEST_PREC)))
    queries = split_heads(qkv_all[:, :D])
    keys_all = split_heads(qkv_all[:, D:2 * D])
    values_all = split_heads(qkv_all[:, 2 * D:])
    scores = low_back(jnp.einsum('hqd,hkd->hqk', queries, keys_all, precision=HIGHEST_PREC) * HS ** (-0.5))
    scores = jnp.where(allowed[None], scores, NEG_FILL)
    top_score = lax.optimization_barrier(jnp.max(scores, axis=-1, keepdims=True))
    weights_exp = jnp.exp(scores - top_score)
    soft_probs = weights_exp / lax.optimization_barrier(jnp.sum(weights_exp, axis=-1, keepdims=True))
    context = jnp.einsum('hqk,hkd->hqd', low(soft_probs), values_all, precision=HIGHEST_PREC)
    context = jnp.transpose(context, (1, 0, 2)).reshape(xin.shape[0], D)
    return (low_back(low(xin)), low_back(low(context)))

def ffn_section(residual, context, weight, gain_row, bias_row):
    mixed = low_back(jnp.dot(context, weight[:, :D], precision=HIGHEST_PREC))
    hidden = residual + mixed
    normed = low(normalize(hidden, gain_row, bias_row))
    pre_act = low_back(jnp.dot(normed, weight[:, D:2 * D], precision=HIGHEST_PREC))
    activated = low(jax.nn.gelu(pre_act))
    branch = jnp.dot(activated, weight[:, 2 * D:], precision=HIGHEST_PREC)
    return (low_back(low(hidden)), low_back(low(branch)))

def reference(tokens, cotangent, section_weight, norm_gain, norm_bias, mol_ids, key_mask):
    start_rows = tokens.astype(jnp.float32).reshape(BLOCKS, ROWS, D)
    weight_all = section_weight.astype(jnp.float32)
    same_mol = mol_ids[:, :, None] == mol_ids[:, None, :]
    own_key = jnp.eye(ROWS, dtype=bool)[None]
    allowed = same_mol & ((key_mask[:, None, :] == 1) | own_key)

    def forward(start_in, weight, gains, biases):

        def one_block(block_items):
            block_rows, allow_block = block_items
            residual, context = attention_section(block_rows, weight[0], gains[0], biases[0], allow_block)
            hidden, branch = ffn_section(residual, context, weight[1], gains[1], biases[1])
            residual, context = attention_section(hidden + branch, weight[2], gains[2], biases[2], allow_block)
            hidden, branch = ffn_section(residual, context, weight[3], gains[3], biases[3])
            return hidden + branch
        return lax.map(jax.checkpoint(one_block), (start_in, allowed))
    final_rows, pullback = jax.vjp(forward, start_rows, weight_all, norm_gain, norm_bias)
    gradients = pullback(cotangent.astype(jnp.float32).reshape(BLOCKS, ROWS, D))
    return (final_rows.reshape(TOKENS, D).astype(jnp.bfloat16), gradients[0].reshape(TOKENS, D), gradients[1], gradients[2], gradients[3])
```

```python
import math
import jax
import jax.numpy as jnp
import numpy as np
from jax import lax
from jax.experimental import pallas as pl
from jax.experimental.pallas import tpu as pltpu
from jax.sharding import PartitionSpec as P

HEADS=32; HS=24; EPS=1e-5; NEG=-1e30
BF = jnp.bfloat16
F32 = jnp.float32
I32 = jnp.int32
MESH = pl.DeviceIdType.MESH

GELU_A=0.7978845608028654; GELU_B=0.044715

def dotf(a,b): return jnp.dot(a,b,preferred_element_type=F32)
def dot_t(a,b): return lax.dot_general(a,b,(((1,),(1,)),((),())),preferred_element_type=F32)

def head_masks():
    m=np.zeros((16,256),np.float32)
    for h in range(16):
        lo=24*h-(0 if h<10 else 128)
        m[h,lo:lo+24]=1
    return m

def ln_fwd(x, g, b):
    c=x-jnp.mean(x,axis=-1,keepdims=True)
    v=jnp.mean(c*c,axis=-1,keepdims=True)
    r=lax.rsqrt(v+EPS)
    xh=c*r
    return xh, r, (xh*g+b).astype(BF)

def ln_bwd(gn, xh, r, g):
    gg=gn*g
    m1=jnp.mean(gg,axis=-1,keepdims=True)
    m2=jnp.mean(gg*xh,axis=-1,keepdims=True)
    return r*(gg-m1-xh*m2)


RC=256
HW=[0]*10+[1]*6
def rows_of(i, n):
    return pl.ds(pl.multiple_of(i * n, n), n)

def layer_fwd(xb, wa, wf, lnp, mb, hm, S, ctxT, vec):
    R,D=xb.shape
    NB=R//128
    xh,r,n=ln_fwd(xb[...].astype(F32), lnp[0:1,:], lnp[1:2,:])
    S["xha"][...]=xh; S["ra"][...]=r; S["an"][...]=n
    S["qkv"][...]=dotf(S["an"][...], wa[...]).astype(BF)
    @pl.loop(0,3)
    def _(i):
        cs=rows_of(i,D)
        S["qkvT"][cs,:]=S["qkv"][:,cs].T
    c=(HS**-0.5)*1.4426950408889634
    @pl.loop(0,NB*2)
    def _(it):
        b=it//2; g=it-2*b
        rows=rows_of(b,128)
        base=g*384
        mbias=mb[rows,:]
        qw=[S["qkv"][rows,pl.ds(pl.multiple_of(base+128*w,128),256)] for w in (0,1)]
        kw=[S["qkv"][rows,pl.ds(pl.multiple_of(D+base+128*w,128),256)] for w in (0,1)]
        for h in range(16):
            s=dot_t(kw[HW[h]]*hm[h:h+1,:], qw[HW[h]])*c+mbias
            m=jnp.max(s,axis=0,keepdims=True)
            ex=jnp.exp2(s-m)
            l=jnp.sum(ex,axis=0,keepdims=True)
            S["pT"][it*16+h]=(ex*(1.0/l)).astype(BF)
    @pl.loop(0,NB*2)
    def _(it):
        b=it//2; g=it-2*b
        rows=rows_of(b,128)
        base=g*384
        for j in range(8):
            vt=S["qkvT"][pl.ds(pl.multiple_of(2*D+base+48*j,16),48),rows]
            o=dotf(vt, jnp.concatenate([S["pT"][it*16+2*j],S["pT"][it*16+2*j+1]],axis=1))
            ctxT[pl.ds(pl.multiple_of(base+48*j,8),24),rows]=o[0:24,0:128]
            ctxT[pl.ds(pl.multiple_of(base+48*j+24,8),24),rows]=o[24:48,128:256]
    S["ctx"][...]=ctxT[...].astype(BF).T
    vec[...]=xb[...].astype(F32)+dotf(S["ctx"][...], wf[:,0:D])
    xh,r,n=ln_fwd(vec[...], lnp[2:3,:], lnp[3:4,:])
    S["xhf"][...]=xh; S["rf"][...]=r; S["fn"][...]=n
    u=dotf(S["fn"][...], wf[:,D:2*D])
    u2=u*u
    t=jnp.tanh(GELU_A*(u+GELU_B*u*u2))
    S["act"][...]=(0.5*u*(1.0+t)).astype(BF)
    S["gp"][...]=0.5*(1.0+t)+0.5*u*(1.0-t*t)*(GELU_A+3*GELU_A*GELU_B*u2)
    br=dotf(S["act"][...], wf[:,2*D:3*D]).astype(BF).astype(F32)
    return (vec[...].astype(BF).astype(F32)+br).astype(BF)

def layer_bwd(G, wa, wf, lnp, hm, S, gwa, gwf, glnp, gxT, gb, gbT, gctx, gctxT, gqT, gqb, gsT, vec, u):
    R,D=G.shape
    NB=R//128
    def put(ref,rows,val):
        ref[rows,:]=jnp.where(u>0,ref[rows,:],0.0)+val
    gbT[...]=G[...].T
    put(gwf,pl.ds(2*D,D),dotf(gbT[...],S["act"][...]))
    gb[...]=(dot_t(G[...], wf[:,2*D:3*D])*S["gp"][...]).astype(BF)
    gbT[...]=gb[...].T
    put(gwf,pl.ds(D,D),dotf(gbT[...],S["fn"][...]))
    vec[...]=dot_t(gb[...], wf[:,D:2*D])
    def lnb(gref, xh, r, grow, gi, resid, outref):
        gn=gref[...]; x=xh[...]
        gv=ln_bwd(gn,x,r[...],grow)
        outref[...]=(gv+resid[...].astype(F32)).astype(BF)
        put(glnp,slice(gi,gi+1),jnp.sum(gn*x,axis=0,keepdims=True)); put(glnp,slice(gi+1,gi+2),jnp.sum(gn,axis=0,keepdims=True))
    lnb(vec,S["xhf"],S["rf"],lnp[2:3,:],2,G,gb)
    gbT[...]=gb[...].T
    put(gwf,pl.ds(0,D),dotf(gbT[...],S["ctx"][...]))
    gctx[...]=dot_t(gb[...], wf[:,0:D]).astype(BF)
    gctxT[...]=gctx[...].T
    sc=HS**-0.5
    @pl.loop(0,NB*2)
    def _(it):
        b=it//2; g=it-2*b
        rows=rows_of(b,128)
        base=g*384
        vw=[S["qkv"][rows,pl.ds(pl.multiple_of(2*D+base+128*w,128),256)] for w in (0,1)]
        gw=[gctx[rows,pl.ds(pl.multiple_of(base+128*w,128),256)] for w in (0,1)]
        for h in range(16):
            gp=dot_t(vw[HW[h]]*hm[h:h+1,:], gw[HW[h]])
            pf=S["pT"][it*16+h].astype(F32)
            d=jnp.sum(pf*gp,axis=0,keepdims=True)
            gsT[it*16+h]=(pf*(gp-d)).astype(BF)
    def prod(k,fn):
        @pl.loop(0,NB*2)
        def _(it):
            b=it//2; g=it-2*b
            rows=rows_of(b,128)
            base=g*384
            for j in range(8):
                v=fn(it,rows,base,j)
                gqT[pl.ds(pl.multiple_of(k*D+base+48*j,8),24),rows]=v[0:24,0:128]
                gqT[pl.ds(pl.multiple_of(k*D+base+48*j+24,8),24),rows]=v[24:48,128:256]
    def pr(ref,it,j,ax): return jnp.concatenate([ref[it*16+2*j],ref[it*16+2*j+1]],axis=ax)
    prod(2,lambda it,rows,base,j: dot_t(gctxT[pl.ds(pl.multiple_of(base+48*j,16),48),rows], pr(S["pT"],it,j,0)))
    prod(1,lambda it,rows,base,j: dot_t(S["qkvT"][pl.ds(pl.multiple_of(base+48*j,16),48),rows], pr(gsT,it,j,0))*sc)
    prod(0,lambda it,rows,base,j: dotf(S["qkvT"][pl.ds(pl.multiple_of(D+base+48*j,16),48),rows], pr(gsT,it,j,1))*sc)
    gqb[...]=gqT[...].astype(BF)
    put(gwa,pl.ds(0,3*D),dotf(gqb[...],S["an"][...]))
    vec[...]=dotf(wa[...],gqb[...]).T
    lnb(vec,S["xha"],S["ra"],lnp[0:1,:],0,gb,gxT)


def remote(src, dst, ss, rs, dev):
    return pltpu.make_async_remote_copy(
        src_ref=src, dst_ref=dst, send_sem=ss, recv_sem=rs, device_id=dev, device_id_type=MESH
    )


UNIT = ("xha", "ra", "an", "qkv", "qkvT", "pT", "ctx", "xhf", "rf", "fn", "act", "gp")


def unit_shapes(R, D):
    return (
        ((R, D), F32), ((R, 1), F32), ((R, D), BF), ((R, 3 * D), BF), ((3 * D, R), BF),
        ((R // 128 * HEADS, 128, 128), BF), ((R, D), BF), ((R, D), F32), ((R, 1), F32),
        ((R, D), BF), ((R, D), BF), ((R, D), F32),
    )


def rotation(meta, R):
    mol = meta[0:1, :]
    c0 = jnp.sum((mol == 0).astype(I32), axis=1, keepdims=True)
    c1 = jnp.sum((mol == 1).astype(I32), axis=1, keepdims=True)
    start = jnp.where(c0 == 128, 0, jnp.where(c1 == 128, c0, c0 + c1))
    i0 = lax.broadcasted_iota(I32, (R, R), 0)
    i1 = lax.broadcasted_iota(I32, (R, R), 1)

    def onehot(a, b):
        t = a + start
        t = jnp.where(t >= R, t - R, t)
        return jnp.where(t == b, 1.0, 0.0).astype(BF)

    return onehot(i0, i1), onehot(i1, i0)


def pair_bias(meta, rot, out, R):
    mk = meta[...].astype(F32).astype(BF)
    row = dot_t(mk, rot)
    col = dot_t(rot, mk)
    k0 = lax.broadcasted_iota(I32, (128, 128), 0)
    q0 = lax.broadcasted_iota(I32, (128, 128), 1)
    for b in range(R // 128):
        rs = slice(b * 128, b * 128 + 128)
        same = col[rs, 0:1] == row[0:1, rs]
        ok = same & ((col[rs, 1:2] > 0.5) | (k0 == q0))
        out[rs, :] = jnp.where(ok, 0.0, NEG)


def relay_kernel(
    tok, cot, w, ln, meta, hm,
    fo, ig, gsum, glsum,
    *scr,
):
    R, D = tok.shape
    n = len(UNIT)
    U = {k: r for k, r in zip(UNIT, scr[:n])}
    (
        wa, wf, lna, lnf, metas, rots, rinv, mb, X, G, ys, fob, igb,
        gwa, gwf, glp, ctxT, vec, gb, gbT, gctx, gctxT, gqT, gqb, gsT, gx, sb, rb, glr,
        wl_s, w_s, w_r, l_s, l_r, m_s, m_r, ex_s, ex_r, y_s, y_r, fo_s, fo_r, g_s, g_r, ig_s, ig_r, p_s, p_r,
    ) = scr[n:]
    s = lax.axis_index("section")
    e = lax.rem(s, 2)
    L = s // 2
    mate = {"section": s + 1 - 2 * e}
    other = {"section": s + 2 - 4 * L}
    bar = pltpu.get_barrier_semaphore()
    pl.semaphore_signal(bar, inc=1, device_id=mate, device_id_type=MESH)
    pl.semaphore_signal(bar, inc=1, device_id=other, device_id_type=MESH)
    pl.semaphore_wait(bar, 2)

    def both(fn):
        @pl.when(e == 0)
        def _():
            fn(wa, lna, glp, gwa, gwf)

        @pl.when(e == 1)
        def _():
            fn(wf, lnf, glp, gwf, gwa)

    def send_w(wd, ld, *_):
        pltpu.make_async_copy(w, wd, wl_s.at[0]).start()
        pltpu.make_async_copy(ln, ld, wl_s.at[1]).start()
        remote(w, wd, w_s, w_r, mate).start()
        remote(ln, ld, l_s, l_r, mate).start()

    both(send_w)
    m_copy = remote(meta, metas, m_s, m_r, other)
    m_copy.start()
    rot, inv = rotation(meta, R)
    rots[...] = rot
    rinv[...] = inv
    xr = dotf(rot, tok[...]).astype(BF)
    cr = dotf(rot, cot[...]).astype(BF)

    @pl.when(L == 0)
    def _():
        X[0] = xr
        ys[0] = cr
        remote(ys.at[0], G.at[0], ex_s, ex_r, other).start()

    @pl.when(L == 1)
    def _():
        ys[0] = xr
        G[1] = cr
        remote(ys.at[0], X.at[1], ex_s, ex_r, other).start()

    m_copy.wait()
    rot2, _ = rotation(metas, R)

    @pl.when(L == 0)
    def _():
        pair_bias(meta, rots[...], mb.at[0], R)
        pair_bias(metas, rot2, mb.at[1], R)

    @pl.when(L == 1)
    def _():
        pair_bias(metas, rot2, mb.at[0], R)
        pair_bias(meta, rots[...], mb.at[1], R)

    def wait_w(wd, ld, *_):
        pltpu.make_async_copy(w, wd, wl_s.at[0]).wait()
        pltpu.make_async_copy(ln, ld, wl_s.at[1]).wait()
        remote(w, wd, w_s, w_r, mate).wait()
        remote(ln, ld, l_s, l_r, mate).wait()

    both(wait_w)
    lnp = LnRows(lna, lnf)

    def unit(u):
        return {k: r.at[u] for k, r in U.items()}

    @pl.loop(0, 2)
    def _(u):
        @pl.when(L == 1)
        def _():
            remote(ys.at[1], X.at[u], y_s.at[u], y_r.at[u], other).wait_recv()

        @pl.when((L == 0) & (u == 1))
        def _():
            remote(ys.at[0], X.at[1], ex_s, ex_r, other).wait_recv()

        y = layer_fwd(X.at[u], wa, wf, lnp, mb.at[u], hm, unit(u), ctxT, vec)

        @pl.when(L == 0)
        def _():
            ys[1 + u] = y
            remote(ys.at[1 + u], X.at[u], y_s.at[u], y_r.at[u], other).start()

        @pl.when((L == 1) & (u == 0))
        def _():
            ys[1] = y
            remote(ys.at[1], fob, fo_s, fo_r, other).start()

        @pl.when((L == 1) & (u == 1))
        def _():
            fob[...] = y

    @pl.loop(0, 2)
    def _(u):
        @pl.when((L == 1) & (u == 0))
        def _():
            remote(ys.at[0], G.at[0], ex_s, ex_r, other).wait_recv()

        @pl.when(L == 0)
        def _():
            remote(gx.at[u], G.at[u], g_s.at[u], g_r.at[u], other).wait_recv()

        layer_bwd(
            G.at[u], wa, wf, lnp, hm, unit(u), gwa, gwf, glp, gx.at[u],
            gb, gbT, gctx, gctxT, gqT, gqb, gsT, vec, u,
        )

        @pl.when(L == 1)
        def _():
            remote(gx.at[u], G.at[u], g_s.at[u], g_r.at[u], other).start()

        @pl.when((L == 0) & (u == 0))
        def _():
            igb[...] = gx[0]

        @pl.when((L == 0) & (u == 1))
        def _():
            remote(gx.at[1], igb, ig_s, ig_r, other).start()

    def swap(wd, ld, gl, mine, theirs):
        sb[0:3 * D, :] = theirs[...].astype(BF)

    both(swap)
    p_copy = remote(sb, rb, p_s.at[0], p_r.at[0], mate)
    p_copy.start()
    l_copy = remote(glp, glr, p_s.at[1], p_r.at[1], mate)
    l_copy.start()

    @pl.when(L == 0)
    def _():
        remote(ys.at[1], fob, fo_s, fo_r, other).wait_recv()

    @pl.when(L == 1)
    def _():
        remote(gx.at[1], igb, ig_s, ig_r, other).wait_recv()

    fo[...] = dotf(rinv[...], fob[...]).astype(BF)
    ig[...] = dotf(rinv[...], igb[...])
    p_copy.wait()
    l_copy.wait()
    glsum[...] = glp[...] + glr[...]

    def add(wd, ld, gl, mine, theirs):
        gsum[...] = (mine[...] + rb[...].astype(F32)).astype(BF)

    both(add)

    remote(ys.at[0], X.at[1], ex_s, ex_r, other).wait_send()

    @pl.when(L == 0)
    def _():
        remote(ys.at[1], X.at[0], y_s.at[0], y_r.at[0], other).wait_send()
        remote(ys.at[2], X.at[1], y_s.at[1], y_r.at[1], other).wait_send()
        remote(gx.at[1], igb, ig_s, ig_r, other).wait_send()

    @pl.when(L == 1)
    def _():
        remote(ys.at[1], fob, fo_s, fo_r, other).wait_send()
        remote(gx.at[0], G.at[0], g_s.at[0], g_r.at[0], other).wait_send()
        remote(gx.at[1], G.at[1], g_s.at[1], g_r.at[1], other).wait_send()


class LnRows:
    def __init__(self, a, f):
        self.a, self.f = a, f

    def __getitem__(self, ix):
        r = ix[0].start
        src = self.a if r < 2 else self.f
        return src[r % 2:r % 2 + 1, :]


def relay(tok, cot, w, ln, meta, hm):
    R, D = tok.shape
    V = pl.BlockSpec(memory_space=pltpu.VMEM)
    dma, vm = pltpu.SemaphoreType.DMA, pltpu.VMEM
    scratch = [vm((2,) + sh, dt) for sh, dt in unit_shapes(R, D)] + [
        vm((D, 3 * D), BF), vm((D, 3 * D), BF), vm((8, D), F32), vm((8, D), F32),
        vm((8, R), I32), vm((R, R), BF), vm((R, R), BF), vm((2, R, 128), F32),
        vm((2, R, D), BF), vm((2, R, D), BF), vm((3, R, D), BF), vm((R, D), BF), vm((R, D), BF),
        vm((3 * D, D), F32), vm((3 * D, D), F32), vm((8, D), F32),
        vm((D, R), F32), vm((R, D), F32), vm((R, D), BF), vm((D, R), BF), vm((R, D), BF), vm((D, R), BF),
        vm((3 * D, R), F32), vm((3 * D, R), BF), vm((R // 128 * HEADS, 128, 128), BF), vm((2, R, D), BF),
        vm((3 * D, D), BF), vm((3 * D, D), BF), vm((8, D), F32),
        dma((2,)), dma, dma, dma, dma, dma, dma, dma, dma, dma((2,)), dma((2,)), dma, dma,
        dma((2,)), dma((2,)), dma, dma, dma((2,)), dma((2,)),
    ]
    return pl.pallas_call(
        relay_kernel,
        out_shape=[
            jax.ShapeDtypeStruct((R, D), BF),
            jax.ShapeDtypeStruct((R, D), F32),
            jax.ShapeDtypeStruct((3 * D, D), BF),
            jax.ShapeDtypeStruct((8, D), F32),
        ],
        in_specs=[V, V, pl.BlockSpec(memory_space=pl.ANY), V, V, V],
        out_specs=[V] * 4,
        scratch_shapes=scratch,
        compiler_params=pltpu.CompilerParams(
            collective_id=0, has_side_effects=True, vmem_limit_bytes=64 << 20
        ),
        name="relay",
    )(tok, cot, w, ln, meta, hm)


def shards(tokens, cotangent, section_weight, norm_gain, norm_bias, mol_ids, key_mask):
    R, D = tokens.shape
    ln = jnp.concatenate([norm_gain, norm_bias, jnp.zeros((6, D), F32)], axis=0)
    meta = jnp.concatenate([mol_ids, key_mask, jnp.zeros((6, R), I32)], axis=0)
    hm = jnp.asarray(head_masks(), BF)
    fo, ig, gsum, glsum = relay(tokens, cotangent, section_weight[0], ln, meta, hm)
    e = lax.rem(lax.axis_index("section"), 2)
    gl = lax.dynamic_slice_in_dim(glsum, 2 * e, 2, 0)
    gw = lax.psum_scatter(gsum, "dp", scatter_dimension=0, tiled=True)
    gl = lax.psum_scatter(gl, "dp", scatter_dimension=1, tiled=True)
    return fo, ig, gw.astype(F32).T[None], gl[0:1], gl[1:2]


def solution(mesh):
    return jax.shard_map(
        shards,
        mesh=mesh,
        in_specs=(
            P(("dp", "section"), None),
            P(("dp", "section"), None),
            P("section", None, None),
            P("section", None),
            P("section", None),
            P(("dp", "section"), None),
            P(("dp", "section"), None),
        ),
        out_specs=(
            P(("dp", "section"), None),
            P(("dp", "section"), None),
            P("section", None, "dp"),
            P("section", "dp"),
            P("section", "dp"),
        ),
        check_vma=False,
    )
```

```python
import jax
import jax.numpy as jnp
from jax import lax
from jax.experimental import pallas as pl
from jax.experimental.pallas import tpu as pltpu
from jax.sharding import PartitionSpec as P

HEADS = 32
HS = 24
EPS = 1e-5
NEG = -1e30
BF = jnp.bfloat16
F32 = jnp.float32
I32 = jnp.int32
MESH = pl.DeviceIdType.MESH
GELU_A = 0.7978845608028654
GELU_B = 0.044715
LOG2E = 1.4426950408889634
T = 128


def dotf(a, b):
    return jnp.dot(a, b, preferred_element_type=F32)


def dot_t(a, b):
    return lax.dot_general(a, b, (((1,), (1,)), ((), ())), preferred_element_type=F32)


def at(i, n):
    return pl.ds(pl.multiple_of(i * n, n), n)


HEAD_WIN = (0,) * 10 + (1,) * 6


def ln_rows(x, g, b):
    c = x - jnp.mean(x, axis=-1, keepdims=True)
    r = lax.rsqrt(jnp.mean(c * c, axis=-1, keepdims=True) + EPS)
    xh = c * r
    return xh, r, (xh * g + b).astype(BF)


def windows(ref, rows, base):
    return [ref[rows, pl.ds(pl.multiple_of(base + 128 * w, 128), 256)] for w in (0, 1)]


def put_heads(ref, base, j, v):
    ref[pl.ds(pl.multiple_of(base + 48 * j, 8), 24), :] = v[0:24, 0:T]
    ref[pl.ds(pl.multiple_of(base + 48 * j + 24, 8), 24), :] = v[24:48, T:2 * T]


def two(ref, i, axis):
    return jnp.concatenate([ref[i], ref[i + 1]], axis=axis)


def forward_stages(x, y, wa, wf, lna, lnf, mb, hm, S, ctxT, vec):
    D = x.shape[1]

    def norm_a():
        S["xha"][...], S["ra"][...], S["an"][...] = ln_rows(x[...].astype(F32), lna[0][...], lna[1][...])

    def project():
        S["qkv"][...] = dotf(S["an"][...], wa[...]).astype(BF)

    def flip():
        S["qkvT"][...] = S["qkv"][...].T

    def scores():
        @pl.loop(0, 2)
        def _(g):
            base = g * 384
            bias = mb[...]
            qw = windows(S["qkv"], slice(None), base)
            kw = windows(S["qkv"], slice(None), D + base)
            for h in range(16):
                w = HEAD_WIN[h]
                s = dot_t(kw[w] * hm[h:h + 1, :], qw[w]) * (HS ** -0.5 * LOG2E) + bias
                ex = jnp.exp2(s - jnp.max(s, axis=0, keepdims=True))
                S["pT"][g * 16 + h] = (ex * (1.0 / jnp.sum(ex, axis=0, keepdims=True))).astype(BF)

    def mix_values():
        @pl.loop(0, 2)
        def _(g):
            base = g * 384
            for j in range(8):
                vt = S["qkvT"][pl.ds(pl.multiple_of(2 * D + base + 48 * j, 16), 48), :]
                put_heads(ctxT, base, j, dotf(vt, two(S["pT"], g * 16 + 2 * j, 1)))

    def mixed():
        S["ctx"][...] = ctxT[...].astype(BF).T
        vec[...] = x[...].astype(F32) + dotf(S["ctx"][...], wf[:, 0:D])

    def norm_f():
        S["xhf"][...], S["rf"][...], S["fn"][...] = ln_rows(vec[...], lnf[0][...], lnf[1][...])

    def act():
        u = dotf(S["fn"][...], wf[:, D:2 * D])
        u2 = u * u
        t = jnp.tanh(GELU_A * (u + GELU_B * u * u2))
        S["act"][...] = (0.5 * u * (1.0 + t)).astype(BF)
        S["gp"][...] = 0.5 * (1.0 + t) + 0.5 * u * (1.0 - t * t) * (GELU_A + 3 * GELU_A * GELU_B * u2)

    def branch():
        br = dotf(S["act"][...], wf[:, 2 * D:3 * D]).astype(BF).astype(F32)
        y[...] = (vec[...].astype(BF).astype(F32) + br).astype(BF)

    return [norm_a, project, flip, scores, mix_values, mixed, norm_f, act, branch]


def backward_stages(G, gx, waT, wfT, lna, lnf, hm, S, W, glp, gb, gctx, gctxT, gqT, gsT, vec):
    D = G.shape[1]

    def ln_back(gref, xh, r, g, gi, resid, out):
        gn = gref[...]
        x = xh[...]
        gg = gn * g
        m1 = jnp.mean(gg, axis=-1, keepdims=True)
        m2 = jnp.mean(gg * x, axis=-1, keepdims=True)
        out[...] = (r[...] * (gg - m1 - x * m2) + resid[...].astype(F32)).astype(BF)
        glp[gi:gi + 1, :] += jnp.sum(gn * x, axis=0, keepdims=True)
        glp[gi + 1:gi + 2, :] += jnp.sum(gn, axis=0, keepdims=True)

    def g_act():
        W["f"][2 * D:3 * D, :] = G[...].T
        gb[...] = (dotf(G[...], wfT[2 * D:3 * D, :]) * S["gp"][...]).astype(BF)

    def g_norm():
        W["f"][D:2 * D, :] = gb[...].T
        vec[...] = dotf(gb[...], wfT[D:2 * D, :])

    def g_hidden():
        ln_back(vec, S["xhf"], S["rf"], lnf[0][...], 2, G, gb)

    def g_context():
        W["f"][0:D, :] = gb[...].T
        t = dotf(gb[...], wfT[0:D, :]).astype(BF)
        gctx[...] = t
        gctxT[...] = t.T

    def g_scores():
        @pl.loop(0, 2)
        def _(g):
            base = g * 384
            vw = windows(S["qkv"], slice(None), 2 * D + base)
            gw = windows(gctx, slice(None), base)
            for h in range(16):
                w = HEAD_WIN[h]
                gp = dot_t(vw[w] * hm[h:h + 1, :], gw[w])
                p = S["pT"][g * 16 + h].astype(F32)
                d = jnp.sum(p * gp, axis=0, keepdims=True)
                gsT[g * 16 + h] = (p * (gp - d)).astype(BF)

    def g_values():
        @pl.loop(0, 2)
        def _(g):
            base = g * 384
            for j in range(8):
                a = gctxT[pl.ds(pl.multiple_of(base + 48 * j, 16), 48), :]
                put_heads(gqT, 2 * D + base, j, dot_t(a, two(S["pT"], g * 16 + 2 * j, 0)))

    def g_keys():
        @pl.loop(0, 2)
        def _(g):
            base = g * 384
            for j in range(8):
                a = S["qkvT"][pl.ds(pl.multiple_of(base + 48 * j, 16), 48), :]
                put_heads(gqT, D + base, j, dot_t(a, two(gsT, g * 16 + 2 * j, 0)) * HS ** -0.5)

    def g_queries():
        @pl.loop(0, 2)
        def _(g):
            base = g * 384
            for j in range(8):
                a = S["qkvT"][pl.ds(pl.multiple_of(D + base + 48 * j, 16), 48), :]
                put_heads(gqT, base, j, dotf(a, two(gsT, g * 16 + 2 * j, 1)) * HS ** -0.5)

    def g_merge():
        t = gqT[...].astype(BF)
        W["a"][...] = t
        S["qkv"][...] = t.T

    def g_input():
        vec[...] = dotf(S["qkv"][...], waT[...])

    def g_x():
        ln_back(vec, S["xha"], S["ra"], lna[0][...], 0, gb, gx)

    return [g_act, g_norm, g_hidden, g_context, g_scores, g_values, g_keys, g_queries, g_merge, g_input, g_x]


def remote(src, dst, ss, rs, dev):
    return pltpu.make_async_remote_copy(
        src_ref=src, dst_ref=dst, send_sem=ss, recv_sem=rs, device_id=dev, device_id_type=MESH
    )


def when(cond, fn):
    pl.when(cond)(fn)


NZ = 4
SUB = 2
HALF = 1
ORDER = ((3, 2, 1, 0), (3, 0, 2, 1), (0, 3, 1, 2), (0, 1, 2, 3))


def by_place(vals, z):
    r = vals[-1]
    for i in range(len(vals) - 2, -1, -1):
        r = jnp.where(z == i, vals[i], r)
    return r


def rotation(mol, R):
    c0 = jnp.sum((mol == 0).astype(I32), axis=1, keepdims=True)
    c1 = jnp.sum((mol == 1).astype(I32), axis=1, keepdims=True)
    start = jnp.where(c0 == T, 0, jnp.where(c1 == T, c0, c0 + c1))
    i0 = lax.broadcasted_iota(I32, (R, R), 0)
    i1 = lax.broadcasted_iota(I32, (R, R), 1)

    def onehot(a, b):
        t = a + start
        t = jnp.where(t >= R, t - R, t)
        return jnp.where(t == b, 1.0, 0.0).astype(BF)

    return onehot(i0, i1), onehot(i1, i0)


def pair_bias(mol, key, rot, out, base, R):
    mk = jnp.concatenate([mol, key, jnp.zeros((6, R), I32)], axis=0).astype(F32).astype(BF)
    row = dot_t(mk, rot)
    col = dot_t(rot, mk)
    k0 = lax.broadcasted_iota(I32, (T, T), 0)
    q0 = lax.broadcasted_iota(I32, (T, T), 1)
    for b in range(R // T):
        rs = slice(b * T, b * T + T)
        ok = (col[rs, 0:1] == row[0:1, rs]) & ((col[rs, 1:2] > 0.5) | (k0 == q0))
        out[base + b] = jnp.where(ok, 0.0, NEG)


UNIT = ("xha", "ra", "an", "qkv", "qkvT", "pT", "ctx", "xhf", "rf", "fn", "act", "gp")


def unit_shapes(D):
    return (
        ((T, D), F32), ((T, 1), F32), ((T, D), BF), ((T, 3 * D), BF), ((3 * D, T), BF),
        ((HEADS, T, T), BF), ((T, D), BF), ((T, D), F32), ((T, 1), F32),
        ((T, D), BF), ((T, D), BF), ((T, D), F32),
    )


def relay_kernel(fused, tok, cot, w, gain, bias, mol, key, fo, ig, out_w, out_n, *scr):
    R, D = tok.shape
    n = len(UNIT)
    U = {k: r for k, r in zip(UNIT, scr[:n])}
    (
        wa, wf, waT, wfT, lga, lba, lgf, lbf, molo, keyo, rinv, hm, mb, X, G, ex, ys, gx, fob, igb,
        acca, accf, wga, wgf, rb, glp, glr, vec, gb, gctx, gctxT, gqT, gsT,
        wl_s, w_s, w_r, l_s, l_r, m_s, m_r, ex_s, ex_r, y_s, y_r, fo_s, fo_r, g_s, g_r, ig_s, ig_r,
        p_s, p_r, gl_s, gl_r,
    ) = scr[n:n + 54]
    s = lax.axis_index("section")
    e = lax.rem(s, 2)
    L = s // 2
    mate = {"section": s + 1 - 2 * e}
    other = {"section": s + 2 - 4 * L}
    d = lax.axis_index("dp")
    z = d // 2
    y = d - 2 * z
    across = {"dp": d + 1 - 2 * y}

    def on_line(zz):
        return {"dp": zz * 2 + y}

    bar = pltpu.get_barrier_semaphore()
    peers = [mate, other]
    if fused:
        peers += [across] + [on_line(lax.rem(z + t, NZ)) for t in range(1, NZ)]
    for p in peers:
        pl.semaphore_signal(bar, inc=1, device_id=p, device_id_type=MESH)
    pl.semaphore_wait(bar, len(peers))

    def third(c):
        return (slice(None), pl.ds(c * D, D))

    def w_local(k, j):
        src = (w, gain, bias)[j]
        return pltpu.make_async_copy(src, own[k][j], wl_s.at[j])

    def w_rem(k, j):
        if j < 3:
            return remote(w.at[third(j)], own[k][0].at[third(j)], w_s.at[j], w_r.at[j], mate)
        src = (gain, bias)[j - 3]
        return remote(src, own[k][j - 2], l_s.at[j - 3], l_r.at[j - 3], mate)

    own = ((wa, lga, lba), (wf, lgf, lbf))

    def per_core(fn):
        when(e == 0, lambda: fn(0))
        when(e == 1, lambda: fn(1))

    def send_weights(k):
        for j in (3, 4):
            w_rem(k, j).start()
        for j in range(3):
            w_local(k, j).start()
        for j in range(3):
            w_rem(k, j).start()

    per_core(send_weights)
    mol_copy = remote(mol, molo, m_s.at[0], m_r.at[0], other)
    key_copy = remote(key, keyo, m_s.at[1], m_r.at[1], other)
    mol_copy.start()
    key_copy.start()

    rot, inv = rotation(mol[...], R)
    rinv[...] = inv
    xr = dotf(rot, tok[...]).astype(BF)
    cr = dotf(rot, cot[...]).astype(BF)
    xu = xr.reshape(2, T, D)
    cu = cr.reshape(2, T, D)

    def ex_copy(dst):
        return remote(ex, dst, ex_s, ex_r, other)

    def stage0():
        ex[...] = cu
        ex_copy(G.at[pl.ds(0, 2)]).start()
        X[0:2] = xu

    def stage1():
        ex[...] = xu
        ex_copy(X.at[pl.ds(2, 2)]).start()
        G[2:4] = cu

    when(L == 0, stage0)
    when(L == 1, stage1)
    i0 = lax.broadcasted_iota(I32, (16, 256), 0)
    i1 = lax.broadcasted_iota(I32, (16, 256), 1)
    lo = HS * i0 - jnp.where(i0 < 10, 0, 128)
    hm[...] = jnp.where((i1 >= lo) & (i1 < lo + HS), 1.0, 0.0).astype(BF)
    glp[...] = jnp.zeros_like(glp)
    mol_copy.wait()
    key_copy.wait()
    pair_bias(mol[...], key[...], rot, mb, 2 * L, R)
    rot_o, _ = rotation(molo[...], R)
    pair_bias(molo[...], keyo[...], rot_o, mb, 2 - 2 * L, R)

    def wait_local(k):
        for j in range(3):
            w_local(k, j).wait()
        for j in (3, 4):
            w_rem(1 - k, j).wait_recv()

    per_core(wait_local)

    def wait_third(k, c):
        w_rem(k, c).wait_recv()

    def turn_weights():
        @pl.loop(0, 3)
        def _(i):
            cs = at(i, D)
            waT[cs, :] = wa[:, cs].T
            wfT[cs, :] = wf[:, cs].T

    def wait_all(k):
        for c in range(3):
            wait_third(1 - k, c)

    def ready1():
        per_core(wait_all)
        turn_weights()

    when(L == 1, ready1)

    def grads(acc, wg, rhs, p, first):
        for c in range(3):
            rs = slice(c * D, c * D + D)
            v = dotf(wg[p, rs, :], rhs[c][2 * p:2 * p + 2].reshape(2 * T, D))
            if not first:
                v = v + acc[rs, :].astype(F32)
            acc[rs, :] = v.astype(BF)

    def grads_f(p, first):
        grads(accf, wgf, (U["ctx"], U["fn"], U["act"]), p, first)

    def grads_a(p, first):
        grads(acca, wga, (U["an"],) * 3, p, first)

    if fused:
        yb, inb, raw, acc, gy, gz, ry_s, ry_r, rz_s, rz_r, rw_s, rw_r, rg_s, rg_r = scr[n + 54:]
        CH = 3 * D // (2 * NZ)
        SR = CH // SUB
        dest = [by_place([ORDER[k][i] for k in range(NZ)], z) for i in range(NZ)]
        buddy = z + 1 - 2 * lax.rem(z, 2)

        def rows(zz, yy, q):
            return pl.ds(pl.multiple_of((zz * 2 + yy) * CH + q * SR, 16), SR)

        def y_copy(i, q):
            return remote(rb.at[rows(dest[i], 1 - y, q), :], yb.at[i, q], ry_s.at[i, q], ry_r.at[i, q], across)

        def raw_copy(q):
            return remote(
                rb.at[rows(buddy, 1 - y, q), :], raw.at[q], rw_s.at[q], rw_r.at[q], on_line(buddy)
            )

        def piece(i):
            return pl.ds(pl.multiple_of(dest[i] * (2 * CH), 16), 2 * CH)
    else:
        def piece(i):
            return pl.ds(i * (3 * D // NZ), 3 * D // NZ)

    def p_copy(i, src):
        return remote(src.at[piece(i), :], rb.at[piece(i), :], p_s.at[i], p_r.at[i], mate)

    def give(src):
        for i in range(NZ):
            p_copy(i, src).start()

    def take(mine):
        for i in range(NZ):
            p_copy(i, mine).wait_recv()
            r = piece(i)
            rb[r, :] = (rb[r, :].astype(F32) + mine[r, :].astype(F32)).astype(BF)
            if fused and i < NZ - 1:
                def to_buddy():
                    for q in range(HALF):
                        raw_copy(q).start()

                def halves(i=i):
                    for q in range(HALF):
                        y_copy(i, q).start()

                when(dest[i] == buddy, to_buddy)
                when(dest[i] != buddy, halves)
                for q in range(HALF, SUB):
                    y_copy(i, q).start()

    def f_last():
        grads_f(1, False)
        when(e == 0, lambda: give(accf))

    def f_take():
        when(e == 1, lambda: take(accf))

    def a_last():
        grads_a(1, False)
        when(e == 1, lambda: give(acca))

    def y_copy_x(u):
        return remote(ys.at[u], X.at[u], y_s.at[u], y_r.at[u], other)

    def fo_copy(u):
        return remote(ys.at[u], fob.at[u], fo_s.at[u], fo_r.at[u], other)

    def g_copy(u):
        return remote(gx.at[u], G.at[u], g_s.at[u], g_r.at[u], other)

    def ig_copy(u):
        return remote(gx.at[u], igb.at[u - 2], ig_s.at[u - 2], ig_r.at[u - 2], other)

    def forward(u):
        S = {k: r.at[u] for k, r in U.items()}
        when(L == 1, lambda: y_copy_x(u).wait_recv())
        when((L == 0) & (u == 2), lambda: ex_copy(X.at[pl.ds(2, 2)]).wait_recv())
        opening = (L == 0) & (u == 0)
        st = forward_stages(
            X.at[u], ys.at[u], wa, wf, (lga, lba), (lgf, lbf), mb.at[u], hm, S, gqT.at[pl.ds(0, D)], vec
        )
        for f in st:
            if f.__name__ == "project":
                when(opening & (e == 1), lambda: wait_all(1))
            if f.__name__ in ("mixed", "act", "branch"):
                c = ("mixed", "act", "branch").index(f.__name__)
                when(opening & (e == 0), lambda c=c: wait_third(1, c))
            f()
        when(L == 0, lambda: y_copy_x(u).start())
        when((L == 1) & (u < 2), lambda: fo_copy(u).start())

        def keep():
            fob[u - 2] = ys[u]

        when((L == 1) & (u >= 2), keep)

    def backward(u):
        S = {k: r.at[u] for k, r in U.items()}
        when((L == 0) & (u == 0), turn_weights)
        when((L == 1) & (u == 0), lambda: ex_copy(G.at[pl.ds(0, 2)]).wait_recv())
        when(L == 0, lambda: g_copy(u).wait_recv())
        last = (L == 0) & (u == 3)
        p = u // 2
        lanes = at(u - 2 * p, T)
        st = backward_stages(
            G.at[u], gx.at[u], waT, wfT, (lga, lba), (lgf, lbf), hm, S,
            {"a": wga.at[p, :, lanes], "f": wgf.at[p, :, lanes]},
            glp, gb, gctx, gctxT, gqT, gsT, vec,
        )
        for f in st:
            f()
            if f.__name__ == "g_context":
                when(last, f_last)
            if f.__name__ == "g_scores":
                when(last, f_take)
            if f.__name__ == "g_merge":
                when(last, a_last)
        when(L == 1, lambda: g_copy(u).start())
        when((L == 0) & (u >= 2), lambda: ig_copy(u).start())

        def keep():
            igb[u] = gx[u]

        def first_pair():
            grads_f(0, True)
            grads_a(0, True)

        when((L == 0) & (u < 2), keep)
        when((L == 0) & (u == 1), first_pair)

    @pl.loop(0, 8)
    def _(i):
        odd = lax.rem(i, 2)
        is_f = jnp.where(L == 0, jnp.where(i < 4, 1, 0), 1 - odd)
        u = jnp.where(L == 0, lax.rem(i, 4), i // 2)
        when(is_f == 1, lambda: forward(u))
        when(is_f == 0, lambda: backward(u))

    def finish1():
        grads_f(0, True)
        f_last()
        grads_a(0, True)
        f_take()
        a_last()

    when(L == 1, finish1)
    gl_copy = remote(glp, glr, gl_s, gl_r, mate)
    gl_copy.start()
    when(e == 0, lambda: take(acca))

    def bring0():
        for u in range(2):
            fo_copy(u).wait_recv()

    def bring1():
        for u in (2, 3):
            ig_copy(u).wait_recv()

    when(L == 0, bring0)
    when(L == 1, bring1)
    fo[...] = dotf(rinv[...], fob[...].reshape(R, D)).astype(BF)
    ig[...] = dotf(rinv[...], igb[...].reshape(R, D))
    gl_copy.wait()

    if fused:
        gl1 = glp[...] + glr[...]
        glr[...] = gl1
        gy_copy = remote(glr, gy, rg_s.at[0], rg_r.at[0], across)
        gy_copy.start()

        def own_y():
            for q in range(SUB):
                if q < HALF:
                    raw_copy(q).wait()
                    r = rows(z, 1 - y, q)
                    rb[r, :] = (rb[r, :].astype(F32) + raw[q].astype(F32)).astype(BF)
                y_copy(NZ - 1, q).start()

        def hop(i, q):
            zz = dest[i]
            nz = jnp.where(zz > z, z + 1, z - 1)
            slot = jnp.where((nz == zz) & (z > zz), NZ, zz)
            return remote(yb.at[i, q], inb.at[slot, q], rz_s.at[i, q], rz_r.at[slot, q], on_line(nz))

        def arrived(slot, q):
            remote(yb.at[0, q], inb.at[slot, q], rz_s.at[0, q], rz_r.at[slot, q], across).wait_recv()

        for i in range(NZ - 1):
            zz = dest[i]
            for q in range(SUB):
                mine = rb.at[rows(zz, y, q), :]

                def combine(i=i, q=q, mine=mine):
                    y_copy(i, q).wait_recv()
                    yb[i, q] = (mine[...].astype(F32) + yb[i, q].astype(F32)).astype(BF)

                def plain(i=i, q=q, mine=mine):
                    yb[i, q] = mine[...]

                def add_in(i=i, q=q, zz=zz):
                    arrived(zz, q)
                    yb[i, q] = (yb[i, q].astype(F32) + inb[zz, q].astype(F32)).astype(BF)

                if q < HALF:
                    when(zz != buddy, combine)
                    when(zz == buddy, plain)
                else:
                    combine()
                when(jnp.where(zz > z, z > 0, z < NZ - 1), add_in)
                hop(i, q).start()
            if i == NZ - 3:
                own_y()
        gy_copy.wait()
        gl2 = glr[...] + gy[...]
        out_n[...] = gl2
        gz_copies = [
            remote(out_n, gz.at[NZ - t - 1], rg_s.at[t], rg_r.at[NZ - t], on_line(lax.rem(z + t, NZ)))
            for t in range(1, NZ)
        ]
        for c in gz_copies:
            c.start()
        for q in range(SUB):
            acc[q] = rb[rows(z, y, q), :].astype(F32)

            def from_left(q=q):
                arrived(z, q)
                acc[q] += inb[z, q].astype(F32)

            def from_right(q=q):
                arrived(NZ, q)
                acc[q] += inb[NZ, q].astype(F32)

            when(z > 0, from_left)
            when(z < NZ - 1, from_right)
            y_copy(NZ - 1, q).wait_recv()
            acc[q] += yb[NZ - 1, q].astype(F32)
        out_w[...] = acc[...].reshape(CH, D).T
        for i in range(NZ):
            for q in range(SUB):
                if q < HALF and i < NZ - 1:
                    when(dest[i] != buddy, lambda i=i, q=q: y_copy(i, q).wait_send())
                else:
                    y_copy(i, q).wait_send()
                if i < NZ - 1:
                    hop(i, q).wait_send()
        for t, c in zip(range(1, NZ), gz_copies):
            c.wait_send()
        for k in range(NZ - 1):
            remote(out_n, gz.at[k], rg_s.at[0], rg_r.at[k + 1], across).wait_recv()
        out_n[...] = gl2 + gz[0] + gz[1] + gz[2]
    else:
        out_w[...] = rb[...]
        out_n[...] = glp[...] + glr[...]

    def close_weights(k):
        for j in range(5):
            w_rem(k, j).wait_send()

    per_core(close_weights)
    def gave(src):
        for i in range(NZ):
            p_copy(i, src).wait_send()

    when(e == 0, lambda: gave(accf))
    when(e == 1, lambda: gave(acca))
    ex_copy(X.at[pl.ds(2, 2)]).wait_send()

    def close0():
        for u in range(4):
            y_copy_x(u).wait_send()
        for u in (2, 3):
            ig_copy(u).wait_send()

    def close1():
        for u in range(4):
            g_copy(u).wait_send()
        for u in range(2):
            fo_copy(u).wait_send()

    when(L == 0, close0)
    when(L == 1, close1)


def relay(fused, tok, cot, w, gain, bias, mol, key):
    R, D = tok.shape
    V = pl.BlockSpec(memory_space=pltpu.VMEM)
    dma, vm = pltpu.SemaphoreType.DMA, pltpu.VMEM
    scratch = [vm((4,) + sh, dt) for sh, dt in unit_shapes(D)] + [
        vm((D, 3 * D), BF), vm((D, 3 * D), BF), vm((3 * D, D), BF), vm((3 * D, D), BF),
        vm((1, D), F32), vm((1, D), F32), vm((1, D), F32), vm((1, D), F32),
        vm((1, R), I32), vm((1, R), I32), vm((R, R), BF), vm((16, 256), BF), vm((4, T, T), F32),
        vm((4, T, D), BF), vm((4, T, D), BF), vm((2, T, D), BF), vm((4, T, D), BF), vm((4, T, D), BF),
        vm((2, T, D), BF), vm((2, T, D), BF),
        vm((3 * D, D), BF), vm((3 * D, D), BF), vm((2, 3 * D, 2 * T), BF), vm((2, 3 * D, 2 * T), BF),
        vm((3 * D, D), BF), vm((8, D), F32), vm((8, D), F32),
        vm((T, D), F32), vm((T, D), BF), vm((T, D), BF), vm((D, T), BF),
        vm((3 * D, T), F32), vm((HEADS, T, T), BF),
        dma((3,)), dma((3,)), dma((3,)), dma((2,)), dma((2,)), dma((2,)), dma((2,)), dma, dma,
        dma((4,)), dma((4,)), dma((2,)), dma((2,)), dma((4,)), dma((4,)), dma((2,)), dma((2,)),
        dma((NZ,)), dma((NZ,)), dma, dma,
    ]
    if fused:
        CH = 3 * D // (2 * NZ)
        SR = CH // SUB
        scratch += [
            vm((NZ, SUB, SR, D), BF), vm((NZ + 1, SUB, SR, D), BF), vm((HALF, SR, D), BF),
            vm((SUB, SR, D), F32), vm((8, D), F32), vm((NZ - 1, 8, D), F32),
            dma((NZ, SUB)), dma((NZ, SUB)), dma((NZ - 1, SUB)), dma((NZ + 1, SUB)),
            dma((HALF,)), dma((HALF,)), dma((NZ,)), dma((NZ,)),
        ]
        w_out = jax.ShapeDtypeStruct((D, CH), F32)
    else:
        w_out = jax.ShapeDtypeStruct((3 * D, D), BF)
    return pl.pallas_call(
        lambda *refs: relay_kernel(fused, *refs),
        out_shape=[
            jax.ShapeDtypeStruct((R, D), BF),
            jax.ShapeDtypeStruct((R, D), F32),
            w_out,
            jax.ShapeDtypeStruct((8, D), F32),
        ],
        in_specs=[V, V, pl.BlockSpec(memory_space=pl.ANY), V, V, V, V],
        out_specs=[V] * 4,
        scratch_shapes=scratch,
        compiler_params=pltpu.CompilerParams(
            collective_id=0, has_side_effects=True, vmem_limit_bytes=64 << 20
        ),
        name="relay",
    )(tok, cot, w, gain, bias, mol, key)


def shards(tokens, cotangent, section_weight, norm_gain, norm_bias, mol_ids, key_mask):
    D = tokens.shape[1]
    ranks = lax.axis_size("dp")
    fused = ranks == 2 * NZ
    fo, ig, gw, gn = relay(
        fused, tokens, cotangent, section_weight[0], norm_gain, norm_bias, mol_ids, key_mask
    )
    e = lax.rem(lax.axis_index("section"), 2)
    if fused:
        part = D // ranks
        gn = lax.dynamic_slice(gn, (2 * e, lax.axis_index("dp") * part), (2, part))
        return fo, ig, gw[None], gn[0:1], gn[1:2]
    gn = lax.dynamic_slice_in_dim(gn, 2 * e, 2, 0)
    gw = lax.psum_scatter(gw, "dp", scatter_dimension=0, tiled=True)
    gn = lax.psum_scatter(gn, "dp", scatter_dimension=1, tiled=True)
    return fo, ig, gw.astype(F32).T[None], gn[0:1], gn[1:2]


def solution(mesh):
    return jax.shard_map(
        shards,
        mesh=mesh,
        in_specs=(
            P(("dp", "section"), None),
            P(("dp", "section"), None),
            P("section", None, None),
            P("section", None),
            P("section", None),
            P(("dp", "section"), None),
            P(("dp", "section"), None),
        ),
        out_specs=(
            P(("dp", "section"), None),
            P(("dp", "section"), None),
            P("section", None, "dp"),
            P("section", "dp"),
            P("section", "dp"),
        ),
        check_vma=False,
    )
```

```python
import jax
import jax.numpy as jnp
from jax import lax
from jax.experimental import pallas as pl
from jax.experimental.pallas import tpu as pltpu
from jax.sharding import PartitionSpec as P

HEADS = 32
HS = 24
EPS = 1e-5
NEG = -1e30
BF = jnp.bfloat16
F32 = jnp.float32
I32 = jnp.int32
MESH = pl.DeviceIdType.MESH
GELU_A = 0.7978845608028654
GELU_B = 0.044715
LOG2E = 1.4426950408889634
T = 128


def dotf(a, b):
    return jnp.dot(a, b, preferred_element_type=F32)


def dot_t(a, b):
    return lax.dot_general(a, b, (((1,), (1,)), ((), ())), preferred_element_type=F32)


def at(i, n):
    return pl.ds(pl.multiple_of(i * n, n), n)


HEAD_WIN = (0,) * 10 + (1,) * 6


def ln_rows(x, g, b):
    c = x - jnp.mean(x, axis=-1, keepdims=True)
    r = lax.rsqrt(jnp.mean(c * c, axis=-1, keepdims=True) + EPS)
    xh = c * r
    return xh, r, (xh * g + b).astype(BF)


def windows(ref, rows, base):
    return [ref[rows, base + 128 * w:base + 128 * w + 256] for w in (0, 1)]


def put_heads(ref, base, j, v):
    ref[base + 48 * j:base + 48 * j + 24, :] = v[0:24, 0:T]
    ref[base + 48 * j + 24:base + 48 * j + 48, :] = v[24:48, T:2 * T]


def two(ref, i, axis):
    return jnp.concatenate([ref[i], ref[i + 1]], axis=axis)


def forward_stages(x, y, wa, wf, lna, lnf, mb, hm, S, ctxT, vec):
    D = x.shape[1]

    def norm_a():
        S["xha"][...], S["ra"][...], S["an"][...] = ln_rows(x[...].astype(F32), lna[0][...], lna[1][...])

    def project():
        S["qkv"][...] = dotf(S["an"][...], wa[...]).astype(BF)

    def flip():
        S["qkvT"][...] = S["qkv"][...].T

    def scores():
        bias = mb[...]
        for g in range(2):
            base = g * 384
            qw = windows(S["qkv"], slice(None), base)
            kw = windows(S["qkv"], slice(None), D + base)
            for h in range(16):
                w = HEAD_WIN[h]
                s = dot_t(kw[w] * hm[h:h + 1, :], qw[w]) * (HS ** -0.5 * LOG2E) + bias
                ex = jnp.exp2(s - jnp.max(s, axis=0, keepdims=True))
                S["pT"][g * 16 + h] = (ex * (1.0 / jnp.sum(ex, axis=0, keepdims=True))).astype(BF)

    def mix_values():
        for g in range(2):
            base = g * 384
            for j in range(8):
                vt = S["qkvT"][2 * D + base + 48 * j:2 * D + base + 48 * j + 48, :]
                put_heads(ctxT, base, j, dotf(vt, two(S["pT"], g * 16 + 2 * j, 1)))

    def mixed():
        S["ctx"][...] = ctxT[...].astype(BF).T
        vec[...] = x[...].astype(F32) + dotf(S["ctx"][...], wf[:, 0:D])

    def norm_f():
        S["xhf"][...], S["rf"][...], S["fn"][...] = ln_rows(vec[...], lnf[0][...], lnf[1][...])

    def act():
        u = dotf(S["fn"][...], wf[:, D:2 * D])
        u2 = u * u
        t = jnp.tanh(GELU_A * (u + GELU_B * u * u2))
        S["act"][...] = (0.5 * u * (1.0 + t)).astype(BF)
        S["gp"][...] = 0.5 * (1.0 + t) + 0.5 * u * (1.0 - t * t) * (GELU_A + 3 * GELU_A * GELU_B * u2)

    def branch():
        br = dotf(S["act"][...], wf[:, 2 * D:3 * D]).astype(BF).astype(F32)
        y[...] = (vec[...].astype(BF).astype(F32) + br).astype(BF)

    return [norm_a, project, flip, scores, mix_values, mixed, norm_f, act, branch]


def backward_stages(G, gx, waT, wfT, lna, lnf, hm, S, W, glp, gb, gctx, gctxT, gqT, gsT, vec):
    D = G.shape[1]

    def ln_back(gref, xh, r, g, gi, resid, out):
        gn = gref[...]
        x = xh[...]
        gg = gn * g
        m1 = jnp.mean(gg, axis=-1, keepdims=True)
        m2 = jnp.mean(gg * x, axis=-1, keepdims=True)
        out[...] = (r[...] * (gg - m1 - x * m2) + resid[...].astype(F32)).astype(BF)
        glp[gi:gi + 1, :] += jnp.sum(gn * x, axis=0, keepdims=True)
        glp[gi + 1:gi + 2, :] += jnp.sum(gn, axis=0, keepdims=True)

    def g_act():
        W["f"][2 * D:3 * D, :] = G[...].T
        gb[...] = (dotf(G[...], wfT[2 * D:3 * D, :]) * S["gp"][...]).astype(BF)

    def g_norm():
        W["f"][D:2 * D, :] = gb[...].T
        vec[...] = dotf(gb[...], wfT[D:2 * D, :])

    def g_hidden():
        ln_back(vec, S["xhf"], S["rf"], lnf[0][...], 2, G, gb)

    def g_context():
        W["f"][0:D, :] = gb[...].T
        t = dotf(gb[...], wfT[0:D, :]).astype(BF)
        gctx[...] = t
        gctxT[...] = t.T

    def g_scores():
        for g in range(2):
            base = g * 384
            vw = windows(S["qkv"], slice(None), 2 * D + base)
            gw = windows(gctx, slice(None), base)
            for h in range(16):
                w = HEAD_WIN[h]
                gp = dot_t(vw[w] * hm[h:h + 1, :], gw[w])
                p = S["pT"][g * 16 + h].astype(F32)
                d = jnp.sum(p * gp, axis=0, keepdims=True)
                gsT[g * 16 + h] = (p * (gp - d)).astype(BF)

    def g_heads():
        for g in range(2):
            base = g * 384
            for j in range(8):
                i = g * 16 + 2 * j
                at48 = slice(base + 48 * j, base + 48 * j + 48)
                put_heads(gqT, 2 * D + base, j, dot_t(gctxT[at48, :], two(S["pT"], i, 0)))
                put_heads(gqT, D + base, j, dot_t(S["qkvT"][at48, :], two(gsT, i, 0)) * HS ** -0.5)
                k48 = slice(D + base + 48 * j, D + base + 48 * j + 48)
                put_heads(gqT, base, j, dotf(S["qkvT"][k48, :], two(gsT, i, 1)) * HS ** -0.5)

    def g_merge():
        t = gqT[...].astype(BF)
        W["a"][...] = t
        S["qkv"][...] = t.T

    def g_input():
        vec[...] = dotf(S["qkv"][...], waT[...])

    def g_x():
        ln_back(vec, S["xha"], S["ra"], lna[0][...], 0, gb, gx)

    return [g_act, g_norm, g_hidden, g_context, g_scores, g_heads, g_merge, g_input, g_x]


def remote(src, dst, ss, rs, dev):
    return pltpu.make_async_remote_copy(
        src_ref=src, dst_ref=dst, send_sem=ss, recv_sem=rs, device_id=dev, device_id_type=MESH
    )


def when(cond, fn):
    pl.when(cond)(fn)


NZ = 4
SUB = 2
HALF = 1
ORDER = ((3, 2, 1, 0), (3, 0, 2, 1), (0, 3, 1, 2), (0, 1, 2, 3))


def by_place(vals, z):
    r = vals[-1]
    for i in range(len(vals) - 2, -1, -1):
        r = jnp.where(z == i, vals[i], r)
    return r


def rotation(mol, R):
    c0 = jnp.sum((mol == 0).astype(I32), axis=1, keepdims=True)
    c1 = jnp.sum((mol == 1).astype(I32), axis=1, keepdims=True)
    start = jnp.where(c0 == T, 0, jnp.where(c1 == T, c0, c0 + c1))
    i0 = lax.broadcasted_iota(I32, (R, R), 0)
    i1 = lax.broadcasted_iota(I32, (R, R), 1)

    def onehot(a, b):
        t = a + start
        t = jnp.where(t >= R, t - R, t)
        return jnp.where(t == b, 1.0, 0.0).astype(BF)

    return onehot(i0, i1), onehot(i1, i0)


def pair_bias(mol, key, rot, out, base, R):
    mk = jnp.concatenate([mol, key, jnp.zeros((6, R), I32)], axis=0).astype(F32).astype(BF)
    row = dot_t(mk, rot)
    col = dot_t(rot, mk)
    k0 = lax.broadcasted_iota(I32, (T, T), 0)
    q0 = lax.broadcasted_iota(I32, (T, T), 1)
    for b in range(R // T):
        rs = slice(b * T, b * T + T)
        ok = (col[rs, 0:1] == row[0:1, rs]) & ((col[rs, 1:2] > 0.5) | (k0 == q0))
        out[base + b] = jnp.where(ok, 0.0, NEG)


UNIT = ("xha", "ra", "an", "qkv", "qkvT", "pT", "ctx", "xhf", "rf", "fn", "act", "gp")


def unit_shapes(D):
    return (
        ((T, D), F32), ((T, 1), F32), ((T, D), BF), ((T, 3 * D), BF), ((3 * D, T), BF),
        ((HEADS, T, T), BF), ((T, D), BF), ((T, D), F32), ((T, 1), F32),
        ((T, D), BF), ((T, D), BF), ((T, D), F32),
    )


def relay_kernel(fused, tok, cot, w, gain, bias, mol, key, fo_hbm, ig_hbm, w_hbm, *scr):
    R, D = tok.shape
    norms, scr = (scr[:2], scr[2:]) if fused else (scr[:1], scr[1:])
    n = len(UNIT)
    U = {k: r for k, r in zip(UNIT, scr[:n])}
    (
        wa, wf, waT, wfT, lga, lba, lgf, lbf, molo, keyo, rinv, hm, mb, X, G, ex, ys, gx, fob, igb,
        acca, accf, wga, wgf, rb, glp, glr, vec, gb, gctx, gctxT, gqT, gsT,
        wl_s, w_s, w_r, l_s, l_r, m_s, m_r, ex_s, ex_r, y_s, y_r, fo_s, fo_r, g_s, g_r, ig_s, ig_r,
        p_s, p_r, gl_s, gl_r, fo, ig, o_s,
    ) = scr[n:n + 57]
    s = lax.axis_index("section")
    e = lax.rem(s, 2)
    L = s // 2
    mate = {"section": s + 1 - 2 * e}
    other = {"section": s + 2 - 4 * L}
    d = lax.axis_index("dp")
    z = d // 2
    y = d - 2 * z
    across = {"dp": d + 1 - 2 * y}

    def on_line(zz):
        return {"dp": zz * 2 + y}

    bar = pltpu.get_barrier_semaphore()
    peers = [mate, other]
    if fused:
        peers += [across] + [on_line(lax.rem(z + t, NZ)) for t in range(1, NZ)]
    for p in peers:
        pl.semaphore_signal(bar, inc=1, device_id=p, device_id_type=MESH)
    pl.semaphore_wait(bar, len(peers))

    def third(c):
        return (slice(None), pl.ds(c * D, D))

    def w_local(k, j):
        src = (w, gain, bias)[j]
        return pltpu.make_async_copy(src, own[k][j], wl_s.at[j])

    def w_rem(k, j):
        if j < 3:
            return remote(w.at[third(j)], own[k][0].at[third(j)], w_s.at[j], w_r.at[j], mate)
        src = (gain, bias)[j - 3]
        return remote(src, own[k][j - 2], l_s.at[j - 3], l_r.at[j - 3], mate)

    own = ((wa, lga, lba), (wf, lgf, lbf))

    def per_core(fn):
        when(e == 0, lambda: fn(0))
        when(e == 1, lambda: fn(1))

    def send_weights(k):
        for j in (3, 4):
            w_rem(k, j).start()
        for j in range(3):
            w_local(k, j).start()
        for j in range(3):
            w_rem(k, j).start()

    per_core(send_weights)
    mol_copy = remote(mol, molo, m_s.at[0], m_r.at[0], other)
    key_copy = remote(key, keyo, m_s.at[1], m_r.at[1], other)
    mol_copy.start()
    key_copy.start()

    rot, inv = rotation(mol[...], R)
    rinv[...] = inv
    xr = dotf(rot, tok[...]).astype(BF)
    cr = dotf(rot, cot[...]).astype(BF)
    xu = xr.reshape(2, T, D)
    cu = cr.reshape(2, T, D)

    def ex_copy(dst):
        return remote(ex, dst, ex_s, ex_r, other)

    def stage0():
        ex[...] = cu
        ex_copy(G.at[pl.ds(0, 2)]).start()
        X[0:2] = xu

    def stage1():
        ex[...] = xu
        ex_copy(X.at[pl.ds(2, 2)]).start()
        G[2:4] = cu

    when(L == 0, stage0)
    when(L == 1, stage1)
    i0 = lax.broadcasted_iota(I32, (16, 256), 0)
    i1 = lax.broadcasted_iota(I32, (16, 256), 1)
    lo = HS * i0 - jnp.where(i0 < 10, 0, 128)
    hm[...] = jnp.where((i1 >= lo) & (i1 < lo + HS), 1.0, 0.0).astype(BF)
    glp[...] = jnp.zeros_like(glp)
    mol_copy.wait()
    key_copy.wait()
    pair_bias(mol[...], key[...], rot, mb, 2 * L, R)
    rot_o, _ = rotation(molo[...], R)
    pair_bias(molo[...], keyo[...], rot_o, mb, 2 - 2 * L, R)

    def wait_local(k):
        for j in range(3):
            w_local(k, j).wait()
        for j in (3, 4):
            w_rem(1 - k, j).wait_recv()

    per_core(wait_local)

    def wait_third(k, c):
        w_rem(k, c).wait_recv()

    def turn_weights():
        @pl.loop(0, 3)
        def _(i):
            cs = at(i, D)
            waT[cs, :] = wa[:, cs].T
            wfT[cs, :] = wf[:, cs].T

    def wait_all(k):
        for c in range(3):
            wait_third(1 - k, c)

    def ready1():
        per_core(wait_all)
        turn_weights()

    when(L == 1, ready1)

    def grads(acc, wg, rhs, p, first):
        for c in range(3):
            rs = slice(c * D, c * D + D)
            v = dotf(wg[p, rs, :], rhs[c][2 * p:2 * p + 2].reshape(2 * T, D))
            if not first:
                v = v + acc[rs, :].astype(F32)
            acc[rs, :] = v.astype(BF)

    def grads_f(p, first):
        grads(accf, wgf, (U["ctx"], U["fn"], U["act"]), p, first)

    def grads_a(p, first):
        grads(acca, wga, (U["an"],) * 3, p, first)

    if fused:
        yb, inb, raw, acc, gy, gz, gn, out_w, ry_s, ry_r, rz_s, rz_r, rw_s, rw_r, rg_s, rg_r = scr[n + 57:]
        CH = 3 * D // (2 * NZ)
        SR = CH // SUB
        dest = [by_place([ORDER[k][i] for k in range(NZ)], z) for i in range(NZ)]
        buddy = z + 1 - 2 * lax.rem(z, 2)

        def rows(zz, yy, q):
            return pl.ds(pl.multiple_of((zz * 2 + yy) * CH + q * SR, 16), SR)

        def y_copy(i, q):
            return remote(rb.at[rows(dest[i], 1 - y, q), :], yb.at[i, q], ry_s.at[i, q], ry_r.at[i, q], across)

        def raw_copy(q):
            return remote(
                rb.at[rows(buddy, 1 - y, q), :], raw.at[q], rw_s.at[q], rw_r.at[q], on_line(buddy)
            )

        def piece(i):
            return pl.ds(pl.multiple_of(dest[i] * (2 * CH), 16), 2 * CH)
    else:
        def piece(i):
            return pl.ds(i * (3 * D // NZ), 3 * D // NZ)

    def p_copy(i, src):
        return remote(src.at[piece(i), :], rb.at[piece(i), :], p_s.at[i], p_r.at[i], mate)

    def give(src):
        for i in range(NZ):
            p_copy(i, src).start()

    def take(mine):
        for i in range(NZ):
            p_copy(i, mine).wait_recv()
            r = piece(i)
            rb[r, :] = (rb[r, :].astype(F32) + mine[r, :].astype(F32)).astype(BF)
            if fused and i < NZ - 1:
                def to_buddy():
                    for q in range(HALF):
                        raw_copy(q).start()

                def halves(i=i):
                    for q in range(HALF):
                        y_copy(i, q).start()

                when(dest[i] == buddy, to_buddy)
                when(dest[i] != buddy, halves)
                for q in range(HALF, SUB):
                    y_copy(i, q).start()

    def f_last():
        grads_f(1, False)
        when(e == 0, lambda: give(accf))

    def f_take():
        when(e == 1, lambda: take(accf))

    def a_last():
        rhs = U["an"][2:4].reshape(2 * T, D)
        for i in range(NZ):
            r = piece(i)
            acca[r, :] = (dotf(wga[1, r, :], rhs) + acca[r, :].astype(F32)).astype(BF)
            when(e == 1, lambda i=i: p_copy(i, acca).start())

    def y_copy_x(u):
        return remote(ys.at[u], X.at[u], y_s.at[u], y_r.at[u], other)

    def fo_copy(u):
        return remote(ys.at[u], fob.at[u], fo_s.at[u], fo_r.at[u], other)

    def g_copy(u):
        return remote(gx.at[u], G.at[u], g_s.at[u], g_r.at[u], other)

    def ig_copy(u):
        return remote(gx.at[u], igb.at[u - 2], ig_s.at[u - 2], ig_r.at[u - 2], other)

    def forward(u):
        S = {k: r.at[u] for k, r in U.items()}
        when(L == 1, lambda: y_copy_x(u).wait_recv())
        when((L == 0) & (u == 2), lambda: ex_copy(X.at[pl.ds(2, 2)]).wait_recv())
        opening = (L == 0) & (u == 0)
        st = forward_stages(
            X.at[u], ys.at[u], wa, wf, (lga, lba), (lgf, lbf), mb.at[u], hm, S, gqT.at[pl.ds(0, D)], vec
        )
        for f in st:
            if f.__name__ == "project":
                when(opening & (e == 1), lambda: wait_all(1))
            if f.__name__ in ("mixed", "act", "branch"):
                c = ("mixed", "act", "branch").index(f.__name__)
                when(opening & (e == 0), lambda c=c: wait_third(1, c))
            f()
        when(L == 0, lambda: y_copy_x(u).start())
        when((L == 1) & (u < 2), lambda: fo_copy(u).start())

        def keep():
            fob[u - 2] = ys[u]

        when((L == 1) & (u >= 2), keep)

    def backward(u):
        S = {k: r.at[u] for k, r in U.items()}
        when((L == 0) & (u == 0), turn_weights)
        when((L == 1) & (u == 0), lambda: ex_copy(G.at[pl.ds(0, 2)]).wait_recv())
        when(L == 0, lambda: g_copy(u).wait_recv())
        last = (L == 0) & (u == 3)
        p = u // 2
        lanes = at(u - 2 * p, T)
        st = backward_stages(
            G.at[u], gx.at[u], waT, wfT, (lga, lba), (lgf, lbf), hm, S,
            {"a": wga.at[p, :, lanes], "f": wgf.at[p, :, lanes]},
            glp, gb, gctx, gctxT, gqT, gsT, vec,
        )
        for f in st:
            f()
            if f.__name__ == "g_context":
                when(last, f_last)
            if f.__name__ == "g_merge":
                when(last, a_last)
                when(last, f_take)
        when(L == 1, lambda: g_copy(u).start())
        when((L == 0) & (u >= 2), lambda: ig_copy(u).start())

        def keep():
            igb[u] = gx[u]

        def first_pair():
            grads_f(0, True)
            grads_a(0, True)

        when((L == 0) & (u < 2), keep)
        when((L == 0) & (u == 1), first_pair)

    @pl.loop(0, 8)
    def _(i):
        odd = lax.rem(i, 2)
        is_f = jnp.where(L == 0, jnp.where(i < 4, 1, 0), 1 - odd)
        u = jnp.where(L == 0, lax.rem(i, 4), i // 2)
        when(is_f == 1, lambda: forward(u))
        when(is_f == 0, lambda: backward(u))

    def finish1():
        grads_f(0, True)
        f_last()
        grads_a(0, True)
        a_last()
        f_take()

    when(L == 1, finish1)
    gl_copy = remote(glp, glr, gl_s, gl_r, mate)
    gl_copy.start()
    when(e == 0, lambda: take(acca))

    def bring0():
        for u in range(2):
            fo_copy(u).wait_recv()

    def bring1():
        for u in (2, 3):
            ig_copy(u).wait_recv()

    when(L == 0, bring0)
    when(L == 1, bring1)
    fo[...] = dotf(rinv[...], fob[...].reshape(R, D)).astype(BF)
    ig[...] = dotf(rinv[...], igb[...].reshape(R, D))
    emits = [pltpu.make_async_copy(fo, fo_hbm, o_s.at[0]), pltpu.make_async_copy(ig, ig_hbm, o_s.at[1])]
    for c in emits:
        c.start()
    gl_copy.wait()

    if fused:
        gl1 = glp[...] + glr[...]
        glr[...] = gl1
        gy_copy = remote(glr, gy, rg_s.at[0], rg_r.at[0], across)
        gy_copy.start()

        def own_y():
            for q in range(SUB):
                if q < HALF:
                    raw_copy(q).wait()
                    r = rows(z, 1 - y, q)
                    rb[r, :] = (rb[r, :].astype(F32) + raw[q].astype(F32)).astype(BF)
                y_copy(NZ - 1, q).start()

        def hop(i, q):
            zz = dest[i]
            nz = jnp.where(zz > z, z + 1, z - 1)
            slot = jnp.where((nz == zz) & (z > zz), NZ, zz)
            return remote(yb.at[i, q], inb.at[slot, q], rz_s.at[i, q], rz_r.at[slot, q], on_line(nz))

        def arrived(slot, q):
            remote(yb.at[0, q], inb.at[slot, q], rz_s.at[0, q], rz_r.at[slot, q], across).wait_recv()

        for i in range(NZ - 1):
            zz = dest[i]
            for q in range(SUB):
                mine = rb.at[rows(zz, y, q), :]

                def combine(i=i, q=q, mine=mine):
                    y_copy(i, q).wait_recv()
                    yb[i, q] = (mine[...].astype(F32) + yb[i, q].astype(F32)).astype(BF)

                def plain(i=i, q=q, mine=mine):
                    yb[i, q] = mine[...]

                def add_in(i=i, q=q, zz=zz):
                    arrived(zz, q)
                    yb[i, q] = (yb[i, q].astype(F32) + inb[zz, q].astype(F32)).astype(BF)

                if q < HALF:
                    when(zz != buddy, combine)
                    when(zz == buddy, plain)
                else:
                    combine()
                when(jnp.where(zz > z, z > 0, z < NZ - 1), add_in)
                hop(i, q).start()
            if i == NZ - 3:
                own_y()
        gy_copy.wait()
        gl2 = glr[...] + gy[...]
        gn[...] = gl2
        gz_copies = [
            remote(gn, gz.at[NZ - t - 1], rg_s.at[t], rg_r.at[NZ - t], on_line(lax.rem(z + t, NZ)))
            for t in range(1, NZ)
        ]
        for c in gz_copies:
            c.start()
        for q in range(SUB):
            acc[q] = rb[rows(z, y, q), :].astype(F32)

            def from_left(q=q):
                arrived(z, q)
                acc[q] += inb[z, q].astype(F32)

            def from_right(q=q):
                arrived(NZ, q)
                acc[q] += inb[NZ, q].astype(F32)

            when(z > 0, from_left)
            when(z < NZ - 1, from_right)
            y_copy(NZ - 1, q).wait_recv()
            acc[q] += yb[NZ - 1, q].astype(F32)
        out_w[...] = acc[...].reshape(CH, D)
        w_copy = pltpu.make_async_copy(out_w, w_hbm, o_s.at[2])
        w_copy.start()
        for i in range(NZ):
            for q in range(SUB):
                if q < HALF and i < NZ - 1:
                    when(dest[i] != buddy, lambda i=i, q=q: y_copy(i, q).wait_send())
                else:
                    y_copy(i, q).wait_send()
                if i < NZ - 1:
                    hop(i, q).wait_send()
        for t, c in zip(range(1, NZ), gz_copies):
            c.wait_send()
        for k in range(NZ - 1):
            remote(gn, gz.at[k], rg_s.at[0], rg_r.at[k + 1], across).wait_recv()
        gl3 = gl2 + gz[0] + gz[1] + gz[2]
        part = D // (2 * NZ)
        for k in range(2 * NZ):
            def own_part(k=k):
                for j in range(2):
                    v = gl3[:, k * part:(k + 1) * part]
                    norms[j][...] = jnp.where(e == 0, v[j:j + 1, :], v[2 + j:3 + j, :])

            when(d == k, own_part)
    else:
        norms[0][...] = glp[...] + glr[...]
        w_copy = pltpu.make_async_copy(rb, w_hbm, o_s.at[2])
        w_copy.start()
    for c in emits + [w_copy]:
        c.wait()

    def close_weights(k):
        for j in range(5):
            w_rem(k, j).wait_send()

    per_core(close_weights)
    def gave(src):
        for i in range(NZ):
            p_copy(i, src).wait_send()

    when(e == 0, lambda: gave(accf))
    when(e == 1, lambda: gave(acca))
    ex_copy(X.at[pl.ds(2, 2)]).wait_send()

    def close0():
        for u in range(4):
            y_copy_x(u).wait_send()
        for u in (2, 3):
            ig_copy(u).wait_send()

    def close1():
        for u in range(4):
            g_copy(u).wait_send()
        for u in range(2):
            fo_copy(u).wait_send()

    when(L == 0, close0)
    when(L == 1, close1)


def relay(fused, tok, cot, w, gain, bias, mol, key):
    R, D = tok.shape
    V = pl.BlockSpec(memory_space=pltpu.VMEM)
    dma, vm = pltpu.SemaphoreType.DMA, pltpu.VMEM
    scratch = [vm((4,) + sh, dt) for sh, dt in unit_shapes(D)] + [
        vm((D, 3 * D), BF), vm((D, 3 * D), BF), vm((3 * D, D), BF), vm((3 * D, D), BF),
        vm((1, D), F32), vm((1, D), F32), vm((1, D), F32), vm((1, D), F32),
        vm((1, R), I32), vm((1, R), I32), vm((R, R), BF), vm((16, 256), BF), vm((4, T, T), F32),
        vm((4, T, D), BF), vm((4, T, D), BF), vm((2, T, D), BF), vm((4, T, D), BF), vm((4, T, D), BF),
        vm((2, T, D), BF), vm((2, T, D), BF),
        vm((3 * D, D), BF), vm((3 * D, D), BF), vm((2, 3 * D, 2 * T), BF), vm((2, 3 * D, 2 * T), BF),
        vm((3 * D, D), BF), vm((8, D), F32), vm((8, D), F32),
        vm((T, D), F32), vm((T, D), BF), vm((T, D), BF), vm((D, T), BF),
        vm((3 * D, T), F32), vm((HEADS, T, T), BF),
        dma((3,)), dma((3,)), dma((3,)), dma((2,)), dma((2,)), dma((2,)), dma((2,)), dma, dma,
        dma((4,)), dma((4,)), dma((2,)), dma((2,)), dma((4,)), dma((4,)), dma((2,)), dma((2,)),
        dma((NZ,)), dma((NZ,)), dma, dma, vm((R, D), BF), vm((R, D), F32), dma((3,)),
    ]
    if fused:
        CH = 3 * D // (2 * NZ)
        SR = CH // SUB
        scratch += [
            vm((NZ, SUB, SR, D), BF), vm((NZ + 1, SUB, SR, D), BF), vm((HALF, SR, D), BF),
            vm((SUB, SR, D), F32), vm((8, D), F32), vm((NZ - 1, 8, D), F32), vm((8, D), F32), vm((CH, D), F32),
            dma((NZ, SUB)), dma((NZ, SUB)), dma((NZ - 1, SUB)), dma((NZ + 1, SUB)),
            dma((HALF,)), dma((HALF,)), dma((NZ,)), dma((NZ,)),
        ]
        outs = [jax.ShapeDtypeStruct((CH, D), F32)] + [jax.ShapeDtypeStruct((1, D // (2 * NZ)), F32)] * 2
    else:
        outs = [jax.ShapeDtypeStruct((3 * D, D), BF), jax.ShapeDtypeStruct((8, D), F32)]
    A = pl.BlockSpec(memory_space=pl.ANY)
    return pl.pallas_call(
        lambda *refs: relay_kernel(fused, *refs),
        out_shape=[jax.ShapeDtypeStruct((R, D), BF), jax.ShapeDtypeStruct((R, D), F32)] + outs,
        in_specs=[V, V, A, V, V, V, V],
        out_specs=[A, A, A] + [V] * (len(outs) - 1),
        scratch_shapes=scratch,
        compiler_params=pltpu.CompilerParams(
            collective_id=0, has_side_effects=True, vmem_limit_bytes=64 << 20
        ),
        name="relay",
    )(tok, cot, w, gain, bias, mol, key)


def emit_kernel(*refs):
    n = len(refs) // 3
    sems = refs[-1]
    ins = [pltpu.make_async_copy(refs[i], refs[2 * n + i], sems.at[0, i]) for i in range(n)]
    outs = [pltpu.make_async_copy(refs[2 * n + i], refs[n + i], sems.at[1, i]) for i in range(n)]
    for c in ins:
        c.start()
    for a, b in zip(ins, outs):
        a.wait()
        b.start()
    for c in outs:
        c.wait()


def emit(arrays):
    A = pl.BlockSpec(memory_space=pl.ANY)
    n = len(arrays)
    return pl.pallas_call(
        emit_kernel,
        out_shape=[jax.ShapeDtypeStruct(a.shape, a.dtype) for a in arrays],
        in_specs=[A] * n,
        out_specs=[A] * n,
        scratch_shapes=[pltpu.VMEM(a.shape, a.dtype) for a in arrays] + [pltpu.SemaphoreType.DMA((2, n))],
        name="emit",
    )(*arrays)


def shards(tokens, cotangent, section_weight, norm_gain, norm_bias, mol_ids, key_mask):
    fused = lax.axis_size("dp") == 2 * NZ
    got = relay(fused, tokens, cotangent, section_weight[0], norm_gain, norm_bias, mol_ids, key_mask)
    if fused:
        fo, ig, gw, gg, gb = emit(got)
        return fo, ig, gw.T[None], gg, gb
    fo, ig, gw, gn = got
    e = lax.rem(lax.axis_index("section"), 2)
    gn = lax.dynamic_slice_in_dim(gn, 2 * e, 2, 0)
    gw = lax.psum_scatter(gw, "dp", scatter_dimension=0, tiled=True)
    gn = lax.psum_scatter(gn, "dp", scatter_dimension=1, tiled=True)
    return fo, ig, gw.astype(F32).T[None], gn[0:1], gn[1:2]


def solution(mesh):
    return jax.shard_map(
        shards,
        mesh=mesh,
        in_specs=(
            P(("dp", "section"), None),
            P(("dp", "section"), None),
            P("section", None, None),
            P("section", None),
            P("section", None),
            P(("dp", "section"), None),
            P(("dp", "section"), None),
        ),
        out_specs=(
            P(("dp", "section"), None),
            P(("dp", "section"), None),
            P("section", None, "dp"),
            P("section", "dp"),
            P("section", "dp"),
        ),
        check_vma=False,
    )
```

```python
import jax
import jax.numpy as jnp
from jax import lax
from jax.experimental import pallas as pl
from jax.experimental.pallas import tpu as pltpu
from jax.sharding import PartitionSpec as P

HEADS = 32
HS = 24
EPS = 1e-5
NEG = -1e30
BF = jnp.bfloat16
F32 = jnp.float32
I32 = jnp.int32
MESH = pl.DeviceIdType.MESH
GELU_A = 0.7978845608028654
GELU_B = 0.044715
LOG2E = 1.4426950408889634
T = 128


def dotf(a, b):
    return jnp.dot(a, b, preferred_element_type=F32)


def dot_t(a, b):
    return lax.dot_general(a, b, (((1,), (1,)), ((), ())), preferred_element_type=F32)


def at(i, n):
    return pl.ds(pl.multiple_of(i * n, n), n)


HEAD_WIN = (0,) * 10 + (1,) * 6


def ln_rows(x, g, b):
    c = x - jnp.mean(x, axis=-1, keepdims=True)
    r = lax.rsqrt(jnp.mean(c * c, axis=-1, keepdims=True) + EPS)
    xh = c * r
    return xh, r, (xh * g + b).astype(BF)


def windows(ref, rows, base):
    return [ref[rows, base + 128 * w:base + 128 * w + 256] for w in (0, 1)]


def put_heads(ref, base, j, v):
    ref[base + 48 * j:base + 48 * j + 24, :] = v[0:24, 0:T]
    ref[base + 48 * j + 24:base + 48 * j + 48, :] = v[24:48, T:2 * T]


def two(ref, i, axis):
    return jnp.concatenate([ref[i], ref[i + 1]], axis=axis)


def forward_stages(x, y, wa, wf, lna, lnf, mb, hm, S, ctxT, vec):
    D = x.shape[1]

    def norm_a():
        S["xha"][...], S["ra"][...], S["an"][...] = ln_rows(x[...].astype(F32), lna[0][...], lna[1][...])

    def project():
        S["qkv"][...] = dotf(S["an"][...], wa[...]).astype(BF)

    def flip():
        S["qkvT"][...] = S["qkv"][...].T

    def scores():
        bias = mb[...]
        for g in range(2):
            base = g * 384
            qw = windows(S["qkv"], slice(None), base)
            kw = windows(S["qkv"], slice(None), D + base)
            for h in range(16):
                w = HEAD_WIN[h]
                s = dot_t(kw[w] * hm[h:h + 1, :], qw[w]) * (HS ** -0.5 * LOG2E) + bias
                ex = jnp.exp2(s - jnp.max(s, axis=0, keepdims=True))
                S["pT"][g * 16 + h] = (ex * (1.0 / jnp.sum(ex, axis=0, keepdims=True))).astype(BF)

    def mix_values():
        for g in range(2):
            base = g * 384
            for j in range(8):
                vt = S["qkvT"][2 * D + base + 48 * j:2 * D + base + 48 * j + 48, :]
                put_heads(ctxT, base, j, dotf(vt, two(S["pT"], g * 16 + 2 * j, 1)))

    def mixed():
        S["cfa"][0] = ctxT[...].astype(BF).T
        vec[...] = x[...].astype(F32) + dotf(S["cfa"][0], wf[:, 0:D])

    def norm_f():
        S["xhf"][...], S["rf"][...], S["cfa"][1] = ln_rows(vec[...], lnf[0][...], lnf[1][...])

    def act():
        u = dotf(S["cfa"][1], wf[:, D:2 * D])
        u2 = u * u
        t = jnp.tanh(GELU_A * (u + GELU_B * u * u2))
        S["cfa"][2] = (0.5 * u * (1.0 + t)).astype(BF)
        S["gp"][...] = 0.5 * (1.0 + t) + 0.5 * u * (1.0 - t * t) * (GELU_A + 3 * GELU_A * GELU_B * u2)

    def branch():
        br = dotf(S["cfa"][2], wf[:, 2 * D:3 * D]).astype(BF).astype(F32)
        y[...] = (vec[...].astype(BF).astype(F32) + br).astype(BF)

    return [norm_a, project, flip, scores, mix_values, mixed, norm_f, act, branch]


def backward_stages(G, gx, waT, wfT, lna, lnf, hm, S, W, glp, gb, gctx, gctxT, gqT, gsT, vec):
    D = G.shape[1]

    def ln_back(gref, xh, r, g, gi, resid, out):
        gn = gref[...]
        x = xh[...]
        gg = gn * g
        m1 = jnp.mean(gg, axis=-1, keepdims=True)
        m2 = jnp.mean(gg * x, axis=-1, keepdims=True)
        out[...] = (r[...] * (gg - m1 - x * m2) + resid[...].astype(F32)).astype(BF)
        glp[gi:gi + 1, :] += jnp.sum(gn * x, axis=0, keepdims=True)
        glp[gi + 1:gi + 2, :] += jnp.sum(gn, axis=0, keepdims=True)

    def g_act():
        W["f"][2 * D:3 * D, :] = G[...].T
        gb[...] = (dotf(G[...], wfT[2 * D:3 * D, :]) * S["gp"][...]).astype(BF)

    def g_norm():
        W["f"][D:2 * D, :] = gb[...].T
        vec[...] = dotf(gb[...], wfT[D:2 * D, :])

    def g_hidden():
        ln_back(vec, S["xhf"], S["rf"], lnf[0][...], 2, G, gb)

    def g_context():
        W["f"][0:D, :] = gb[...].T
        t = dotf(gb[...], wfT[0:D, :]).astype(BF)
        gctx[...] = t
        gctxT[...] = t.T

    def g_scores():
        for g in range(2):
            base = g * 384
            vw = windows(S["qkv"], slice(None), 2 * D + base)
            gw = windows(gctx, slice(None), base)
            for h in range(16):
                w = HEAD_WIN[h]
                gp = dot_t(vw[w] * hm[h:h + 1, :], gw[w])
                p = S["pT"][g * 16 + h].astype(F32)
                d = jnp.sum(p * gp, axis=0, keepdims=True)
                gsT[g * 16 + h] = (p * (gp - d)).astype(BF)

    def g_heads():
        for g in range(2):
            base = g * 384
            for j in range(8):
                i = g * 16 + 2 * j
                at48 = slice(base + 48 * j, base + 48 * j + 48)
                put_heads(gqT, 2 * D + base, j, dot_t(gctxT[at48, :], two(S["pT"], i, 0)))
                put_heads(gqT, D + base, j, dot_t(S["qkvT"][at48, :], two(gsT, i, 0)) * HS ** -0.5)
                k48 = slice(D + base + 48 * j, D + base + 48 * j + 48)
                put_heads(gqT, base, j, dotf(S["qkvT"][k48, :], two(gsT, i, 1)) * HS ** -0.5)

    def g_merge():
        t = gqT[...].astype(BF)
        W["a"][...] = t
        S["qkv"][...] = t.T

    def g_input():
        vec[...] = dotf(S["qkv"][...], waT[...])

    def g_x():
        ln_back(vec, S["xha"], S["ra"], lna[0][...], 0, gb, gx)

    return [g_act, g_norm, g_hidden, g_context, g_scores, g_heads, g_merge, g_input, g_x]


def remote(src, dst, ss, rs, dev):
    return pltpu.make_async_remote_copy(
        src_ref=src, dst_ref=dst, send_sem=ss, recv_sem=rs, device_id=dev, device_id_type=MESH
    )


def when(cond, fn):
    pl.when(cond)(fn)


NZ = 4
SUB = 2
HALF = 1
ORDER = ((3, 2, 1, 0), (3, 0, 2, 1), (0, 3, 1, 2), (0, 1, 2, 3))


def by_place(vals, z):
    r = vals[-1]
    for i in range(len(vals) - 2, -1, -1):
        r = jnp.where(z == i, vals[i], r)
    return r


def rotation(mol, R):
    c0 = jnp.sum((mol == 0).astype(I32), axis=1, keepdims=True)
    c1 = jnp.sum((mol == 1).astype(I32), axis=1, keepdims=True)
    start = jnp.where(c0 == T, 0, jnp.where(c1 == T, c0, c0 + c1))
    i0 = lax.broadcasted_iota(I32, (R, R), 0)
    i1 = lax.broadcasted_iota(I32, (R, R), 1)

    def onehot(a, b):
        t = a + start
        t = jnp.where(t >= R, t - R, t)
        return jnp.where(t == b, 1.0, 0.0).astype(BF)

    return onehot(i0, i1), onehot(i1, i0)


def pair_bias(mol, key, rot, out, base, R):
    mk = jnp.concatenate([mol, key, jnp.zeros((6, R), I32)], axis=0).astype(F32).astype(BF)
    row = dot_t(mk, rot)
    col = dot_t(rot, mk)
    k0 = lax.broadcasted_iota(I32, (T, T), 0)
    q0 = lax.broadcasted_iota(I32, (T, T), 1)
    for b in range(R // T):
        rs = slice(b * T, b * T + T)
        ok = (col[rs, 0:1] == row[0:1, rs]) & ((col[rs, 1:2] > 0.5) | (k0 == q0))
        out[base + b] = jnp.where(ok, 0.0, NEG)


UNIT = ("xha", "ra", "an", "qkv", "qkvT", "pT", "xhf", "rf", "cfa", "gp")


def unit_shapes(D):
    return (
        ((T, D), F32), ((T, 1), F32), ((T, D), BF), ((T, 3 * D), BF), ((3 * D, T), BF),
        ((HEADS, T, T), BF), ((T, D), F32), ((T, 1), F32), ((3, T, D), BF), ((T, D), F32),
    )


def relay_kernel(fused, tok, cot, w, gain, bias, mol, key, fo_hbm, ig_hbm, w_hbm, *scr):
    R, D = tok.shape
    norms, scr = (scr[:2], scr[2:]) if fused else (scr[:1], scr[1:])
    n = len(UNIT)
    U = {k: r for k, r in zip(UNIT, scr[:n])}
    (
        wa, wf, waT, wfT, lga, lba, lgf, lbf, molo, keyo, rinv, hm, mb, X, G, ex, ys, gx, fob, igb,
        wta, wtf, mw, mr, rb, glp, glr, vec, gb, gctx, gctxT, gqT, gsT,
        wl_s, w_s, w_r, l_s, l_r, m_s, m_r, ex_s, ex_r, y_s, y_r, fo_s, fo_r, g_s, g_r, ig_s, ig_r,
        mw_s, mw_r, mr_s, mr_r, q_s, q_r, gl_s, gl_r, fo, ig, o_s,
    ) = scr[n:n + 61]
    s = lax.axis_index("section")
    e = lax.rem(s, 2)
    L = s // 2
    mate = {"section": s + 1 - 2 * e}
    other = {"section": s + 2 - 4 * L}
    d = lax.axis_index("dp")
    z = d // 2
    y = d - 2 * z
    across = {"dp": d + 1 - 2 * y}

    def on_line(zz):
        return {"dp": zz * 2 + y}

    bar = pltpu.get_barrier_semaphore()
    peers = [mate, other]
    if fused:
        peers += [across] + [on_line(lax.rem(z + t, NZ)) for t in range(1, NZ)]
    for p in peers:
        pl.semaphore_signal(bar, inc=1, device_id=p, device_id_type=MESH)
    pl.semaphore_wait(bar, len(peers))

    def third(c):
        return (slice(None), pl.ds(c * D, D))

    def w_local(k, j):
        src = (w, gain, bias)[j]
        return pltpu.make_async_copy(src, own[k][j], wl_s.at[j])

    def w_rem(k, j):
        if j < 3:
            return remote(w.at[third(j)], own[k][0].at[third(j)], w_s.at[j], w_r.at[j], mate)
        src = (gain, bias)[j - 3]
        return remote(src, own[k][j - 2], l_s.at[j - 3], l_r.at[j - 3], mate)

    own = ((wa, lga, lba), (wf, lgf, lbf))

    def per_core(fn):
        when(e == 0, lambda: fn(0))
        when(e == 1, lambda: fn(1))

    def send_weights(k):
        for j in (3, 4):
            w_rem(k, j).start()
        for j in range(3):
            w_local(k, j).start()

    def send_thirds(k):
        for j in range(3):
            w_rem(k, j).start()

    per_core(send_weights)
    when((L == 1) & (e == 0), lambda: send_thirds(0))
    when(e == 1, lambda: send_thirds(1))
    mol_copy = remote(mol, molo, m_s.at[0], m_r.at[0], other)
    key_copy = remote(key, keyo, m_s.at[1], m_r.at[1], other)
    mol_copy.start()
    key_copy.start()

    rot, inv = rotation(mol[...], R)
    rinv[...] = inv
    xr = dotf(rot, tok[...]).astype(BF)
    cr = dotf(rot, cot[...]).astype(BF)
    xu = xr.reshape(2, T, D)
    cu = cr.reshape(2, T, D)

    def ex_copy(dst):
        return remote(ex, dst, ex_s, ex_r, other)

    def stage0():
        ex[...] = cu
        ex_copy(G.at[pl.ds(0, 2)]).start()
        X[0:2] = xu

    def stage1():
        ex[...] = xu
        ex_copy(X.at[pl.ds(2, 2)]).start()
        G[2:4] = cu

    when(L == 0, stage0)
    when(L == 1, stage1)
    i0 = lax.broadcasted_iota(I32, (16, 256), 0)
    i1 = lax.broadcasted_iota(I32, (16, 256), 1)
    lo = HS * i0 - jnp.where(i0 < 10, 0, 128)
    hm[...] = jnp.where((i1 >= lo) & (i1 < lo + HS), 1.0, 0.0).astype(BF)
    glp[...] = jnp.zeros_like(glp)
    mol_copy.wait()
    key_copy.wait()
    pair_bias(mol[...], key[...], rot, mb, 2 * L, R)
    rot_o, _ = rotation(molo[...], R)
    pair_bias(molo[...], keyo[...], rot_o, mb, 2 - 2 * L, R)

    def wait_local(k):
        for j in range(3):
            w_local(k, j).wait()
        for j in (3, 4):
            w_rem(1 - k, j).wait_recv()

    per_core(wait_local)

    def wait_third(k, c):
        w_rem(k, c).wait_recv()

    def turn_weights():
        @pl.loop(0, 3)
        def _(i):
            cs = at(i, D)
            waT[cs, :] = wa[:, cs].T
            wfT[cs, :] = wf[:, cs].T

    def wait_all(k):
        for c in range(3):
            wait_third(1 - k, c)

    def ready1():
        per_core(wait_all)
        turn_weights()

    when(L == 1, ready1)

    def mw_copy(k, u):
        return remote((wta, wtf)[k].at[u], mw.at[u], mw_s.at[u], mw_r.at[u], mate)

    def mr_copy(k, u, c):
        src = (U["an"].at[u], U["cfa"].at[u, c])[k]
        return remote(src, mr.at[u, c], mr_s.at[u, c], mr_r.at[u, c], mate)

    def mine(k, u, r, c):
        left = jnp.concatenate([(wta, wtf)[k][u, r, :], mw[u, r, :]], axis=1)
        right = jnp.concatenate([U["an"][u] if k == 0 else U["cfa"][u, c], mr[u, c]], axis=0)
        return left, right

    def pair_dot(k, p, r, c):
        a, b = mine(k, 2 * p, r, c), mine(k, 2 * p + 1, r, c)
        return dotf(jnp.concatenate([a[0], b[0]], axis=1), jnp.concatenate([a[1], b[1]], axis=0))

    def wait_factors(k, us):
        for u in us:
            mw_copy(k, u).wait_recv()
            for c in range(1 if k == 0 else 3):
                if k == 0 and u == 0:
                    when(L == 1, lambda: mr_copy(0, 0, 0).wait_recv())
                else:
                    mr_copy(1, u, c).wait_recv()

    def first_pair(k):
        wait_factors(k, (0, 1))
        for c in range(3):
            r = slice(c * D, c * D + D)
            rb[r, :] = pair_dot(k, 0, r, 0 if k == 0 else c).astype(BF)

    if fused:
        yb, inb, raw, acc, gy, gz, gn, out_w, ry_s, ry_r, rz_s, rz_r, rw_s, rw_r, rg_s, rg_r = scr[n + 61:]
        CH = 3 * D // (2 * NZ)
        SR = CH // SUB
        dest = [by_place([ORDER[k][i] for k in range(NZ)], z) for i in range(NZ)]
        buddy = z + 1 - 2 * lax.rem(z, 2)

        def rows(zz, yy, q):
            return pl.ds(pl.multiple_of((zz * 2 + yy) * CH + q * SR, 16), SR)

        def y_copy(i, q):
            return remote(rb.at[rows(dest[i], 1 - y, q), :], yb.at[i, q], ry_s.at[i, q], ry_r.at[i, q], across)

        def raw_copy(q):
            return remote(
                rb.at[rows(buddy, 1 - y, q), :], raw.at[q], rw_s.at[q], rw_r.at[q], on_line(buddy)
            )

        def piece(i):
            return pl.ds(pl.multiple_of(dest[i] * (2 * CH), 16), 2 * CH)
    else:
        def piece(i):
            return pl.ds(i * (3 * D // NZ), 3 * D // NZ)

    def finish(k):
        wait_factors(k, (2, 3))
        n3 = 3 * D // NZ // 3
        for i in range(NZ):
            if k == 0:
                r = piece(i)
                rb[r, :] = (pair_dot(0, 1, r, 0) + rb[r, :].astype(F32)).astype(BF)
            else:
                for h in range(3):
                    blk = (dest[i] if fused else i) * 3 + h
                    r = pl.ds(pl.multiple_of(blk * n3, 16), n3)
                    rb[r, :] = (pair_dot(1, 1, r, blk * n3 // D) + rb[r, :].astype(F32)).astype(BF)
            if fused and i < NZ - 1:
                def to_buddy():
                    for q in range(HALF):
                        raw_copy(q).start()

                def halves(i=i):
                    for q in range(HALF):
                        y_copy(i, q).start()

                when(dest[i] == buddy, to_buddy)
                when(dest[i] != buddy, halves)
                for q in range(HALF, SUB):
                    y_copy(i, q).start()

    def y_copy_x(u):
        return remote(ys.at[u], X.at[u], y_s.at[u], y_r.at[u], other)

    def fo_copy(u):
        return remote(ys.at[u], fob.at[u], fo_s.at[u], fo_r.at[u], other)

    def g_copy(u):
        return remote(gx.at[u], G.at[u], g_s.at[u], g_r.at[u], other)

    def ig_copy(u):
        return remote(gx.at[u], igb.at[u - 2], ig_s.at[u - 2], ig_r.at[u - 2], other)

    q_copy = remote(U["qkv"].at[3], U["qkv"].at[0], q_s, q_r, mate)

    def forward(u):
        S = {k: r.at[u] for k, r in U.items()}
        when(L == 1, lambda: y_copy_x(u).wait_recv())
        when((L == 0) & (u == 2), lambda: ex_copy(X.at[pl.ds(2, 2)]).wait_recv())
        opening = (L == 0) & (u == 0)
        lent = opening & (e == 1)

        def lend():
            mr_copy(0, 0, 0).wait_recv()
            U["qkv"][3] = dotf(mr[0, 0], wa[...]).astype(BF)
            q_copy.start()
            send_thirds(0)
        st = forward_stages(
            X.at[u], ys.at[u], wa, wf, (lga, lba), (lgf, lbf), mb.at[u], hm, S, gqT.at[pl.ds(0, D)], vec
        )
        for f in st:
            if f.__name__ == "project":
                when(e == 1, lambda: mr_copy(0, u, 0).start())
                when(lent, q_copy.wait_recv)
                when((L == 0) & (u == 1) & (e == 1), lambda: wait_all(1))
                when(jnp.logical_not(lent), f)
                when(opening & (e == 0), lend)
                continue
            if f.__name__ in ("mixed", "act", "branch"):
                c = ("mixed", "act", "branch").index(f.__name__)
                when(opening & (e == 0), lambda c=c: wait_third(1, c))
            f()
        when(L == 0, lambda: y_copy_x(u).start())

        def share():
            for c in range(3):
                mr_copy(1, u, c).start()

        when(e == 0, share)
        when((L == 0) & (u == 0) & (e == 0), q_copy.wait_send)
        when((L == 1) & (u < 2), lambda: fo_copy(u).start())

        def keep():
            fob[u - 2] = ys[u]

        when((L == 1) & (u >= 2), keep)

    def backward(u):
        S = {k: r.at[u] for k, r in U.items()}
        when((L == 0) & (u == 0), turn_weights)
        when((L == 1) & (u == 0), lambda: ex_copy(G.at[pl.ds(0, 2)]).wait_recv())
        when(L == 0, lambda: g_copy(u).wait_recv())
        last = (L == 0) & (u == 3)
        st = backward_stages(
            G.at[u], gx.at[u], waT, wfT, (lga, lba), (lgf, lbf), hm, S,
            {"a": wta.at[u], "f": wtf.at[u]},
            glp, gb, gctx, gctxT, gqT, gsT, vec,
        )
        for f in st:
            f()
            if f.__name__ == "g_context":
                when(e == 0, lambda: mw_copy(1, u).start())
            if f.__name__ == "g_merge":
                when(e == 1, lambda: mw_copy(0, u).start())
                when(last & (e == 1), lambda: finish(1))
        when(L == 1, lambda: g_copy(u).start())
        when((L == 0) & (u >= 2), lambda: ig_copy(u).start())

        def keep():
            igb[u] = gx[u]

        when((L == 0) & (u < 2), keep)
        when((L == 0) & (u == 2), lambda: per_core(first_pair))

    @pl.loop(0, 8)
    def _(i):
        odd = lax.rem(i, 2)
        is_f = jnp.where(L == 0, jnp.where(i < 4, 1, 0), 1 - odd)
        u = jnp.where(L == 0, lax.rem(i, 4), i // 2)
        when(is_f == 1, lambda: forward(u))
        when(is_f == 0, lambda: backward(u))

    when(L == 1, lambda: per_core(first_pair))
    gl_copy = remote(glp, glr, gl_s, gl_r, mate)
    gl_copy.start()
    when(e == 0, lambda: finish(0))
    when((e == 1) & (L == 1), lambda: finish(1))

    def bring0():
        for u in range(2):
            fo_copy(u).wait_recv()

    def bring1():
        for u in (2, 3):
            ig_copy(u).wait_recv()

    when(L == 0, bring0)
    when(L == 1, bring1)
    fo[...] = dotf(rinv[...], fob[...].reshape(R, D)).astype(BF)
    ig[...] = dotf(rinv[...], igb[...].reshape(R, D))
    emits = [pltpu.make_async_copy(fo, fo_hbm, o_s.at[0]), pltpu.make_async_copy(ig, ig_hbm, o_s.at[1])]
    for c in emits:
        c.start()
    gl_copy.wait()

    if fused:
        gl1 = glp[...] + glr[...]
        glr[...] = gl1
        gy_copy = remote(glr, gy, rg_s.at[0], rg_r.at[0], across)
        gy_copy.start()

        def own_y():
            for q in range(SUB):
                if q < HALF:
                    raw_copy(q).wait()
                    r = rows(z, 1 - y, q)
                    rb[r, :] = (rb[r, :].astype(F32) + raw[q].astype(F32)).astype(BF)
                y_copy(NZ - 1, q).start()

        def hop(i, q):
            zz = dest[i]
            nz = jnp.where(zz > z, z + 1, z - 1)
            slot = jnp.where((nz == zz) & (z > zz), NZ, zz)
            return remote(yb.at[i, q], inb.at[slot, q], rz_s.at[i, q], rz_r.at[slot, q], on_line(nz))

        def arrived(slot, q):
            remote(yb.at[0, q], inb.at[slot, q], rz_s.at[0, q], rz_r.at[slot, q], across).wait_recv()

        for i in range(NZ - 1):
            zz = dest[i]
            for q in range(SUB):
                mine = rb.at[rows(zz, y, q), :]

                def combine(i=i, q=q, mine=mine):
                    y_copy(i, q).wait_recv()
                    yb[i, q] = (mine[...].astype(F32) + yb[i, q].astype(F32)).astype(BF)

                def plain(i=i, q=q, mine=mine):
                    yb[i, q] = mine[...]

                def add_in(i=i, q=q, zz=zz):
                    arrived(zz, q)
                    yb[i, q] = (yb[i, q].astype(F32) + inb[zz, q].astype(F32)).astype(BF)

                if q < HALF:
                    when(zz != buddy, combine)
                    when(zz == buddy, plain)
                else:
                    combine()
                when(jnp.where(zz > z, z > 0, z < NZ - 1), add_in)
                hop(i, q).start()
            if i == NZ - 3:
                own_y()
        gy_copy.wait()
        gl2 = glr[...] + gy[...]
        gn[...] = gl2
        gz_copies = [
            remote(gn, gz.at[NZ - t - 1], rg_s.at[t], rg_r.at[NZ - t], on_line(lax.rem(z + t, NZ)))
            for t in range(1, NZ)
        ]
        for c in gz_copies:
            c.start()
        for q in range(SUB):
            acc[q] = rb[rows(z, y, q), :].astype(F32)

            def from_left(q=q):
                arrived(z, q)
                acc[q] += inb[z, q].astype(F32)

            def from_right(q=q):
                arrived(NZ, q)
                acc[q] += inb[NZ, q].astype(F32)

            when(z > 0, from_left)
            when(z < NZ - 1, from_right)
            y_copy(NZ - 1, q).wait_recv()
            acc[q] += yb[NZ - 1, q].astype(F32)
        out_w[...] = acc[...].reshape(CH, D)
        w_copy = pltpu.make_async_copy(out_w, w_hbm, o_s.at[2])
        w_copy.start()
        for i in range(NZ):
            for q in range(SUB):
                if q < HALF and i < NZ - 1:
                    when(dest[i] != buddy, lambda i=i, q=q: y_copy(i, q).wait_send())
                else:
                    y_copy(i, q).wait_send()
                if i < NZ - 1:
                    hop(i, q).wait_send()
        for t, c in zip(range(1, NZ), gz_copies):
            c.wait_send()
        for k in range(NZ - 1):
            remote(gn, gz.at[k], rg_s.at[0], rg_r.at[k + 1], across).wait_recv()
        gl3 = gl2 + gz[0] + gz[1] + gz[2]
        part = D // (2 * NZ)
        for k in range(2 * NZ):
            def own_part(k=k):
                for j in range(2):
                    v = gl3[:, k * part:(k + 1) * part]
                    norms[j][...] = jnp.where(e == 0, v[j:j + 1, :], v[2 + j:3 + j, :])

            when(d == k, own_part)
    else:
        norms[0][...] = glp[...] + glr[...]
        w_copy = pltpu.make_async_copy(rb, w_hbm, o_s.at[2])
        w_copy.start()
    for c in emits + [w_copy]:
        c.wait()

    def close_weights(k):
        for j in range(5):
            w_rem(k, j).wait_send()

    per_core(close_weights)
    def gave0():
        for u in range(4):
            mw_copy(1, u).wait_send()
            for c in range(3):
                mr_copy(1, u, c).wait_send()

    def gave1():
        for u in range(4):
            mw_copy(0, u).wait_send()
            mr_copy(0, u, 0).wait_send()

    when(e == 0, gave0)
    when(e == 1, gave1)
    ex_copy(X.at[pl.ds(2, 2)]).wait_send()

    def close0():
        for u in range(4):
            y_copy_x(u).wait_send()
        for u in (2, 3):
            ig_copy(u).wait_send()

    def close1():
        for u in range(4):
            g_copy(u).wait_send()
        for u in range(2):
            fo_copy(u).wait_send()

    when(L == 0, close0)
    when(L == 1, close1)


def relay(fused, tok, cot, w, gain, bias, mol, key):
    R, D = tok.shape
    V = pl.BlockSpec(memory_space=pltpu.VMEM)
    dma, vm = pltpu.SemaphoreType.DMA, pltpu.VMEM
    scratch = [vm((4,) + sh, dt) for sh, dt in unit_shapes(D)] + [
        vm((D, 3 * D), BF), vm((D, 3 * D), BF), vm((3 * D, D), BF), vm((3 * D, D), BF),
        vm((1, D), F32), vm((1, D), F32), vm((1, D), F32), vm((1, D), F32),
        vm((1, R), I32), vm((1, R), I32), vm((R, R), BF), vm((16, 256), BF), vm((4, T, T), F32),
        vm((4, T, D), BF), vm((4, T, D), BF), vm((2, T, D), BF), vm((4, T, D), BF), vm((4, T, D), BF),
        vm((2, T, D), BF), vm((2, T, D), BF),
        vm((4, 3 * D, T), BF), vm((4, 3 * D, T), BF), vm((4, 3 * D, T), BF), vm((4, 3, T, D), BF),
        vm((3 * D, D), BF), vm((8, D), F32), vm((8, D), F32),
        vm((T, D), F32), vm((T, D), BF), vm((T, D), BF), vm((D, T), BF),
        vm((3 * D, T), F32), vm((HEADS, T, T), BF),
        dma((3,)), dma((3,)), dma((3,)), dma((2,)), dma((2,)), dma((2,)), dma((2,)), dma, dma,
        dma((4,)), dma((4,)), dma((2,)), dma((2,)), dma((4,)), dma((4,)), dma((2,)), dma((2,)),
        dma((4,)), dma((4,)), dma((4, 3)), dma((4, 3)), dma, dma, dma, dma, vm((R, D), BF), vm((R, D), F32), dma((3,)),
    ]
    if fused:
        CH = 3 * D // (2 * NZ)
        SR = CH // SUB
        scratch += [
            vm((NZ, SUB, SR, D), BF), vm((NZ + 1, SUB, SR, D), BF), vm((HALF, SR, D), BF),
            vm((SUB, SR, D), F32), vm((8, D), F32), vm((NZ - 1, 8, D), F32), vm((8, D), F32), vm((CH, D), F32),
            dma((NZ, SUB)), dma((NZ, SUB)), dma((NZ - 1, SUB)), dma((NZ + 1, SUB)),
            dma((HALF,)), dma((HALF,)), dma((NZ,)), dma((NZ,)),
        ]
        outs = [jax.ShapeDtypeStruct((CH, D), F32)] + [jax.ShapeDtypeStruct((1, D // (2 * NZ)), F32)] * 2
    else:
        outs = [jax.ShapeDtypeStruct((3 * D, D), BF), jax.ShapeDtypeStruct((8, D), F32)]
    A = pl.BlockSpec(memory_space=pl.ANY)
    return pl.pallas_call(
        lambda *refs: relay_kernel(fused, *refs),
        out_shape=[jax.ShapeDtypeStruct((R, D), BF), jax.ShapeDtypeStruct((R, D), F32)] + outs,
        in_specs=[V, V, A, V, V, V, V],
        out_specs=[A, A, A] + [V] * (len(outs) - 1),
        scratch_shapes=scratch,
        compiler_params=pltpu.CompilerParams(
            collective_id=0, has_side_effects=True, vmem_limit_bytes=64 << 20
        ),
        name="relay",
    )(tok, cot, w, gain, bias, mol, key)


def emit_kernel(*refs):
    n = len(refs) // 3
    sems = refs[-1]
    ins = [pltpu.make_async_copy(refs[i], refs[2 * n + i], sems.at[0, i]) for i in range(n)]
    outs = [pltpu.make_async_copy(refs[2 * n + i], refs[n + i], sems.at[1, i]) for i in range(n)]
    for c in ins:
        c.start()
    for a, b in zip(ins, outs):
        a.wait()
        b.start()
    for c in outs:
        c.wait()


def emit(arrays):
    A = pl.BlockSpec(memory_space=pl.ANY)
    n = len(arrays)
    return pl.pallas_call(
        emit_kernel,
        out_shape=[jax.ShapeDtypeStruct(a.shape, a.dtype) for a in arrays],
        in_specs=[A] * n,
        out_specs=[A] * n,
        scratch_shapes=[pltpu.VMEM(a.shape, a.dtype) for a in arrays] + [pltpu.SemaphoreType.DMA((2, n))],
        name="emit",
    )(*arrays)


def shards(tokens, cotangent, section_weight, norm_gain, norm_bias, mol_ids, key_mask):
    fused = lax.axis_size("dp") == 2 * NZ
    got = relay(fused, tokens, cotangent, section_weight[0], norm_gain, norm_bias, mol_ids, key_mask)
    if fused:
        fo, ig, gw, gg, gb = emit(got)
        return fo, ig, gw.T[None], gg, gb
    fo, ig, gw, gn = got
    e = lax.rem(lax.axis_index("section"), 2)
    gn = lax.dynamic_slice_in_dim(gn, 2 * e, 2, 0)
    gw = lax.psum_scatter(gw, "dp", scatter_dimension=0, tiled=True)
    gn = lax.psum_scatter(gn, "dp", scatter_dimension=1, tiled=True)
    return fo, ig, gw.astype(F32).T[None], gn[0:1], gn[1:2]


def solution(mesh):
    return jax.shard_map(
        shards,
        mesh=mesh,
        in_specs=(
            P(("dp", "section"), None),
            P(("dp", "section"), None),
            P("section", None, None),
            P("section", None),
            P("section", None),
            P(("dp", "section"), None),
            P(("dp", "section"), None),
        ),
        out_specs=(
            P(("dp", "section"), None),
            P(("dp", "section"), None),
            P("section", None, "dp"),
            P("section", "dp"),
            P("section", "dp"),
        ),
        check_vma=False,
    )
```

```python
import jax
import jax.numpy as jnp
from jax import lax
from jax.experimental import pallas as pl
from jax.experimental.pallas import tpu as pltpu
from jax.sharding import PartitionSpec as P

HEADS = 32
HS = 24
EPS = 1e-5
NEG = -1e30
BF = jnp.bfloat16
F32 = jnp.float32
I32 = jnp.int32
MESH = pl.DeviceIdType.MESH
GELU_A = 0.7978845608028654
GELU_B = 0.044715
LOG2E = 1.4426950408889634
T = 128


def dotf(a, b):
    return jnp.dot(a, b, preferred_element_type=F32)


def dot_t(a, b):
    return lax.dot_general(a, b, (((1,), (1,)), ((), ())), preferred_element_type=F32)


def at(i, n):
    return pl.ds(pl.multiple_of(i * n, n), n)


HEAD_WIN = (0,) * 10 + (1,) * 6


def ln_rows(x, g, b):
    c = x - jnp.mean(x, axis=-1, keepdims=True)
    r = lax.rsqrt(jnp.mean(c * c, axis=-1, keepdims=True) + EPS)
    xh = c * r
    return xh, r, (xh * g + b).astype(BF)


def windows(ref, rows, base):
    return [ref[rows, base + 128 * w:base + 128 * w + 256] for w in (0, 1)]


def put_heads(ref, base, j, v):
    ref[base + 48 * j:base + 48 * j + 24, :] = v[0:24, 0:T]
    ref[base + 48 * j + 24:base + 48 * j + 48, :] = v[24:48, T:2 * T]


def two(ref, i, axis):
    return jnp.concatenate([ref[i], ref[i + 1]], axis=axis)


def forward_stages(x, y, wa, wf, lna, lnf, mb, hm, S, ctxT, vec):
    D = x.shape[1]

    def norm_a():
        S["xha"][...], S["ra"][...], S["an"][...] = ln_rows(x[...].astype(F32), lna[0][...], lna[1][...])

    def project():
        S["qkv"][...] = dotf(S["an"][...], wa[...]).astype(BF)

    def flip():
        S["qkvT"][...] = S["qkv"][...].T

    def scores():
        bias = mb[...]
        for g in range(2):
            base = g * 384
            qw = windows(S["qkv"], slice(None), base)
            kw = windows(S["qkv"], slice(None), D + base)
            for h in range(16):
                w = HEAD_WIN[h]
                s = dot_t(kw[w] * hm[h:h + 1, :], qw[w]) * (HS ** -0.5 * LOG2E) + bias
                ex = jnp.exp2(s - jnp.max(s, axis=0, keepdims=True))
                S["pT"][g * 16 + h] = (ex * (1.0 / jnp.sum(ex, axis=0, keepdims=True))).astype(BF)

    def mix_values():
        for g in range(2):
            base = g * 384
            for j in range(8):
                vt = S["qkvT"][2 * D + base + 48 * j:2 * D + base + 48 * j + 48, :]
                put_heads(ctxT, base, j, dotf(vt, two(S["pT"], g * 16 + 2 * j, 1)))

    def mixed():
        S["cfa"][0] = ctxT[...].astype(BF).T
        vec[...] = x[...].astype(F32) + dotf(S["cfa"][0], wf[:, 0:D])

    def norm_f():
        S["xhf"][...], S["rf"][...], S["cfa"][1] = ln_rows(vec[...], lnf[0][...], lnf[1][...])

    def act():
        u = dotf(S["cfa"][1], wf[:, D:2 * D])
        u2 = u * u
        t = jnp.tanh(GELU_A * (u + GELU_B * u * u2))
        S["cfa"][2] = (0.5 * u * (1.0 + t)).astype(BF)
        S["gp"][...] = 0.5 * (1.0 + t) + 0.5 * u * (1.0 - t * t) * (GELU_A + 3 * GELU_A * GELU_B * u2)

    def branch():
        br = dotf(S["cfa"][2], wf[:, 2 * D:3 * D]).astype(BF).astype(F32)
        y[...] = (vec[...].astype(BF).astype(F32) + br).astype(BF)

    return [norm_a, project, flip, scores, mix_values, mixed, norm_f, act, branch]


def backward_stages(G, gx, waT, wfT, lna, lnf, hm, S, W, glp, gb, gctx, gctxT, gqT, gsT, vec):
    D = G.shape[1]

    def ln_back(gref, xh, r, g, gi, resid, out):
        gn = gref[...]
        x = xh[...]
        gg = gn * g
        m1 = jnp.mean(gg, axis=-1, keepdims=True)
        m2 = jnp.mean(gg * x, axis=-1, keepdims=True)
        out[...] = (r[...] * (gg - m1 - x * m2) + resid[...].astype(F32)).astype(BF)
        glp[gi:gi + 1, :] += jnp.sum(gn * x, axis=0, keepdims=True)
        glp[gi + 1:gi + 2, :] += jnp.sum(gn, axis=0, keepdims=True)

    def g_act():
        W["f"][2 * D:3 * D, :] = G[...].T
        gb[...] = (dotf(G[...], wfT[2 * D:3 * D, :]) * S["gp"][...]).astype(BF)

    def g_norm():
        W["f"][D:2 * D, :] = gb[...].T
        vec[...] = dotf(gb[...], wfT[D:2 * D, :])

    def g_hidden():
        ln_back(vec, S["xhf"], S["rf"], lnf[0][...], 2, G, gb)

    def g_context():
        W["f"][0:D, :] = gb[...].T
        t = dotf(gb[...], wfT[0:D, :]).astype(BF)
        gctx[...] = t
        gctxT[...] = t.T

    def g_scores():
        for g in range(2):
            base = g * 384
            vw = windows(S["qkv"], slice(None), 2 * D + base)
            gw = windows(gctx, slice(None), base)
            for h in range(16):
                w = HEAD_WIN[h]
                gp = dot_t(vw[w] * hm[h:h + 1, :], gw[w])
                p = S["pT"][g * 16 + h].astype(F32)
                d = jnp.sum(p * gp, axis=0, keepdims=True)
                gsT[g * 16 + h] = (p * (gp - d)).astype(BF)

    def g_heads():
        for g in range(2):
            base = g * 384
            for j in range(8):
                i = g * 16 + 2 * j
                at48 = slice(base + 48 * j, base + 48 * j + 48)
                put_heads(gqT, 2 * D + base, j, dot_t(gctxT[at48, :], two(S["pT"], i, 0)))
                put_heads(gqT, D + base, j, dot_t(S["qkvT"][at48, :], two(gsT, i, 0)) * HS ** -0.5)
                k48 = slice(D + base + 48 * j, D + base + 48 * j + 48)
                put_heads(gqT, base, j, dotf(S["qkvT"][k48, :], two(gsT, i, 1)) * HS ** -0.5)

    def g_merge():
        t = gqT[...].astype(BF)
        W["a"][...] = t
        S["qkv"][...] = t.T

    def g_input():
        vec[...] = dotf(S["qkv"][...], waT[...])

    def g_x():
        ln_back(vec, S["xha"], S["ra"], lna[0][...], 0, gb, gx)

    return [g_act, g_norm, g_hidden, g_context, g_scores, g_heads, g_merge, g_input, g_x]


def remote(src, dst, ss, rs, dev):
    return pltpu.make_async_remote_copy(
        src_ref=src, dst_ref=dst, send_sem=ss, recv_sem=rs, device_id=dev, device_id_type=MESH
    )


def when(cond, fn):
    pl.when(cond)(fn)


NZ = 4
SUB = 2
HALF = 1
ORDER = ((3, 2, 1, 0), (3, 0, 2, 1), (0, 3, 1, 2), (0, 1, 2, 3))


def by_place(vals, z):
    r = vals[-1]
    for i in range(len(vals) - 2, -1, -1):
        r = jnp.where(z == i, vals[i], r)
    return r


def rotation(mol, R):
    c0 = jnp.sum((mol == 0).astype(I32), axis=1, keepdims=True)
    c1 = jnp.sum((mol == 1).astype(I32), axis=1, keepdims=True)
    start = jnp.where(c0 == T, 0, jnp.where(c1 == T, c0, c0 + c1))
    i0 = lax.broadcasted_iota(I32, (R, R), 0)
    i1 = lax.broadcasted_iota(I32, (R, R), 1)

    def onehot(a, b):
        t = a + start
        t = jnp.where(t >= R, t - R, t)
        return jnp.where(t == b, 1.0, 0.0).astype(BF)

    return onehot(i0, i1), onehot(i1, i0)


def pair_bias(mol, key, rot, out, base, R):
    mk = jnp.concatenate([mol, key, jnp.zeros((6, R), I32)], axis=0).astype(F32).astype(BF)
    row = dot_t(mk, rot)
    col = dot_t(rot, mk)
    k0 = lax.broadcasted_iota(I32, (T, T), 0)
    q0 = lax.broadcasted_iota(I32, (T, T), 1)
    for b in range(R // T):
        rs = slice(b * T, b * T + T)
        ok = (col[rs, 0:1] == row[0:1, rs]) & ((col[rs, 1:2] > 0.5) | (k0 == q0))
        out[base + b] = jnp.where(ok, 0.0, NEG)


UNIT = ("xha", "ra", "an", "qkv", "qkvT", "pT", "xhf", "rf", "cfa", "gp")


def unit_shapes(D):
    return (
        ((T, D), F32), ((T, 1), F32), ((T, D), BF), ((T, 3 * D), BF), ((3 * D, T), BF),
        ((HEADS, T, T), BF), ((T, D), F32), ((T, 1), F32), ((3, T, D), BF), ((T, D), F32),
    )


def relay_kernel(fused, tok, cot, w, gain, bias, mol, key, fo_hbm, ig_hbm, w_hbm, *scr):
    R, D = tok.shape
    norms, scr = (scr[:2], scr[2:]) if fused else (scr[:1], scr[1:])
    n = len(UNIT)
    U = {k: r for k, r in zip(UNIT, scr[:n])}
    (
        wa, wf, waT, wfT, lga, lba, lgf, lbf, molo, keyo, rinv, hm, mb, X, G, ex, ys, gx, fob, igb,
        wta, wtf, mw, mr, rb, glp, glr, vec, gb, gctx, gctxT, gqT, gsT,
        wl_s, w_s, w_r, l_s, l_r, m_s, m_r, ex_s, ex_r, y_s, y_r, fo_s, fo_r, g_s, g_r, ig_s, ig_r,
        mw_s, mw_r, mr_s, mr_r, x_s, x_r, q_s, q_r, gl_s, gl_r, fo, ig, o_s,
    ) = scr[n:n + 63]
    s = lax.axis_index("section")
    e = lax.rem(s, 2)
    L = s // 2
    mate = {"section": s + 1 - 2 * e}
    other = {"section": s + 2 - 4 * L}
    d = lax.axis_index("dp")
    z = d // 2
    y = d - 2 * z
    across = {"dp": d + 1 - 2 * y}

    def on_line(zz):
        return {"dp": zz * 2 + y}

    bar = pltpu.get_barrier_semaphore()
    peers = [mate, other]
    if fused:
        peers += [across] + [on_line(lax.rem(z + t, NZ)) for t in range(1, NZ)]
    for p in peers:
        pl.semaphore_signal(bar, inc=1, device_id=p, device_id_type=MESH)

    own = ((wa, lga, lba), (wf, lgf, lbf))

    def per_core(fn):
        when(e == 0, lambda: fn(0))
        when(e == 1, lambda: fn(1))

    def third(c):
        return (slice(None), pl.ds(c * D, D))

    def w_local(k, j):
        src = (w, gain, bias)[j]
        return pltpu.make_async_copy(src, own[k][j], wl_s.at[j])

    def w_rem(k, j):
        if j < 3:
            return remote(w.at[third(j)], own[k][0].at[third(j)], w_s.at[j], w_r.at[j], mate)
        src = (gain, bias)[j - 3]
        return remote(src, own[k][j - 2], l_s.at[j - 3], l_r.at[j - 3], mate)

    def start_local(k):
        for j in range(3):
            w_local(k, j).start()

    def wait_local(k):
        for j in range(3):
            w_local(k, j).wait()

    per_core(start_local)
    rot, inv = rotation(mol[...], R)
    rinv[...] = inv
    xu = dotf(rot, tok[...]).astype(BF).reshape(2, T, D)
    cu = dotf(rot, cot[...]).astype(BF).reshape(2, T, D)

    def stage0():
        ex[...] = cu
        X[0:2] = xu

    def stage1():
        ex[...] = xu
        G[2:4] = cu

    when(L == 0, stage0)
    when(L == 1, stage1)
    i0 = lax.broadcasted_iota(I32, (16, 256), 0)
    i1 = lax.broadcasted_iota(I32, (16, 256), 1)
    lo = HS * i0 - jnp.where(i0 < 10, 0, 128)
    hm[...] = jnp.where((i1 >= lo) & (i1 < lo + HS), 1.0, 0.0).astype(BF)
    glp[...] = jnp.zeros_like(glp)
    pair_bias(mol[...], key[...], rot, mb, 2 * L, R)

    def unit_forward(u):
        S = {k: r.at[u] for k, r in U.items()}
        return forward_stages(
            X.at[u], ys.at[u], wa, wf, (lga, lba), (lgf, lbf), mb.at[u], hm, S, gqT.at[pl.ds(0, D)], vec
        )

    first = {f.__name__: f for f in unit_forward(0)}

    def own_projection():
        wait_local(0)
        first["norm_a"]()
        first["project"]()

    when((L == 0) & (e == 0), own_projection)
    pl.semaphore_wait(bar, len(peers))

    x_copy = remote(X.at[0], U["an"].at[3], x_s, x_r, mate)
    q_copy = remote(U["qkv"].at[3], U["qkv"].at[0], q_s, q_r, mate)
    mol_copy = remote(mol, molo, m_s.at[0], m_r.at[0], other)
    key_copy = remote(key, keyo, m_s.at[1], m_r.at[1], other)

    def cot_copy(u):
        return remote(ex.at[u], G.at[u], ex_s.at[u], ex_r.at[u], other)

    def tok_copy(u):
        return remote(ex.at[u - 2], X.at[u], ex_s.at[u - 2], ex_r.at[u - 2], other)

    def send_rows(k):
        for j in (3, 4):
            w_rem(k, j).start()

    def send_thirds(k):
        for j in range(3):
            w_rem(k, j).start()

    def wait_rows(k):
        for j in (3, 4):
            w_rem(1 - k, j).wait_recv()

    def wait_third(k, c):
        w_rem(k, c).wait_recv()

    def wait_all(k):
        for c in range(3):
            wait_third(1 - k, c)

    when((L == 0) & (e == 1), x_copy.start)
    per_core(send_rows)
    when((L == 1) & (e == 0), lambda: send_thirds(0))
    when(e == 1, lambda: send_thirds(1))
    mol_copy.start()
    key_copy.start()

    def toks():
        tok_copy(2).start()
        tok_copy(3).start()

    when(L == 0, lambda: cot_copy(0).start())
    when(L == 1, toks)

    def turn_weights():
        @pl.loop(0, 3)
        def _(i):
            cs = at(i, D)
            waT[cs, :] = wa[:, cs].T
            wfT[cs, :] = wf[:, cs].T

    def other_bias():
        mol_copy.wait()
        key_copy.wait()
        rot_o, _ = rotation(molo[...], R)
        pair_bias(molo[...], keyo[...], rot_o, mb, 2 - 2 * L, R)

    def ready1():
        other_bias()
        per_core(wait_local)
        per_core(wait_rows)
        per_core(wait_all)
        turn_weights()

    when(L == 1, ready1)

    def mw_copy(k, u):
        return remote((wta, wtf)[k].at[u], mw.at[u], mw_s.at[u], mw_r.at[u], mate)

    def mr_copy(k, u, c):
        src = (U["an"].at[u], U["cfa"].at[u, c])[k]
        return remote(src, mr.at[u, c], mr_s.at[u, c], mr_r.at[u, c], mate)

    def mine(k, u, r, c):
        left = jnp.concatenate([(wta, wtf)[k][u, r, :], mw[u, r, :]], axis=1)
        right = jnp.concatenate([U["an"][u] if k == 0 else U["cfa"][u, c], mr[u, c]], axis=0)
        return left, right

    def pair_dot(k, p, r, c):
        a, b = mine(k, 2 * p, r, c), mine(k, 2 * p + 1, r, c)
        return dotf(jnp.concatenate([a[0], b[0]], axis=1), jnp.concatenate([a[1], b[1]], axis=0))

    def wait_factors(k, us):
        for u in us:
            mw_copy(k, u).wait_recv()
            for c in range(1 if k == 0 else 3):
                if k == 0 and u == 0:
                    when(L == 1, lambda: mr_copy(0, 0, 0).wait_recv())
                else:
                    mr_copy(1, u, c).wait_recv()

    def first_pair(k):
        wait_factors(k, (0, 1))
        for c in range(3):
            r = slice(c * D, c * D + D)
            rb[r, :] = pair_dot(k, 0, r, 0 if k == 0 else c).astype(BF)

    if fused:
        yb, inb, raw, acc, gy, gz, gn, out_w, ry_s, ry_r, rz_s, rz_r, rw_s, rw_r, rg_s, rg_r = scr[n + 63:]
        CH = 3 * D // (2 * NZ)
        SR = CH // SUB
        dest = [by_place([ORDER[k][i] for k in range(NZ)], z) for i in range(NZ)]
        buddy = z + 1 - 2 * lax.rem(z, 2)

        def rows(zz, yy, q):
            return pl.ds(pl.multiple_of((zz * 2 + yy) * CH + q * SR, 16), SR)

        def y_copy(i, q):
            return remote(rb.at[rows(dest[i], 1 - y, q), :], yb.at[i, q], ry_s.at[i, q], ry_r.at[i, q], across)

        def raw_copy(q):
            return remote(
                rb.at[rows(buddy, 1 - y, q), :], raw.at[q], rw_s.at[q], rw_r.at[q], on_line(buddy)
            )

        def piece(i):
            return pl.ds(pl.multiple_of(dest[i] * (2 * CH), 16), 2 * CH)
    else:
        def piece(i):
            return pl.ds(i * (3 * D // NZ), 3 * D // NZ)

    def finish(k, i):
        n3 = 3 * D // NZ // 3
        if i == 0:
            wait_factors(k, (2, 3))
        if k == 0:
            r = piece(i)
            rb[r, :] = (pair_dot(0, 1, r, 0) + rb[r, :].astype(F32)).astype(BF)
        else:
            for h in range(3):
                blk = (dest[i] if fused else i) * 3 + h
                r = pl.ds(pl.multiple_of(blk * n3, 16), n3)
                rb[r, :] = (pair_dot(1, 1, r, blk * n3 // D) + rb[r, :].astype(F32)).astype(BF)
        if fused and i < NZ - 1:
            def to_buddy():
                for q in range(HALF):
                    raw_copy(q).start()

            def halves():
                for q in range(HALF):
                    y_copy(i, q).start()

            when(dest[i] == buddy, to_buddy)
            when(dest[i] != buddy, halves)
            for q in range(HALF, SUB):
                y_copy(i, q).start()

    def finish_rest(k):
        for i in range(1, NZ):
            finish(k, i)

    def y_copy_x(u):
        return remote(ys.at[u], X.at[u], y_s.at[u], y_r.at[u], other)

    def fo_copy(u):
        return remote(ys.at[u], fob.at[u], fo_s.at[u], fo_r.at[u], other)

    def g_copy(u):
        return remote(gx.at[u], G.at[u], g_s.at[u], g_r.at[u], other)

    def ig_copy(u):
        return remote(gx.at[u], igb.at[u - 2], ig_s.at[u - 2], ig_r.at[u - 2], other)

    def share(u):
        def factors0():
            for c in range(3):
                mr_copy(1, u, c).start()

        when(e == 0, factors0)
        when((e == 1) & ((L == 1) | (u > 0)), lambda: mr_copy(0, u, 0).start())

    def lend():
        x_copy.wait_recv()
        mr[0, 0] = ln_rows(U["an"][3].astype(F32), lga[...], lba[...])[2]
        U["qkv"][3] = dotf(mr[0, 0], wa[...]).astype(BF)
        q_copy.start()
        send_thirds(0)

    def borrow():
        wait_local(1)
        first["norm_a"]()
        q_copy.wait_recv()

    def opening():
        when(e == 0, lend)
        per_core(wait_rows)
        when(e == 1, borrow)
        for name in ("flip", "scores", "mix_values"):
            first[name]()
        for c, name in enumerate(("mixed", "act", "branch")):
            when(e == 0, lambda c=c: wait_third(1, c))
            first[name]()
            if name == "mixed":
                first["norm_f"]()
        y_copy_x(0).start()
        share(0)
        other_bias()
        when(e == 0, q_copy.wait_send)
        when(e == 1, x_copy.wait_send)
        when(e == 1, lambda: wait_all(1))

    def forward(u):
        when(L == 1, lambda: y_copy_x(u).wait_recv())
        when((L == 0) & (u >= 2), lambda: tok_copy(u).wait_recv())
        for f in unit_forward(u):
            f()
        when(L == 0, lambda: y_copy_x(u).start())
        when((L == 0) & (u == 1), lambda: cot_copy(u).start())
        share(u)

        def keep():
            fob[u - 2] = ys[u]

        when((L == 1) & (u >= 2), keep)

    def unit_backward(u):
        S = {k: r.at[u] for k, r in U.items()}
        return backward_stages(
            G.at[u], gx.at[u], waT, wfT, (lga, lba), (lgf, lbf), hm, S,
            {"a": wta.at[u], "f": wtf.at[u]},
            glp, gb, gctx, gctxT, gqT, gsT, vec,
        )

    def backward(u):
        when((L == 0) & (u == 0), turn_weights)
        when((L == 1) & (u < 2), lambda: cot_copy(u).wait_recv())
        when(L == 0, lambda: g_copy(u).wait_recv())
        for f in unit_backward(u):
            f()
        when(L == 1, lambda: g_copy(u).start())
        per_core(lambda k: mw_copy(1 - k, u).start())
        when((L == 0) & (u == 2), lambda: ig_copy(u).start())

        def keep():
            igb[u] = gx[u]

        when((L == 0) & (u < 2), keep)
        when((L == 0) & (u == 2), lambda: per_core(first_pair))

    gl_copy = remote(glp, glr, gl_s, gl_r, mate)

    def closing():
        g_copy(3).wait_recv()
        for f in unit_backward(3):
            f()
            if f.__name__ == "g_context":
                when(e == 0, lambda: mw_copy(1, 3).start())
            if f.__name__ == "g_merge":
                when(e == 1, lambda: mw_copy(0, 3).start())
                when(e == 1, lambda: finish(1, 0))
        ig_copy(3).start()

    when(L == 0, opening)

    @pl.loop(0, 8)
    def _(i):
        odd = lax.rem(i, 2)
        is_f = jnp.where(L == 0, jnp.where((i >= 1) & (i <= 3), 1, 0), 1 - odd)
        is_b = jnp.where(L == 0, jnp.where((i >= 4) & (i <= 6), 1, 0), odd)
        u = jnp.where(L == 0, lax.rem(i, 4), i // 2)
        when(is_f == 1, lambda: forward(u))
        when(is_b == 1, lambda: backward(u))

    when(L == 0, closing)
    gl_copy.start()
    when(L == 1, lambda: per_core(first_pair))
    when(e == 0, lambda: finish(0, 0))
    when((e == 1) & (L == 1), lambda: finish(1, 0))
    gl_copy.wait()
    glr[...] = glp[...] + glr[...]
    if fused:
        gy_copy = remote(glr, gy, rg_s.at[0], rg_r.at[0], across)
        gy_copy.start()
    per_core(finish_rest)

    def send_fo():
        for u in range(2):
            fo_copy(u).start()

    when(L == 1, send_fo)
    emits = []

    def bring():
        def bring0():
            for u in range(2):
                fo_copy(u).wait_recv()

        def bring1():
            for u in (2, 3):
                ig_copy(u).wait_recv()

        when(L == 0, bring0)
        when(L == 1, bring1)
        fo[...] = dotf(rinv[...], fob[...].reshape(R, D)).astype(BF)
        ig[...] = dotf(rinv[...], igb[...].reshape(R, D))
        emits.extend([pltpu.make_async_copy(fo, fo_hbm, o_s.at[0]), pltpu.make_async_copy(ig, ig_hbm, o_s.at[1])])
        for c in emits:
            c.start()

    if fused:
        def own_y():
            for q in range(SUB):
                if q < HALF:
                    raw_copy(q).wait()
                    r = rows(z, 1 - y, q)
                    rb[r, :] = (rb[r, :].astype(F32) + raw[q].astype(F32)).astype(BF)
                y_copy(NZ - 1, q).start()

        def hop(i, q):
            zz = dest[i]
            nz = jnp.where(zz > z, z + 1, z - 1)
            slot = jnp.where((nz == zz) & (z > zz), NZ, zz)
            return remote(yb.at[i, q], inb.at[slot, q], rz_s.at[i, q], rz_r.at[slot, q], on_line(nz))

        def arrived(slot, q):
            remote(yb.at[0, q], inb.at[slot, q], rz_s.at[0, q], rz_r.at[slot, q], across).wait_recv()

        for i in range(NZ - 1):
            zz = dest[i]
            for q in range(SUB):
                mine = rb.at[rows(zz, y, q), :]

                def combine(i=i, q=q, mine=mine):
                    y_copy(i, q).wait_recv()
                    yb[i, q] = (mine[...].astype(F32) + yb[i, q].astype(F32)).astype(BF)

                def plain(i=i, q=q, mine=mine):
                    yb[i, q] = mine[...]

                def add_in(i=i, q=q, zz=zz):
                    arrived(zz, q)
                    yb[i, q] = (yb[i, q].astype(F32) + inb[zz, q].astype(F32)).astype(BF)

                if q < HALF:
                    when(zz != buddy, combine)
                    when(zz == buddy, plain)
                else:
                    combine()
                when(jnp.where(zz > z, z > 0, z < NZ - 1), add_in)
                hop(i, q).start()
            if i == 0:
                gy_copy.wait()
                gl2 = glr[...] + gy[...]
                gn[...] = gl2
                gz_copies = [
                    remote(gn, gz.at[NZ - t - 1], rg_s.at[t], rg_r.at[NZ - t], on_line(lax.rem(z + t, NZ)))
                    for t in range(1, NZ)
                ]
                for c in gz_copies:
                    c.start()
            if i == NZ - 3:
                own_y()
        bring()
        for q in range(SUB):
            acc[q] = rb[rows(z, y, q), :].astype(F32)

            def from_left(q=q):
                arrived(z, q)
                acc[q] += inb[z, q].astype(F32)

            def from_right(q=q):
                arrived(NZ, q)
                acc[q] += inb[NZ, q].astype(F32)

            when(z > 0, from_left)
            when(z < NZ - 1, from_right)
            y_copy(NZ - 1, q).wait_recv()
            acc[q] += yb[NZ - 1, q].astype(F32)
        out_w[...] = acc[...].reshape(CH, D)
        w_copy = pltpu.make_async_copy(out_w, w_hbm, o_s.at[2])
        w_copy.start()
        for i in range(NZ):
            for q in range(SUB):
                if q < HALF and i < NZ - 1:
                    when(dest[i] != buddy, lambda i=i, q=q: y_copy(i, q).wait_send())
                else:
                    y_copy(i, q).wait_send()
                if i < NZ - 1:
                    hop(i, q).wait_send()
        for t, c in zip(range(1, NZ), gz_copies):
            c.wait_send()
        for k in range(NZ - 1):
            remote(gn, gz.at[k], rg_s.at[0], rg_r.at[k + 1], across).wait_recv()
        gl3 = gl2 + gz[0] + gz[1] + gz[2]
        part = D // (2 * NZ)
        for k in range(2 * NZ):
            def own_part(k=k):
                for j in range(2):
                    v = gl3[:, k * part:(k + 1) * part]
                    norms[j][...] = jnp.where(e == 0, v[j:j + 1, :], v[2 + j:3 + j, :])

            when(d == k, own_part)
    else:
        bring()
        norms[0][...] = glr[...]
        w_copy = pltpu.make_async_copy(rb, w_hbm, o_s.at[2])
        w_copy.start()
    for c in emits + [w_copy]:
        c.wait()

    def close_weights(k):
        for j in range(5):
            w_rem(k, j).wait_send()

    per_core(close_weights)
    def gave0():
        for u in range(4):
            mw_copy(1, u).wait_send()
            for c in range(3):
                mr_copy(1, u, c).wait_send()

    def gave1():
        for u in range(4):
            mw_copy(0, u).wait_send()
            if u == 0:
                when(L == 1, lambda: mr_copy(0, 0, 0).wait_send())
            else:
                mr_copy(0, u, 0).wait_send()

    when(e == 0, gave0)
    when(e == 1, gave1)
    for u in range(2):
        cot_copy(u).wait_send()

    def close0():
        for u in range(4):
            y_copy_x(u).wait_send()
        for u in (2, 3):
            ig_copy(u).wait_send()

    def close1():
        for u in range(4):
            g_copy(u).wait_send()
        for u in range(2):
            fo_copy(u).wait_send()

    when(L == 0, close0)
    when(L == 1, close1)


def relay(fused, tok, cot, w, gain, bias, mol, key):
    R, D = tok.shape
    V = pl.BlockSpec(memory_space=pltpu.VMEM)
    dma, vm = pltpu.SemaphoreType.DMA, pltpu.VMEM
    scratch = [vm((4,) + sh, dt) for sh, dt in unit_shapes(D)] + [
        vm((D, 3 * D), BF), vm((D, 3 * D), BF), vm((3 * D, D), BF), vm((3 * D, D), BF),
        vm((1, D), F32), vm((1, D), F32), vm((1, D), F32), vm((1, D), F32),
        vm((1, R), I32), vm((1, R), I32), vm((R, R), BF), vm((16, 256), BF), vm((4, T, T), F32),
        vm((4, T, D), BF), vm((4, T, D), BF), vm((2, T, D), BF), vm((4, T, D), BF), vm((4, T, D), BF),
        vm((2, T, D), BF), vm((2, T, D), BF),
        vm((4, 3 * D, T), BF), vm((4, 3 * D, T), BF), vm((4, 3 * D, T), BF), vm((4, 3, T, D), BF),
        vm((3 * D, D), BF), vm((8, D), F32), vm((8, D), F32),
        vm((T, D), F32), vm((T, D), BF), vm((T, D), BF), vm((D, T), BF),
        vm((3 * D, T), F32), vm((HEADS, T, T), BF),
        dma((3,)), dma((3,)), dma((3,)), dma((2,)), dma((2,)), dma((2,)), dma((2,)), dma((2,)), dma((2,)),
        dma((4,)), dma((4,)), dma((2,)), dma((2,)), dma((4,)), dma((4,)), dma((2,)), dma((2,)),
        dma((4,)), dma((4,)), dma((4, 3)), dma((4, 3)), dma, dma, dma, dma, dma, dma, vm((R, D), BF), vm((R, D), F32), dma((3,)),
    ]
    if fused:
        CH = 3 * D // (2 * NZ)
        SR = CH // SUB
        scratch += [
            vm((NZ, SUB, SR, D), BF), vm((NZ + 1, SUB, SR, D), BF), vm((HALF, SR, D), BF),
            vm((SUB, SR, D), F32), vm((8, D), F32), vm((NZ - 1, 8, D), F32), vm((8, D), F32), vm((CH, D), F32),
            dma((NZ, SUB)), dma((NZ, SUB)), dma((NZ - 1, SUB)), dma((NZ + 1, SUB)),
            dma((HALF,)), dma((HALF,)), dma((NZ,)), dma((NZ,)),
        ]
        outs = [jax.ShapeDtypeStruct((CH, D), F32)] + [jax.ShapeDtypeStruct((1, D // (2 * NZ)), F32)] * 2
    else:
        outs = [jax.ShapeDtypeStruct((3 * D, D), BF), jax.ShapeDtypeStruct((8, D), F32)]
    A = pl.BlockSpec(memory_space=pl.ANY)
    return pl.pallas_call(
        lambda *refs: relay_kernel(fused, *refs),
        out_shape=[jax.ShapeDtypeStruct((R, D), BF), jax.ShapeDtypeStruct((R, D), F32)] + outs,
        in_specs=[V, V, A, V, V, V, V],
        out_specs=[A, A, A] + [V] * (len(outs) - 1),
        scratch_shapes=scratch,
        compiler_params=pltpu.CompilerParams(
            collective_id=0, has_side_effects=True, vmem_limit_bytes=64 << 20
        ),
        name="relay",
    )(tok, cot, w, gain, bias, mol, key)


def emit_kernel(*refs):
    n = len(refs) // 3
    sems = refs[-1]
    ins = [pltpu.make_async_copy(refs[i], refs[2 * n + i], sems.at[0, i]) for i in range(n)]
    outs = [pltpu.make_async_copy(refs[2 * n + i], refs[n + i], sems.at[1, i]) for i in range(n)]
    for c in ins:
        c.start()
    for a, b in zip(ins, outs):
        a.wait()
        b.start()
    for c in outs:
        c.wait()


def emit(arrays):
    A = pl.BlockSpec(memory_space=pl.ANY)
    n = len(arrays)
    return pl.pallas_call(
        emit_kernel,
        out_shape=[jax.ShapeDtypeStruct(a.shape, a.dtype) for a in arrays],
        in_specs=[A] * n,
        out_specs=[A] * n,
        scratch_shapes=[pltpu.VMEM(a.shape, a.dtype) for a in arrays] + [pltpu.SemaphoreType.DMA((2, n))],
        name="emit",
    )(*arrays)


def shards(tokens, cotangent, section_weight, norm_gain, norm_bias, mol_ids, key_mask):
    fused = lax.axis_size("dp") == 2 * NZ
    got = relay(fused, tokens, cotangent, section_weight[0], norm_gain, norm_bias, mol_ids, key_mask)
    if fused:
        fo, ig, gw, gg, gb = emit(got)
        return fo, ig, gw.T[None], gg, gb
    fo, ig, gw, gn = got
    e = lax.rem(lax.axis_index("section"), 2)
    gn = lax.dynamic_slice_in_dim(gn, 2 * e, 2, 0)
    gw = lax.psum_scatter(gw, "dp", scatter_dimension=0, tiled=True)
    gn = lax.psum_scatter(gn, "dp", scatter_dimension=1, tiled=True)
    return fo, ig, gw.astype(F32).T[None], gn[0:1], gn[1:2]


def solution(mesh):
    return jax.shard_map(
        shards,
        mesh=mesh,
        in_specs=(
            P(("dp", "section"), None),
            P(("dp", "section"), None),
            P("section", None, None),
            P("section", None),
            P("section", None),
            P(("dp", "section"), None),
            P(("dp", "section"), None),
        ),
        out_specs=(
            P(("dp", "section"), None),
            P(("dp", "section"), None),
            P("section", None, "dp"),
            P("section", "dp"),
            P("section", "dp"),
        ),
        check_vma=False,
    )
```

```python
import jax
import jax.numpy as jnp
from jax import lax
from jax.experimental import pallas as pl
from jax.experimental.pallas import tpu as pltpu
from jax.sharding import PartitionSpec as P

HEADS = 32
HS = 24
EPS = 1e-5
NEG = -1e30
BF = jnp.bfloat16
F32 = jnp.float32
I32 = jnp.int32
MESH = pl.DeviceIdType.MESH
GELU_A = 0.7978845608028654
GELU_B = 0.044715
LOG2E = 1.4426950408889634
T = 128


def dotf(a, b):
    return jnp.dot(a, b, preferred_element_type=F32)


def dot_t(a, b):
    return lax.dot_general(a, b, (((1,), (1,)), ((), ())), preferred_element_type=F32)


def at(i, n):
    return pl.ds(pl.multiple_of(i * n, n), n)


HEAD_WIN = (0,) * 10 + (1,) * 6


def ln_rows(x, g, b):
    c = x - jnp.mean(x, axis=-1, keepdims=True)
    r = lax.rsqrt(jnp.mean(c * c, axis=-1, keepdims=True) + EPS)
    xh = c * r
    return xh, r, (xh * g + b).astype(BF)


def windows(ref, rows, base):
    return [ref[rows, base + 128 * w:base + 128 * w + 256] for w in (0, 1)]


def put_heads(ref, base, j, v):
    ref[base + 48 * j:base + 48 * j + 24, :] = v[0:24, 0:T]
    ref[base + 48 * j + 24:base + 48 * j + 48, :] = v[24:48, T:2 * T]


def two(ref, i, axis):
    return jnp.concatenate([ref[i], ref[i + 1]], axis=axis)


def forward_stages(x, y, wa, wf, lna, lnf, mb, hm, S, ctxT, vec):
    D = x.shape[1]

    def norm_a():
        S["xha"][...], S["ra"][...], S["an"][...] = ln_rows(x[...].astype(F32), lna[0][...], lna[1][...])

    def project():
        S["qkv"][...] = dotf(S["an"][...], wa[...]).astype(BF)

    def flip():
        S["qkvT"][...] = S["qkv"][...].T

    def scores():
        bias = mb[...]
        for g in range(2):
            base = g * 384
            qw = windows(S["qkv"], slice(None), base)
            kw = windows(S["qkv"], slice(None), D + base)
            for h in range(16):
                w = HEAD_WIN[h]
                s = dot_t(kw[w] * hm[h:h + 1, :], qw[w]) * (HS ** -0.5 * LOG2E) + bias
                ex = jnp.exp2(s - jnp.max(s, axis=0, keepdims=True))
                S["pT"][g * 16 + h] = (ex * (1.0 / jnp.sum(ex, axis=0, keepdims=True))).astype(BF)

    def mix_values():
        for g in range(2):
            base = g * 384
            for j in range(8):
                vt = S["qkvT"][2 * D + base + 48 * j:2 * D + base + 48 * j + 48, :]
                put_heads(ctxT, base, j, dotf(vt, two(S["pT"], g * 16 + 2 * j, 1)))

    def mixed():
        S["cfa"][0] = ctxT[...].astype(BF).T
        vec[...] = x[...].astype(F32) + dotf(S["cfa"][0], wf[:, 0:D])

    def norm_f():
        S["xhf"][...], S["rf"][...], S["cfa"][1] = ln_rows(vec[...], lnf[0][...], lnf[1][...])

    def act():
        u = dotf(S["cfa"][1], wf[:, D:2 * D])
        u2 = u * u
        t = jnp.tanh(GELU_A * (u + GELU_B * u * u2))
        S["cfa"][2] = (0.5 * u * (1.0 + t)).astype(BF)
        S["gp"][...] = 0.5 * (1.0 + t) + 0.5 * u * (1.0 - t * t) * (GELU_A + 3 * GELU_A * GELU_B * u2)

    def branch():
        br = dotf(S["cfa"][2], wf[:, 2 * D:3 * D]).astype(BF).astype(F32)
        y[...] = (vec[...].astype(BF).astype(F32) + br).astype(BF)

    return [norm_a, project, flip, scores, mix_values, mixed, norm_f, act, branch]


def backward_stages(G, gx, waT, wfT, lna, lnf, hm, S, W, glp, gb, gctx, gctxT, gqT, gsT, vec):
    D = G.shape[1]

    def ln_back(gref, xh, r, g, gi, resid, out):
        gn = gref[...]
        x = xh[...]
        gg = gn * g
        m1 = jnp.mean(gg, axis=-1, keepdims=True)
        m2 = jnp.mean(gg * x, axis=-1, keepdims=True)
        out[...] = (r[...] * (gg - m1 - x * m2) + resid[...].astype(F32)).astype(BF)
        glp[gi:gi + 1, :] += jnp.sum(gn * x, axis=0, keepdims=True)
        glp[gi + 1:gi + 2, :] += jnp.sum(gn, axis=0, keepdims=True)

    def g_act():
        W["f"][2 * D:3 * D, :] = G[...].T
        gb[...] = (dotf(G[...], wfT[2 * D:3 * D, :]) * S["gp"][...]).astype(BF)

    def g_norm():
        W["f"][D:2 * D, :] = gb[...].T
        vec[...] = dotf(gb[...], wfT[D:2 * D, :])

    def g_hidden():
        ln_back(vec, S["xhf"], S["rf"], lnf[0][...], 2, G, gb)

    def g_context():
        W["f"][0:D, :] = gb[...].T
        t = dotf(gb[...], wfT[0:D, :]).astype(BF)
        gctx[...] = t
        gctxT[...] = t.T

    def g_scores():
        for g in range(2):
            base = g * 384
            vw = windows(S["qkv"], slice(None), 2 * D + base)
            gw = windows(gctx, slice(None), base)
            for h in range(16):
                w = HEAD_WIN[h]
                gp = dot_t(vw[w] * hm[h:h + 1, :], gw[w])
                p = S["pT"][g * 16 + h].astype(F32)
                d = jnp.sum(p * gp, axis=0, keepdims=True)
                gsT[g * 16 + h] = (p * (gp - d)).astype(BF)

    def g_heads():
        for g in range(2):
            base = g * 384
            for j in range(8):
                i = g * 16 + 2 * j
                at48 = slice(base + 48 * j, base + 48 * j + 48)
                put_heads(gqT, 2 * D + base, j, dot_t(gctxT[at48, :], two(S["pT"], i, 0)))
                put_heads(gqT, D + base, j, dot_t(S["qkvT"][at48, :], two(gsT, i, 0)) * HS ** -0.5)
                k48 = slice(D + base + 48 * j, D + base + 48 * j + 48)
                put_heads(gqT, base, j, dotf(S["qkvT"][k48, :], two(gsT, i, 1)) * HS ** -0.5)

    def g_merge():
        t = gqT[...].astype(BF)
        W["a"][...] = t
        S["qkv"][...] = t.T

    def g_input():
        vec[...] = dotf(S["qkv"][...], waT[...])

    def g_x():
        ln_back(vec, S["xha"], S["ra"], lna[0][...], 0, gb, gx)

    return [g_act, g_norm, g_hidden, g_context, g_scores, g_heads, g_merge, g_input, g_x]


def remote(src, dst, ss, rs, dev):
    return pltpu.make_async_remote_copy(
        src_ref=src, dst_ref=dst, send_sem=ss, recv_sem=rs, device_id=dev, device_id_type=MESH
    )


def when(cond, fn):
    pl.when(cond)(fn)


NZ = 4
SUB = 3
HALF = 1
ORDER = ((3, 2, 1, 0), (3, 0, 2, 1), (0, 3, 1, 2), (0, 1, 2, 3))


def by_place(vals, z):
    r = vals[-1]
    for i in range(len(vals) - 2, -1, -1):
        r = jnp.where(z == i, vals[i], r)
    return r


def rotation(mol, R):
    c0 = jnp.sum((mol == 0).astype(I32), axis=1, keepdims=True)
    c1 = jnp.sum((mol == 1).astype(I32), axis=1, keepdims=True)
    start = jnp.where(c0 == T, 0, jnp.where(c1 == T, c0, c0 + c1))
    i0 = lax.broadcasted_iota(I32, (R, R), 0)
    i1 = lax.broadcasted_iota(I32, (R, R), 1)

    def onehot(a, b):
        t = a + start
        t = jnp.where(t >= R, t - R, t)
        return jnp.where(t == b, 1.0, 0.0).astype(BF)

    return onehot(i0, i1), onehot(i1, i0)


def pair_bias(mol, key, rot, out, mine, R):
    mk = jnp.concatenate([mol, key, jnp.zeros((6, R), I32)], axis=0).astype(F32).astype(BF)
    row = dot_t(mk, rot)
    col = dot_t(rot, mk)
    k0 = lax.broadcasted_iota(I32, (T, T), 0)
    q0 = lax.broadcasted_iota(I32, (T, T), 1)
    for b in range(R // T):
        rs = slice(b * T, b * T + T)
        ok = (col[rs, 0:1] == row[0:1, rs]) & ((col[rs, 1:2] > 0.5) | (k0 == q0))
        out[jnp.where(mine == 0, 3 * b, 1 + b)] = jnp.where(ok, 0.0, NEG)


UNIT = ("xha", "ra", "an", "qkv", "qkvT", "pT", "xhf", "rf", "cfa", "gp")


def unit_shapes(D):
    return (
        ((T, D), F32), ((T, 1), F32), ((T, D), BF), ((T, 3 * D), BF), ((3 * D, T), BF),
        ((HEADS, T, T), BF), ((T, D), F32), ((T, 1), F32), ((3, T, D), BF), ((T, D), F32),
    )


def relay_kernel(fused, tok, cot, w, gain, bias, mol, key, fo_hbm, ig_hbm, w_hbm, *scr):
    R, D = tok.shape
    norms, scr = (scr[:2], scr[2:]) if fused else (scr[:1], scr[1:])
    n = len(UNIT)
    U = {k: r for k, r in zip(UNIT, scr[:n])}
    (
        wa, wf, waT, wfT, lga, lba, lgf, lbf, molo, keyo, rinv, hm, mb, X, G, ex, ys, gx, fob, igb,
        wta, wtf, mw, mr, rb, glp, glr, ctxT, vec, gb, gctx, gctxT, gqT, gsT,
        wl_s, w_s, w_r, l_s, l_r, m_s, m_r, ex_s, ex_r, y_s, y_r, fo_s, fo_r, g_s, g_r, ig_s, ig_r,
        mw_s, mw_r, mr_s, mr_r, x_s, x_r, q_s, q_r, gl_s, gl_r, fo, ig, o_s,
    ) = scr[n:n + 64]
    s = lax.axis_index("section")
    e = lax.rem(s, 2)
    L = s // 2
    mate = {"section": s + 1 - 2 * e}
    other = {"section": s + 2 - 4 * L}
    d = lax.axis_index("dp")
    z = d // 2
    y = d - 2 * z
    across = {"dp": d + 1 - 2 * y}

    def on_line(zz):
        return {"dp": zz * 2 + y}

    bar = pltpu.get_barrier_semaphore()
    peers = [mate, other]
    if fused:
        peers += [across] + [on_line(lax.rem(z + t, NZ)) for t in range(1, NZ)]
    for p in peers:
        pl.semaphore_signal(bar, inc=1, device_id=p, device_id_type=MESH)

    own = ((wa, lga, lba), (wf, lgf, lbf))

    def per_core(fn):
        when(e == 0, lambda: fn(0))
        when(e == 1, lambda: fn(1))

    def third(c):
        return (slice(None), pl.ds(c * D, D))

    def w_local(k, j):
        src = (w, gain, bias)[j]
        return pltpu.make_async_copy(src, own[k][j], wl_s.at[j])

    def w_rem(k, j):
        if j < 3:
            return remote(w.at[third(j)], own[k][0].at[third(j)], w_s.at[j], w_r.at[j], mate)
        src = (gain, bias)[j - 3]
        return remote(src, own[k][j - 2], l_s.at[j - 3], l_r.at[j - 3], mate)

    def start_local(k):
        for j in range(3):
            w_local(k, j).start()

    def wait_local(k):
        for j in range(3):
            w_local(k, j).wait()

    per_core(start_local)
    rot, inv = rotation(mol[...], R)
    rinv[...] = inv
    xu = dotf(rot, tok[...]).astype(BF).reshape(2, T, D)

    def rows0():
        X[0] = xu[0]
        X[3] = xu[1]

    def rows1():
        ex[...] = xu

    when(L == 0, rows0)
    when(L == 1, rows1)

    def unit_forward(u, heads=None, rows=None):
        S = {k: r.at[u] for k, r in U.items()}
        return forward_stages(
            X.at[u], ys.at[u], wa, wf, (lga, lba), (lgf, lbf), mb.at[u], hm, S,
            gqT.at[pl.ds(0, D)] if heads is None else heads, vec if rows is None else rows,
        )

    first = {f.__name__: f for f in unit_forward(0)}

    def own_projection():
        first["norm_a"]()
        first["project"]()

    pl.semaphore_wait(bar, len(peers))

    x_copy = remote(X.at[0], U["an"].at[3], x_s, x_r, mate)
    q_copy = remote(U["qkv"].at[3], U["qkv"].at[0], q_s, q_r, mate)
    mol_copy = remote(mol, molo, m_s.at[0], m_r.at[0], other)
    key_copy = remote(key, keyo, m_s.at[1], m_r.at[1], other)

    def cot_copy(u):
        return remote(ex.at[u // 3], G.at[u], ex_s.at[u // 3], ex_r.at[u // 3], other)

    def tok_copy(u):
        return remote(ex.at[u - 1], X.at[u], ex_s.at[u - 1], ex_r.at[u - 1], other)

    def send_rows(k):
        for j in (3, 4):
            w_rem(k, j).start()

    def send_thirds(k):
        for j in range(3):
            w_rem(k, j).start()

    def wait_rows(k):
        for j in (3, 4):
            w_rem(1 - k, j).wait_recv()

    def wait_third(k, c):
        w_rem(k, c).wait_recv()

    def wait_all(k):
        for c in range(3):
            wait_third(1 - k, c)

    when((L == 0) & (e == 1), x_copy.start)
    per_core(send_rows)
    when((L == 1) & (e == 0), lambda: send_thirds(0))
    when(e == 1, lambda: send_thirds(1))
    mol_copy.start()
    key_copy.start()

    def toks():
        tok_copy(1).start()
        tok_copy(2).start()

    when(L == 1, toks)
    cu = dotf(rot, cot[...]).astype(BF).reshape(2, T, D)

    def cots0():
        ex[...] = cu
        cot_copy(0).start()

    def cots1():
        G[1:3] = cu

    when(L == 0, cots0)
    when(L == 1, cots1)
    i0 = lax.broadcasted_iota(I32, (16, 256), 0)
    i1 = lax.broadcasted_iota(I32, (16, 256), 1)
    lo = HS * i0 - jnp.where(i0 < 10, 0, 128)
    hm[...] = jnp.where((i1 >= lo) & (i1 < lo + HS), 1.0, 0.0).astype(BF)
    glp[...] = jnp.zeros_like(glp)
    pair_bias(mol[...], key[...], rot, mb, L, R)

    def turn_weights():
        @pl.loop(0, 3)
        def _(i):
            cs = at(i, D)
            waT[cs, :] = wa[:, cs].T
            wfT[cs, :] = wf[:, cs].T

    def other_bias():
        mol_copy.wait()
        key_copy.wait()
        rot_o, _ = rotation(molo[...], R)
        pair_bias(molo[...], keyo[...], rot_o, mb, 1 - L, R)

    def ready1():
        other_bias()
        per_core(wait_local)
        per_core(wait_rows)
        per_core(wait_all)
        turn_weights()

    when(L == 1, ready1)

    def mw_copy(k, u):
        return remote((wta, wtf)[k].at[u], mw.at[u], mw_s.at[u], mw_r.at[u], mate)

    def mr_copy(k, u, c):
        src = (U["an"].at[u], U["cfa"].at[u, c])[k]
        return remote(src, mr.at[u, c], mr_s.at[u, c], mr_r.at[u, c], mate)

    def mine(k, u, r, c):
        left = jnp.concatenate([(wta, wtf)[k][u, r, :], mw[u, r, :]], axis=1)
        right = jnp.concatenate([U["an"][u] if k == 0 else U["cfa"][u, c], mr[u, c]], axis=0)
        return left, right

    def all_units(k, r, c):
        parts = [mine(k, u, r, c) for u in range(4)]
        return dotf(
            jnp.concatenate([a for a, _ in parts], axis=1), jnp.concatenate([b for _, b in parts], axis=0)
        )

    def wait_factors(k):
        for u in range(4):
            mw_copy(k, u).wait_recv()
            for c in range(1 if k == 0 else 3):
                if k == 0 and u == 0:
                    when(L == 1, lambda: mr_copy(0, 0, 0).wait_recv())
                else:
                    mr_copy(1, u, c).wait_recv()

    if fused:
        yb, inb, raw, acc, gy, gz, gn, ry_s, ry_r, rz_s, rz_r, rw_s, rw_r, rg_s, rg_r = scr[n + 64:]
        CH = 3 * D // (2 * NZ)
        SR = CH // SUB
        dest = [by_place([ORDER[k][i] for k in range(NZ)], z) for i in range(NZ)]
        buddy = z + 1 - 2 * lax.rem(z, 2)

        def rows(zz, yy, q):
            return pl.ds(pl.multiple_of((zz * 2 + yy) * CH + q * SR, 16), SR)

        def y_copy(i, q):
            return remote(rb.at[rows(dest[i], 1 - y, q), :], yb.at[i, q], ry_s.at[i, q], ry_r.at[i, q], across)

        def raw_copy(q):
            return remote(
                rb.at[rows(buddy, 1 - y, q), :], raw.at[q], rw_s.at[q], rw_r.at[q], on_line(buddy)
            )

        def hop(i, q):
            zz = dest[i]
            nz = jnp.where(zz > z, z + 1, z - 1)
            slot = jnp.where((nz == zz) & (z > zz), NZ, zz)
            return remote(yb.at[i, q], inb.at[slot, q], rz_s.at[i, q], rz_r.at[slot, q], on_line(nz))

        def piece(i):
            return pl.ds(pl.multiple_of(dest[i] * (2 * CH), 16), 2 * CH)
    else:
        def piece(i):
            return pl.ds(i * (3 * D // NZ), 3 * D // NZ)

    def finish(k, i):
        n3 = 3 * D // NZ // 3
        if i == 0:
            wait_factors(k)
        if k == 0:
            r = piece(i)
            rb[r, :] = all_units(0, r, 0).astype(BF)
        else:
            for h in range(3):
                blk = (dest[i] if fused else i) * 3 + h
                r = pl.ds(pl.multiple_of(blk * n3, 16), n3)
                rb[r, :] = all_units(1, r, blk * n3 // D).astype(BF)
        if fused and i < NZ - 1:
            def to_buddy():
                for q in range(HALF):
                    raw_copy(q).start()

            def halves():
                for q in range(HALF):
                    y_copy(i, q).start()

            when(dest[i] == buddy, to_buddy)
            when(dest[i] != buddy, halves)
            for q in range(HALF, SUB):
                y_copy(i, q).start()

    def finish_rest(k):
        for i in range(1, NZ):
            finish(k, i)

    def y_copy_x(u):
        return remote(ys.at[u], X.at[u], y_s.at[u], y_r.at[u], other)

    def fo_copy(u):
        return remote(ys.at[u], fob.at[u // 3], fo_s.at[u // 3], fo_r.at[u // 3], other)

    def g_copy(u):
        return remote(gx.at[u], G.at[u], g_s.at[u], g_r.at[u], other)

    def ig_copy(u):
        return remote(gx.at[u], igb.at[u - 1], ig_s.at[u - 1], ig_r.at[u - 1], other)

    def share(u):
        def factors0():
            for c in range(3):
                mr_copy(1, u, c).start()

        when(e == 0, factors0)
        when((e == 1) & ((L == 1) | (u > 0)), lambda: mr_copy(0, u, 0).start())

    def lend():
        wait_local(0)
        x_copy.wait_recv()
        mr[0, 0] = ln_rows(U["an"][3].astype(F32), lga[...], lba[...])[2]
        U["qkv"][3] = dotf(mr[0, 0], wa[...]).astype(BF)
        q_copy.start()
        send_thirds(0)
        own_projection()

    def borrow():
        wait_local(1)
        first["norm_a"]()
        q_copy.wait_recv()

    def opening():
        when(e == 0, lend)
        per_core(wait_rows)
        when(e == 1, borrow)
        for name in ("flip", "scores", "mix_values"):
            first[name]()
        for c, name in enumerate(("mixed", "act", "branch")):
            when(e == 0, lambda c=c: wait_third(1, c))
            first[name]()
            if name == "mixed":
                first["norm_f"]()
        y_copy_x(0).start()
        share(0)
        other_bias()
        when(e == 0, q_copy.wait_send)
        when(e == 1, x_copy.wait_send)
        when(e == 1, lambda: wait_all(1))

    def after_forward(u):
        share(u)

        def keep():
            fob[u - 1] = ys[u]

        when((L == 1) & ((u == 1) | (u == 2)), keep)

    def forward(u):
        when(L == 1, lambda: y_copy_x(u).wait_recv())
        when((L == 0) & (u < 3), lambda: tok_copy(u).wait_recv())
        for f in unit_forward(u):
            f()
        when(L == 0, lambda: y_copy_x(u).start())
        when((L == 0) & (u == 3), lambda: cot_copy(u).start())
        after_forward(u)

    def unit_backward(u):
        S = {k: r.at[u] for k, r in U.items()}
        return backward_stages(
            G.at[u], gx.at[u], waT, wfT, (lga, lba), (lgf, lbf), hm, S,
            {"a": wta.at[u], "f": wtf.at[u]},
            glp, gb, gctx, gctxT, gqT, gsT, vec,
        )

    def after_backward(u):
        when(L == 1, lambda: g_copy(u).start())
        per_core(lambda k: mw_copy(1 - k, u).start())

    def backward(u):
        when((L == 0) & (u == 0), turn_weights)
        when(L == 1, lambda: cot_copy(u).wait_recv())
        when(L == 0, lambda: g_copy(u).wait_recv())
        for f in unit_backward(u):
            f()
        after_backward(u)
        when((L == 0) & (u > 0), lambda: ig_copy(u).start())

        def keep():
            igb[0] = gx[0]

        when((L == 0) & (u == 0), keep)

    def both_ways(u):
        y_copy_x(u + 1).wait_recv()
        when(u == 0, lambda: cot_copy(0).wait_recv())
        fs, bs = unit_forward(u + 1, ctxT, ig.at[pl.ds(0, T)]), unit_backward(u)
        for i in range(max(len(fs), len(bs))):
            for st in (bs, fs):
                if i < len(st):
                    st[i]()
        after_backward(u)
        after_forward(u + 1)

    gl_copy = remote(glp, glr, gl_s, gl_r, mate)

    def closing():
        g_copy(3).wait_recv()
        for f in unit_backward(3):
            f()
            if f.__name__ == "g_context":
                when(e == 0, lambda: mw_copy(1, 3).start())
            if f.__name__ == "g_merge":
                when(e == 1, lambda: mw_copy(0, 3).start())
                when(e == 1, lambda: finish(1, 0))
        igb[1] = gx[3]

    when(L == 0, opening)

    @pl.loop(0, 7)
    def _(i):
        is_f = jnp.where(L == 0, jnp.where((i >= 1) & (i <= 3), 1, 0), jnp.where(i == 0, 1, 0))
        is_b = jnp.where(L == 0, jnp.where(i >= 4, 1, 0), jnp.where(i == 4, 1, 0))
        when(is_f == 1, lambda: forward(i))
        when((L == 1) & (i >= 1) & (i <= 3), lambda: both_ways(i - 1))
        when(is_b == 1, lambda: backward(jnp.where(L == 0, i - 4, 3)))

    when(L == 0, closing)
    gl_copy.start()
    when(e == 0, lambda: finish(0, 0))
    when((e == 1) & (L == 1), lambda: finish(1, 0))
    gl_copy.wait()
    glr[...] = glp[...] + glr[...]
    if fused:
        gy_copy = remote(glr, gy, rg_s.at[0], rg_r.at[0], across)
        gy_copy.start()
    per_core(finish_rest)

    def send_fo():
        for u in (0, 3):
            fo_copy(u).start()

    when(L == 1, send_fo)
    emits = []

    def bring():
        def bring0():
            for u in (0, 3):
                fo_copy(u).wait_recv()

        def bring1():
            for u in (1, 2):
                ig_copy(u).wait_recv()

        when(L == 0, bring0)
        when(L == 1, bring1)
        fo[...] = dotf(rinv[...], fob[...].reshape(R, D)).astype(BF)
        ig[...] = dotf(rinv[...], igb[...].reshape(R, D))
        emits.extend([pltpu.make_async_copy(fo, fo_hbm, o_s.at[0]), pltpu.make_async_copy(ig, ig_hbm, o_s.at[1])])
        for c in emits:
            c.start()

    if fused:
        def own_y():
            for q in range(SUB):
                if q < HALF:
                    raw_copy(q).wait()
                    r = rows(z, 1 - y, q)
                    rb[r, :] = (rb[r, :].astype(F32) + raw[q].astype(F32)).astype(BF)
                y_copy(NZ - 1, q).start()

        def arrived(slot, q):
            remote(yb.at[0, q], inb.at[slot, q], rz_s.at[0, q], rz_r.at[slot, q], across).wait_recv()

        for i in range(NZ - 1):
            zz = dest[i]
            for q in range(SUB):
                mine = rb.at[rows(zz, y, q), :]

                def combine(i=i, q=q, mine=mine):
                    y_copy(i, q).wait_recv()
                    yb[i, q] = (mine[...].astype(F32) + yb[i, q].astype(F32)).astype(BF)

                def plain(i=i, q=q, mine=mine):
                    yb[i, q] = mine[...]

                def add_in(i=i, q=q, zz=zz):
                    arrived(zz, q)
                    yb[i, q] = (yb[i, q].astype(F32) + inb[zz, q].astype(F32)).astype(BF)

                if q < HALF:
                    when(zz != buddy, combine)
                    when(zz == buddy, plain)
                else:
                    combine()
                when(jnp.where(zz > z, z > 0, z < NZ - 1), add_in)
                hop(i, q).start()
            if i == 0:
                gy_copy.wait()
                gl2 = glr[...] + gy[...]
                gn[...] = gl2
                gz_copies = [
                    remote(gn, gz.at[NZ - t - 1], rg_s.at[t], rg_r.at[NZ - t], on_line(lax.rem(z + t, NZ)))
                    for t in range(1, NZ)
                ]
                for c in gz_copies:
                    c.start()
            if i == NZ - 3:
                own_y()
        bring()
        w_copies = []
        for q in range(SUB):
            acc[q] = rb[rows(z, y, q), :].astype(F32)

            def from_left(q=q):
                arrived(z, q)
                acc[q] += inb[z, q].astype(F32)

            def from_right(q=q):
                arrived(NZ, q)
                acc[q] += inb[NZ, q].astype(F32)

            when(z > 0, from_left)
            when(z < NZ - 1, from_right)
            y_copy(NZ - 1, q).wait_recv()
            acc[q] += yb[NZ - 1, q].astype(F32)
            w_copies.append(pltpu.make_async_copy(acc.at[q], w_hbm.at[pl.ds(q * SR, SR)], o_s.at[2 + q]))
            w_copies[-1].start()
        for i in range(NZ):
            for q in range(SUB):
                if q < HALF and i < NZ - 1:
                    when(dest[i] != buddy, lambda i=i, q=q: y_copy(i, q).wait_send())
                else:
                    y_copy(i, q).wait_send()
                if i < NZ - 1:
                    hop(i, q).wait_send()
        for t, c in zip(range(1, NZ), gz_copies):
            c.wait_send()
        for k in range(NZ - 1):
            remote(gn, gz.at[k], rg_s.at[0], rg_r.at[k + 1], across).wait_recv()
        gl3 = gl2 + gz[0] + gz[1] + gz[2]
        part = D // (2 * NZ)
        for k in range(2 * NZ):
            def own_part(k=k):
                for j in range(2):
                    v = gl3[:, k * part:(k + 1) * part]
                    norms[j][...] = jnp.where(e == 0, v[j:j + 1, :], v[2 + j:3 + j, :])

            when(d == k, own_part)
    else:
        bring()
        norms[0][...] = glr[...]
        w_copies = [pltpu.make_async_copy(rb, w_hbm, o_s.at[2])]
        w_copies[0].start()
    for c in emits + w_copies:
        c.wait()

    def close_weights(k):
        for j in range(5):
            w_rem(k, j).wait_send()

    per_core(close_weights)
    def gave0():
        for u in range(4):
            mw_copy(1, u).wait_send()
            for c in range(3):
                mr_copy(1, u, c).wait_send()

    def gave1():
        for u in range(4):
            mw_copy(0, u).wait_send()
            if u == 0:
                when(L == 1, lambda: mr_copy(0, 0, 0).wait_send())
            else:
                mr_copy(0, u, 0).wait_send()

    when(e == 0, gave0)
    when(e == 1, gave1)
    for u in (1, 2):
        tok_copy(u).wait_send()

    def close0():
        for u in range(4):
            y_copy_x(u).wait_send()
        for u in (1, 2):
            ig_copy(u).wait_send()

    def close1():
        for u in range(4):
            g_copy(u).wait_send()
        for u in (0, 3):
            fo_copy(u).wait_send()

    when(L == 0, close0)
    when(L == 1, close1)


def relay(fused, tok, cot, w, gain, bias, mol, key):
    R, D = tok.shape
    V = pl.BlockSpec(memory_space=pltpu.VMEM)
    dma, vm = pltpu.SemaphoreType.DMA, pltpu.VMEM
    scratch = [vm((4,) + sh, dt) for sh, dt in unit_shapes(D)] + [
        vm((D, 3 * D), BF), vm((D, 3 * D), BF), vm((3 * D, D), BF), vm((3 * D, D), BF),
        vm((1, D), F32), vm((1, D), F32), vm((1, D), F32), vm((1, D), F32),
        vm((1, R), I32), vm((1, R), I32), vm((R, R), BF), vm((16, 256), BF), vm((4, T, T), F32),
        vm((4, T, D), BF), vm((4, T, D), BF), vm((2, T, D), BF), vm((4, T, D), BF), vm((4, T, D), BF),
        vm((2, T, D), BF), vm((2, T, D), BF),
        vm((4, 3 * D, T), BF), vm((4, 3 * D, T), BF), vm((4, 3 * D, T), BF), vm((4, 3, T, D), BF),
        vm((3 * D, D), BF), vm((8, D), F32), vm((8, D), F32),
        vm((D, T), F32), vm((T, D), F32), vm((T, D), BF), vm((T, D), BF), vm((D, T), BF),
        vm((3 * D, T), F32), vm((HEADS, T, T), BF),
        dma((3,)), dma((3,)), dma((3,)), dma((2,)), dma((2,)), dma((2,)), dma((2,)), dma((2,)), dma((2,)),
        dma((4,)), dma((4,)), dma((2,)), dma((2,)), dma((4,)), dma((4,)), dma((2,)), dma((2,)),
        dma((4,)), dma((4,)), dma((4, 3)), dma((4, 3)), dma, dma, dma, dma, dma, dma, vm((R, D), BF), vm((R, D), F32), dma((2 + SUB,)),
    ]
    if fused:
        CH = 3 * D // (2 * NZ)
        SR = CH // SUB
        scratch += [
            vm((NZ, SUB, SR, D), BF), vm((NZ + 1, SUB, SR, D), BF), vm((HALF, SR, D), BF),
            vm((SUB, SR, D), F32), vm((8, D), F32), vm((NZ - 1, 8, D), F32), vm((8, D), F32),
            dma((NZ, SUB)), dma((NZ, SUB)), dma((NZ - 1, SUB)), dma((NZ + 1, SUB)),
            dma((HALF,)), dma((HALF,)), dma((NZ,)), dma((NZ,)),
        ]
        outs = [jax.ShapeDtypeStruct((CH, D), F32)] + [jax.ShapeDtypeStruct((1, D // (2 * NZ)), F32)] * 2
    else:
        outs = [jax.ShapeDtypeStruct((3 * D, D), BF), jax.ShapeDtypeStruct((8, D), F32)]
    A = pl.BlockSpec(memory_space=pl.ANY)
    return pl.pallas_call(
        lambda *refs: relay_kernel(fused, *refs),
        out_shape=[jax.ShapeDtypeStruct((R, D), BF), jax.ShapeDtypeStruct((R, D), F32)] + outs,
        in_specs=[V, V, A, V, V, V, V],
        out_specs=[A, A, A] + [V] * (len(outs) - 1),
        scratch_shapes=scratch,
        compiler_params=pltpu.CompilerParams(
            collective_id=0, has_side_effects=True, vmem_limit_bytes=64 << 20
        ),
        name="relay",
    )(tok, cot, w, gain, bias, mol, key)


def emit_kernel(*refs):
    n = len(refs) // 3
    sems = refs[-1]
    ins = [pltpu.make_async_copy(refs[i], refs[2 * n + i], sems.at[0, i]) for i in range(n)]
    outs = [pltpu.make_async_copy(refs[2 * n + i], refs[n + i], sems.at[1, i]) for i in range(n)]
    for c in ins:
        c.start()
    for a, b in zip(ins, outs):
        a.wait()
        b.start()
    for c in outs:
        c.wait()


def emit(arrays):
    A = pl.BlockSpec(memory_space=pl.ANY)
    n = len(arrays)
    return pl.pallas_call(
        emit_kernel,
        out_shape=[jax.ShapeDtypeStruct(a.shape, a.dtype) for a in arrays],
        in_specs=[A] * n,
        out_specs=[A] * n,
        scratch_shapes=[pltpu.VMEM(a.shape, a.dtype) for a in arrays] + [pltpu.SemaphoreType.DMA((2, n))],
        name="emit",
    )(*arrays)


def shards(tokens, cotangent, section_weight, norm_gain, norm_bias, mol_ids, key_mask):
    fused = lax.axis_size("dp") == 2 * NZ
    got = relay(fused, tokens, cotangent, section_weight[0], norm_gain, norm_bias, mol_ids, key_mask)
    if fused:
        fo, ig, gw, gg, gb = emit(got)
        return fo, ig, gw.T[None], gg, gb
    fo, ig, gw, gn = got
    e = lax.rem(lax.axis_index("section"), 2)
    gn = lax.dynamic_slice_in_dim(gn, 2 * e, 2, 0)
    gw = lax.psum_scatter(gw, "dp", scatter_dimension=0, tiled=True)
    gn = lax.psum_scatter(gn, "dp", scatter_dimension=1, tiled=True)
    return fo, ig, gw.astype(F32).T[None], gn[0:1], gn[1:2]


def solution(mesh):
    return jax.shard_map(
        shards,
        mesh=mesh,
        in_specs=(
            P(("dp", "section"), None),
            P(("dp", "section"), None),
            P("section", None, None),
            P("section", None),
            P("section", None),
            P(("dp", "section"), None),
            P(("dp", "section"), None),
        ),
        out_specs=(
            P(("dp", "section"), None),
            P(("dp", "section"), None),
            P("section", None, "dp"),
            P("section", "dp"),
            P("section", "dp"),
        ),
        check_vma=False,
    )
```

```python
import jax
import jax.numpy as jnp
from jax import lax
from jax.experimental import pallas as pl
from jax.experimental.pallas import tpu as pltpu
from jax.sharding import PartitionSpec as P

HEADS = 32
HS = 24
EPS = 1e-5
NEG = -1e30
BF = jnp.bfloat16
F32 = jnp.float32
I32 = jnp.int32
MESH = pl.DeviceIdType.MESH
GELU_A = 0.7978845608028654
GELU_B = 0.044715
LOG2E = 1.4426950408889634
T = 128


def dotf(a, b):
    return jnp.dot(a, b, preferred_element_type=F32)


def dot_t(a, b):
    return lax.dot_general(a, b, (((1,), (1,)), ((), ())), preferred_element_type=F32)


def at(i, n):
    return pl.ds(pl.multiple_of(i * n, n), n)


HEAD_WIN = (0,) * 10 + (1,) * 6


def ln_rows(x, g, b):
    c = x - jnp.mean(x, axis=-1, keepdims=True)
    r = lax.rsqrt(jnp.mean(c * c, axis=-1, keepdims=True) + EPS)
    xh = c * r
    return xh, r, (xh * g + b).astype(BF)


def windows(ref, rows, base):
    return [ref[rows, base + 128 * w:base + 128 * w + 256] for w in (0, 1)]


def put_heads(ref, base, j, v):
    ref[base + 48 * j:base + 48 * j + 24, :] = v[0:24, 0:T]
    ref[base + 48 * j + 24:base + 48 * j + 48, :] = v[24:48, T:2 * T]


def two(ref, i, axis):
    return jnp.concatenate([ref[i], ref[i + 1]], axis=axis)


def forward_stages(x, y, wa, wf, lna, lnf, mb, hm, S, ctxT, vec):
    D = x.shape[1]

    def norm_a():
        S["xha"][...], S["ra"][...], S["an"][...] = ln_rows(x[...].astype(F32), lna[0][...], lna[1][...])

    def project():
        S["qkv"][...] = dotf(S["an"][...], wa[...]).astype(BF)

    def flip():
        S["qkvT"][...] = S["qkv"][...].T

    def scores():
        bias = mb[...]
        for g in range(2):
            base = g * 384
            qw = windows(S["qkv"], slice(None), base)
            kw = windows(S["qkv"], slice(None), D + base)
            for h in range(16):
                w = HEAD_WIN[h]
                s = dot_t(kw[w] * hm[h:h + 1, :], qw[w]) * (HS ** -0.5 * LOG2E) + bias
                ex = jnp.exp2(s - jnp.max(s, axis=0, keepdims=True))
                S["pT"][g * 16 + h] = (ex * (1.0 / jnp.sum(ex, axis=0, keepdims=True))).astype(BF)

    def mix_values():
        for g in range(2):
            base = g * 384
            for j in range(8):
                vt = S["qkvT"][2 * D + base + 48 * j:2 * D + base + 48 * j + 48, :]
                put_heads(ctxT, base, j, dotf(vt, two(S["pT"], g * 16 + 2 * j, 1)))

    def mixed():
        S["cfa"][0] = ctxT[...].astype(BF).T
        vec[...] = x[...].astype(F32) + dotf(S["cfa"][0], wf[:, 0:D])

    def norm_f():
        S["xhf"][...], S["rf"][...], S["cfa"][1] = ln_rows(vec[...], lnf[0][...], lnf[1][...])

    def act():
        u = dotf(S["cfa"][1], wf[:, D:2 * D])
        u2 = u * u
        t = jnp.tanh(GELU_A * (u + GELU_B * u * u2))
        S["cfa"][2] = (0.5 * u * (1.0 + t)).astype(BF)
        S["gp"][...] = 0.5 * (1.0 + t) + 0.5 * u * (1.0 - t * t) * (GELU_A + 3 * GELU_A * GELU_B * u2)

    def branch():
        br = dotf(S["cfa"][2], wf[:, 2 * D:3 * D]).astype(BF).astype(F32)
        y[...] = (vec[...].astype(BF).astype(F32) + br).astype(BF)

    return [norm_a, project, flip, scores, mix_values, mixed, norm_f, act, branch]


def backward_stages(G, gx, waT, wfT, lna, lnf, hm, S, W, glp, gb, gctx, gctxT, gqT, gsT, vec):
    D = G.shape[1]

    def ln_back(gref, xh, r, g, gi, resid, out):
        gn = gref[...]
        x = xh[...]
        gg = gn * g
        m1 = jnp.mean(gg, axis=-1, keepdims=True)
        m2 = jnp.mean(gg * x, axis=-1, keepdims=True)
        out[...] = (r[...] * (gg - m1 - x * m2) + resid[...].astype(F32)).astype(BF)
        glp[gi:gi + 1, :] += jnp.sum(gn * x, axis=0, keepdims=True)
        glp[gi + 1:gi + 2, :] += jnp.sum(gn, axis=0, keepdims=True)

    def g_act():
        W["f"][2 * D:3 * D, :] = G[...].T
        gb[...] = (dotf(G[...], wfT[2 * D:3 * D, :]) * S["gp"][...]).astype(BF)

    def g_norm():
        W["f"][D:2 * D, :] = gb[...].T
        vec[...] = dotf(gb[...], wfT[D:2 * D, :])

    def g_hidden():
        ln_back(vec, S["xhf"], S["rf"], lnf[0][...], 2, G, gb)

    def g_context():
        W["f"][0:D, :] = gb[...].T
        t = dotf(gb[...], wfT[0:D, :]).astype(BF)
        gctx[...] = t
        gctxT[...] = t.T

    def g_scores():
        for g in range(2):
            base = g * 384
            vw = windows(S["qkv"], slice(None), 2 * D + base)
            gw = windows(gctx, slice(None), base)
            for h in range(16):
                w = HEAD_WIN[h]
                gp = dot_t(vw[w] * hm[h:h + 1, :], gw[w])
                p = S["pT"][g * 16 + h].astype(F32)
                d = jnp.sum(p * gp, axis=0, keepdims=True)
                gsT[g * 16 + h] = (p * (gp - d)).astype(BF)

    def g_heads():
        for g in range(2):
            base = g * 384
            for j in range(8):
                i = g * 16 + 2 * j
                at48 = slice(base + 48 * j, base + 48 * j + 48)
                put_heads(gqT, 2 * D + base, j, dot_t(gctxT[at48, :], two(S["pT"], i, 0)))
                put_heads(gqT, D + base, j, dot_t(S["qkvT"][at48, :], two(gsT, i, 0)) * HS ** -0.5)
                k48 = slice(D + base + 48 * j, D + base + 48 * j + 48)
                put_heads(gqT, base, j, dotf(S["qkvT"][k48, :], two(gsT, i, 1)) * HS ** -0.5)

    def g_merge():
        t = gqT[...].astype(BF)
        W["a"][...] = t
        S["qkv"][...] = t.T

    def g_input():
        vec[...] = dotf(S["qkv"][...], waT[...])

    def g_x():
        ln_back(vec, S["xha"], S["ra"], lna[0][...], 0, gb, gx)

    return [g_act, g_norm, g_hidden, g_context, g_scores, g_heads, g_merge, g_input, g_x]


def remote(src, dst, ss, rs, dev):
    return pltpu.make_async_remote_copy(
        src_ref=src, dst_ref=dst, send_sem=ss, recv_sem=rs, device_id=dev, device_id_type=MESH
    )


def when(cond, fn):
    pl.when(cond)(fn)


NZ = 4
SUB = 3
HALF = 1
ORDER = ((3, 2, 1, 0), (3, 0, 2, 1), (0, 3, 1, 2), (0, 1, 2, 3))


def by_place(vals, z):
    r = vals[-1]
    for i in range(len(vals) - 2, -1, -1):
        r = jnp.where(z == i, vals[i], r)
    return r


def rotation(mol, R):
    c0 = jnp.sum((mol == 0).astype(I32), axis=1, keepdims=True)
    c1 = jnp.sum((mol == 1).astype(I32), axis=1, keepdims=True)
    start = jnp.where(c0 == T, 0, jnp.where(c1 == T, c0, c0 + c1))
    i0 = lax.broadcasted_iota(I32, (R, R), 0)
    i1 = lax.broadcasted_iota(I32, (R, R), 1)

    def onehot(a, b):
        t = a + start
        t = jnp.where(t >= R, t - R, t)
        return jnp.where(t == b, 1.0, 0.0).astype(BF)

    return onehot(i0, i1), onehot(i1, i0)


def pair_bias(mol, key, rot, out, mine, R):
    mk = jnp.concatenate([mol, key, jnp.zeros((6, R), I32)], axis=0).astype(F32).astype(BF)
    row = dot_t(mk, rot)
    col = dot_t(rot, mk)
    k0 = lax.broadcasted_iota(I32, (T, T), 0)
    q0 = lax.broadcasted_iota(I32, (T, T), 1)
    for b in range(R // T):
        rs = slice(b * T, b * T + T)
        ok = (col[rs, 0:1] == row[0:1, rs]) & ((col[rs, 1:2] > 0.5) | (k0 == q0))
        out[jnp.where(mine == 0, 3 * b, 1 + b)] = jnp.where(ok, 0.0, NEG)


UNIT = ("xha", "ra", "an", "qkv", "qkvT", "pT", "xhf", "rf", "cfa", "gp")


def unit_shapes(D):
    return (
        ((T, D), F32), ((T, 1), F32), ((T, D), BF), ((T, 3 * D), BF), ((3 * D, T), BF),
        ((HEADS, T, T), BF), ((T, D), F32), ((T, 1), F32), ((3, T, D), BF), ((T, D), F32),
    )


def relay_kernel(fused, tok_hbm, cot_hbm, w, gain, bias, mol_hbm, key_hbm, fo_hbm, ig_hbm, w_hbm, *scr):
    R, D = tok_hbm.shape
    norms_hbm, scr = (scr[:2], scr[2:]) if fused else (scr[:1], scr[1:])
    n = len(UNIT)
    U = {k: r for k, r in zip(UNIT, scr[:n])}
    (
        wa, wf, waT, wfT, lga, lba, lgf, lbf, molo, keyo, rinv, hm, mb, X, G, ex, ys, gx, fob, igb,
        wta, wtf, mw, mr, rb, glp, glr, ctxT, vec, gb, gctx, gctxT, gqT, gsT,
        wl_s, w_s, w_r, l_s, l_r, m_s, m_r, ex_s, ex_r, y_s, y_r, fo_s, fo_r, g_s, g_r, ig_s, ig_r,
        mw_s, mw_r, mr_s, mr_r, x_s, x_r, q_s, q_r, gl_s, gl_r, fo, ig, o_s,
        tok, cot, mol, key, i_s, n_s,
    ) = scr[n:n + 70]
    s = lax.axis_index("section")
    e = lax.rem(s, 2)
    L = s // 2
    mate = {"section": s + 1 - 2 * e}
    other = {"section": s + 2 - 4 * L}
    d = lax.axis_index("dp")
    z = d // 2
    y = d - 2 * z
    across = {"dp": d + 1 - 2 * y}

    def on_line(zz):
        return {"dp": zz * 2 + y}

    bar = pltpu.get_barrier_semaphore()
    peers = [mate, other]
    if fused:
        peers += [across] + [on_line(lax.rem(z + t, NZ)) for t in range(1, NZ)]
    for p in peers:
        pl.semaphore_signal(bar, inc=1, device_id=p, device_id_type=MESH)

    own = ((wa, lga, lba), (wf, lgf, lbf))

    def per_core(fn):
        when(e == 0, lambda: fn(0))
        when(e == 1, lambda: fn(1))

    def third(c):
        return (slice(None), pl.ds(c * D, D))

    def w_local(k, j):
        src = (w, gain, bias)[j]
        return pltpu.make_async_copy(src, own[k][j], wl_s.at[j])

    def w_rem(k, j):
        if j < 3:
            return remote(w.at[third(j)], own[k][0].at[third(j)], w_s.at[j], w_r.at[j], mate)
        src = (gain, bias)[j - 3]
        return remote(src, own[k][j - 2], l_s.at[j - 3], l_r.at[j - 3], mate)

    def start_local(k):
        for j in range(3):
            w_local(k, j).start()

    def wait_local(k):
        for j in range(3):
            w_local(k, j).wait()

    inputs = [
        pltpu.make_async_copy(a, b, i_s.at[i])
        for i, (a, b) in enumerate(((mol_hbm, mol), (key_hbm, key), (tok_hbm, tok), (cot_hbm, cot)))
    ]
    for c in inputs:
        c.start()
    per_core(start_local)
    inputs[0].wait()
    inputs[1].wait()
    rot, inv = rotation(mol[...], R)
    inputs[2].wait()
    rinv[...] = inv
    xu = dotf(rot, tok[...]).astype(BF).reshape(2, T, D)

    def rows0():
        X[0] = xu[0]
        X[3] = xu[1]

    def rows1():
        ex[...] = xu

    when(L == 0, rows0)
    when(L == 1, rows1)

    def unit_forward(u, heads=None, rows=None):
        S = {k: r.at[u] for k, r in U.items()}
        return forward_stages(
            X.at[u], ys.at[u], wa, wf, (lga, lba), (lgf, lbf), mb.at[u], hm, S,
            gqT.at[pl.ds(0, D)] if heads is None else heads, vec if rows is None else rows,
        )

    first = {f.__name__: f for f in unit_forward(0)}

    def own_projection():
        first["norm_a"]()
        first["project"]()

    pl.semaphore_wait(bar, len(peers))

    x_copy = remote(X.at[0], U["an"].at[3], x_s, x_r, mate)
    q_copy = remote(U["qkv"].at[3], U["qkv"].at[0], q_s, q_r, mate)
    mol_copy = remote(mol, molo, m_s.at[0], m_r.at[0], other)
    key_copy = remote(key, keyo, m_s.at[1], m_r.at[1], other)

    def cot_copy(u):
        return remote(ex.at[u // 3], G.at[u], ex_s.at[u // 3], ex_r.at[u // 3], other)

    def tok_copy(u):
        return remote(ex.at[u - 1], X.at[u], ex_s.at[u - 1], ex_r.at[u - 1], other)

    def send_rows(k):
        for j in (3, 4):
            w_rem(k, j).start()

    def send_thirds(k):
        for j in range(3):
            w_rem(k, j).start()

    def send_from(k, c):
        for j in range(c, 3):
            w_rem(k, j).start()

    def wait_rows(k):
        for j in (3, 4):
            w_rem(1 - k, j).wait_recv()

    def wait_third(k, c):
        w_rem(k, c).wait_recv()

    def wait_all(k):
        for c in range(3):
            wait_third(1 - k, c)

    when((L == 0) & (e == 1), x_copy.start)
    per_core(send_rows)
    when((L == 1) & (e == 0), lambda: send_thirds(0))
    when((L == 0) & (e == 0), lambda: w_rem(0, 0).start())
    when(e == 1, lambda: send_thirds(1))
    mol_copy.start()
    key_copy.start()

    def toks():
        tok_copy(1).start()
        tok_copy(2).start()

    when(L == 1, toks)
    inputs[3].wait()
    cu = dotf(rot, cot[...]).astype(BF).reshape(2, T, D)

    def cots0():
        ex[...] = cu
        cot_copy(0).start()

    def cots1():
        G[1:3] = cu

    when(L == 0, cots0)
    when(L == 1, cots1)
    i0 = lax.broadcasted_iota(I32, (16, 256), 0)
    i1 = lax.broadcasted_iota(I32, (16, 256), 1)
    lo = HS * i0 - jnp.where(i0 < 10, 0, 128)
    hm[...] = jnp.where((i1 >= lo) & (i1 < lo + HS), 1.0, 0.0).astype(BF)
    glp[...] = jnp.zeros_like(glp)
    pair_bias(mol[...], key[...], rot, mb, L, R)

    def turn_weights():
        @pl.loop(0, 3)
        def _(i):
            cs = at(i, D)
            waT[cs, :] = wa[:, cs].T
            wfT[cs, :] = wf[:, cs].T

    def other_bias():
        mol_copy.wait()
        key_copy.wait()
        rot_o, _ = rotation(molo[...], R)
        pair_bias(molo[...], keyo[...], rot_o, mb, 1 - L, R)

    def ready1():
        other_bias()
        per_core(wait_local)
        per_core(wait_rows)
        per_core(wait_all)
        turn_weights()

    when(L == 1, ready1)

    def mw_copy(k, u):
        return remote((wta, wtf)[k].at[u], mw.at[u], mw_s.at[u], mw_r.at[u], mate)

    def mr_copy(k, u, c):
        src = (U["an"].at[u], U["cfa"].at[u, c])[k]
        return remote(src, mr.at[u, c], mr_s.at[u, c], mr_r.at[u, c], mate)

    def mine(k, u, r, c):
        left = jnp.concatenate([(wta, wtf)[k][u, r, :], mw[u, r, :]], axis=1)
        right = jnp.concatenate([U["an"][u] if k == 0 else U["cfa"][u, c], mr[u, c]], axis=0)
        return left, right

    def all_units(k, r, c):
        parts = [mine(k, u, r, c) for u in range(4)]
        return dotf(
            jnp.concatenate([a for a, _ in parts], axis=1), jnp.concatenate([b for _, b in parts], axis=0)
        )

    def wait_factors(k):
        for u in range(4):
            mw_copy(k, u).wait_recv()
            for c in range(1 if k == 0 else 3):
                if k == 0 and u == 0:
                    when(L == 1, lambda: mr_copy(0, 0, 0).wait_recv())
                else:
                    mr_copy(1, u, c).wait_recv()

    if fused:
        yb, inb, raw, acc, gy, gz, gn, norm_g, norm_b, ry_s, ry_r, rz_s, rz_r, rw_s, rw_r, rg_s, rg_r = scr[n + 70:]
        norms = (norm_g, norm_b)
        CH = 3 * D // (2 * NZ)
        SR = CH // SUB
        dest = [by_place([ORDER[k][i] for k in range(NZ)], z) for i in range(NZ)]
        buddy = z + 1 - 2 * lax.rem(z, 2)

        def rows(zz, yy, q):
            return pl.ds(pl.multiple_of((zz * 2 + yy) * CH + q * SR, 16), SR)

        def y_copy(i, q):
            return remote(rb.at[rows(dest[i], 1 - y, q), :], yb.at[i, q], ry_s.at[i, q], ry_r.at[i, q], across)

        def raw_copy(q):
            return remote(
                rb.at[rows(buddy, 1 - y, q), :], raw.at[q], rw_s.at[q], rw_r.at[q], on_line(buddy)
            )

        def hop(i, q):
            zz = dest[i]
            nz = jnp.where(zz > z, z + 1, z - 1)
            slot = jnp.where((nz == zz) & (z > zz), NZ, zz)
            return remote(yb.at[i, q], inb.at[slot, q], rz_s.at[i, q], rz_r.at[slot, q], on_line(nz))

        def piece(i):
            return pl.ds(pl.multiple_of(dest[i] * (2 * CH), 16), 2 * CH)
    else:
        def piece(i):
            return pl.ds(i * (3 * D // NZ), 3 * D // NZ)

    def finish(k, i):
        n3 = 3 * D // NZ // 3
        if i == 0:
            wait_factors(k)
        if k == 0:
            r = piece(i)
            rb[r, :] = all_units(0, r, 0).astype(BF)
        else:
            for h in range(3):
                blk = (dest[i] if fused else i) * 3 + h
                r = pl.ds(pl.multiple_of(blk * n3, 16), n3)
                rb[r, :] = all_units(1, r, blk * n3 // D).astype(BF)
        if fused and i < NZ - 1:
            def to_buddy():
                for q in range(HALF):
                    raw_copy(q).start()

            def halves():
                for q in range(HALF):
                    y_copy(i, q).start()

            when(dest[i] == buddy, to_buddy)
            when(dest[i] != buddy, halves)
            for q in range(HALF, SUB):
                y_copy(i, q).start()

    def finish_rest(k):
        for i in range(1, NZ):
            finish(k, i)

    def y_copy_x(u):
        return remote(ys.at[u], X.at[u], y_s.at[u], y_r.at[u], other)

    def fo_copy(u):
        return remote(ys.at[u], fob.at[u // 3], fo_s.at[u // 3], fo_r.at[u // 3], other)

    def g_copy(u):
        return remote(gx.at[u], G.at[u], g_s.at[u], g_r.at[u], other)

    def ig_copy(u):
        return remote(gx.at[u], igb.at[u - 1], ig_s.at[u - 1], ig_r.at[u - 1], other)

    def share(u):
        def factors0():
            for c in range(3):
                mr_copy(1, u, c).start()

        when(e == 0, factors0)
        when((e == 1) & ((L == 1) | (u > 0)), lambda: mr_copy(0, u, 0).start())

    def lend():
        wait_local(0)
        x_copy.wait_recv()
        mr[0, 0] = ln_rows(U["an"][3].astype(F32), lga[...], lba[...])[2]
        U["qkv"][3] = dotf(mr[0, 0], wa[...]).astype(BF)
        q_copy.start()
        send_from(0, 1)
        own_projection()

    def borrow():
        wait_local(1)
        first["norm_a"]()
        q_copy.wait_recv()

    def opening():
        when(e == 0, lend)
        per_core(wait_rows)
        when(e == 1, borrow)
        for name in ("flip", "scores", "mix_values"):
            first[name]()
        for c, name in enumerate(("mixed", "act", "branch")):
            when(e == 0, lambda c=c: wait_third(1, c))
            first[name]()
            if name == "mixed":
                first["norm_f"]()
        y_copy_x(0).start()
        share(0)
        other_bias()
        when(e == 0, q_copy.wait_send)
        when(e == 1, x_copy.wait_send)
        when(e == 1, lambda: wait_all(1))

    def after_forward(u):
        share(u)

        def keep():
            fob[u - 1] = ys[u]

        when((L == 1) & ((u == 1) | (u == 2)), keep)

    def forward(u):
        when(L == 1, lambda: y_copy_x(u).wait_recv())
        when((L == 0) & (u < 3), lambda: tok_copy(u).wait_recv())
        for f in unit_forward(u):
            f()
        when(L == 0, lambda: y_copy_x(u).start())
        when((L == 0) & (u == 3), lambda: cot_copy(u).start())
        after_forward(u)

    def unit_backward(u):
        S = {k: r.at[u] for k, r in U.items()}
        return backward_stages(
            G.at[u], gx.at[u], waT, wfT, (lga, lba), (lgf, lbf), hm, S,
            {"a": wta.at[u], "f": wtf.at[u]},
            glp, gb, gctx, gctxT, gqT, gsT, vec,
        )

    def after_backward(u):
        when(L == 1, lambda: g_copy(u).start())
        per_core(lambda k: mw_copy(1 - k, u).start())

    def backward(u):
        when((L == 0) & (u == 0), turn_weights)
        when(L == 1, lambda: cot_copy(u).wait_recv())
        when(L == 0, lambda: g_copy(u).wait_recv())
        for f in unit_backward(u):
            f()
        after_backward(u)
        when((L == 0) & (u > 0), lambda: ig_copy(u).start())

        def keep():
            igb[0] = gx[0]

        when((L == 0) & (u == 0), keep)

    def both_ways(u):
        y_copy_x(u + 1).wait_recv()
        when(u == 0, lambda: cot_copy(0).wait_recv())
        fs, bs = unit_forward(u + 1, ctxT, ig.at[pl.ds(0, T)]), unit_backward(u)
        for i in range(max(len(fs), len(bs))):
            for st in (bs, fs):
                if i < len(st):
                    st[i]()
        after_backward(u)
        after_forward(u + 1)

    gl_copy = remote(glp, glr, gl_s, gl_r, mate)

    def closing():
        g_copy(3).wait_recv()
        for f in unit_backward(3):
            f()
            if f.__name__ == "g_context":
                when(e == 0, lambda: mw_copy(1, 3).start())
            if f.__name__ == "g_merge":
                when(e == 1, lambda: mw_copy(0, 3).start())
                when(e == 1, lambda: finish(1, 0))
        igb[1] = gx[3]

    when(L == 0, opening)

    @pl.loop(0, 7)
    def _(i):
        is_f = jnp.where(L == 0, jnp.where((i >= 1) & (i <= 3), 1, 0), jnp.where(i == 0, 1, 0))
        is_b = jnp.where(L == 0, jnp.where(i >= 4, 1, 0), jnp.where(i == 4, 1, 0))
        when(is_f == 1, lambda: forward(i))
        when((L == 1) & (i >= 1) & (i <= 3), lambda: both_ways(i - 1))
        when(is_b == 1, lambda: backward(jnp.where(L == 0, i - 4, 3)))

    when(L == 0, closing)
    gl_copy.start()
    when(e == 0, lambda: finish(0, 0))
    when((e == 1) & (L == 1), lambda: finish(1, 0))
    gl_copy.wait()
    glr[...] = glp[...] + glr[...]
    if fused:
        gy_copy = remote(glr, gy, rg_s.at[0], rg_r.at[0], across)
        gy_copy.start()
    per_core(finish_rest)

    def send_fo():
        for u in (0, 3):
            fo_copy(u).start()

    when(L == 1, send_fo)
    emits = []

    def bring():
        def bring0():
            for u in (0, 3):
                fo_copy(u).wait_recv()

        def bring1():
            for u in (1, 2):
                ig_copy(u).wait_recv()

        when(L == 0, bring0)
        when(L == 1, bring1)
        fo[...] = dotf(rinv[...], fob[...].reshape(R, D)).astype(BF)
        ig[...] = dotf(rinv[...], igb[...].reshape(R, D))
        emits.extend([pltpu.make_async_copy(fo, fo_hbm, o_s.at[0]), pltpu.make_async_copy(ig, ig_hbm, o_s.at[1])])
        for c in emits:
            c.start()

    if fused:
        def own_y():
            for q in range(SUB):
                if q < HALF:
                    raw_copy(q).wait()
                    r = rows(z, 1 - y, q)
                    rb[r, :] = (rb[r, :].astype(F32) + raw[q].astype(F32)).astype(BF)
                y_copy(NZ - 1, q).start()

        def arrived(slot, q):
            remote(yb.at[0, q], inb.at[slot, q], rz_s.at[0, q], rz_r.at[slot, q], across).wait_recv()

        for i in range(NZ - 1):
            zz = dest[i]
            for q in range(SUB):
                mine = rb.at[rows(zz, y, q), :]

                def combine(i=i, q=q, mine=mine):
                    y_copy(i, q).wait_recv()
                    yb[i, q] = (mine[...].astype(F32) + yb[i, q].astype(F32)).astype(BF)

                def plain(i=i, q=q, mine=mine):
                    yb[i, q] = mine[...]

                def add_in(i=i, q=q, zz=zz):
                    arrived(zz, q)
                    yb[i, q] = (yb[i, q].astype(F32) + inb[zz, q].astype(F32)).astype(BF)

                if q < HALF:
                    when(zz != buddy, combine)
                    when(zz == buddy, plain)
                else:
                    combine()
                when(jnp.where(zz > z, z > 0, z < NZ - 1), add_in)
                hop(i, q).start()
            if i == 0:
                gy_copy.wait()
                gl2 = glr[...] + gy[...]
                gn[...] = gl2
                gz_copies = [
                    remote(gn, gz.at[NZ - t - 1], rg_s.at[t], rg_r.at[NZ - t], on_line(lax.rem(z + t, NZ)))
                    for t in range(1, NZ)
                ]
                for c in gz_copies:
                    c.start()
            if i == NZ - 3:
                own_y()
        bring()
        for c in gz_copies:
            c.wait_send()
        for k in range(NZ - 1):
            remote(gn, gz.at[k], rg_s.at[0], rg_r.at[k + 1], across).wait_recv()
        gl3 = gl2 + gz[0] + gz[1] + gz[2]
        part = D // (2 * NZ)
        for k in range(2 * NZ):
            def own_part(k=k):
                for j in range(2):
                    v = gl3[:, k * part:(k + 1) * part]
                    norms[j][...] = jnp.where(e == 0, v[j:j + 1, :], v[2 + j:3 + j, :])

            when(d == k, own_part)
        emits.extend(pltpu.make_async_copy(norms[j], norms_hbm[j], n_s.at[j]) for j in range(2))
        for c in emits[-2:]:
            c.start()
        w_copies = []
        for q in range(SUB):
            acc[q] = rb[rows(z, y, q), :].astype(F32)

            def from_left(q=q):
                arrived(z, q)
                acc[q] += inb[z, q].astype(F32)

            def from_right(q=q):
                arrived(NZ, q)
                acc[q] += inb[NZ, q].astype(F32)

            when(z > 0, from_left)
            when(z < NZ - 1, from_right)
            y_copy(NZ - 1, q).wait_recv()
            acc[q] += yb[NZ - 1, q].astype(F32)
            w_copies.append(pltpu.make_async_copy(acc.at[q], w_hbm.at[pl.ds(q * SR, SR)], o_s.at[2 + q]))
            w_copies[-1].start()
        for i in range(NZ):
            for q in range(SUB):
                if q < HALF and i < NZ - 1:
                    when(dest[i] != buddy, lambda i=i, q=q: y_copy(i, q).wait_send())
                else:
                    y_copy(i, q).wait_send()
                if i < NZ - 1:
                    hop(i, q).wait_send()
    else:
        bring()
        emits.append(pltpu.make_async_copy(glr, norms_hbm[0], n_s.at[0]))
        emits[-1].start()
        w_copies = [pltpu.make_async_copy(rb, w_hbm, o_s.at[2])]
        w_copies[0].start()
    for c in emits + w_copies:
        c.wait()

    def close_weights(k):
        for j in range(5):
            w_rem(k, j).wait_send()

    per_core(close_weights)
    def gave0():
        for u in range(4):
            mw_copy(1, u).wait_send()
            for c in range(3):
                mr_copy(1, u, c).wait_send()

    def gave1():
        for u in range(4):
            mw_copy(0, u).wait_send()
            if u == 0:
                when(L == 1, lambda: mr_copy(0, 0, 0).wait_send())
            else:
                mr_copy(0, u, 0).wait_send()

    when(e == 0, gave0)
    when(e == 1, gave1)
    for u in (1, 2):
        tok_copy(u).wait_send()

    def close0():
        for u in range(4):
            y_copy_x(u).wait_send()
        for u in (1, 2):
            ig_copy(u).wait_send()

    def close1():
        for u in range(4):
            g_copy(u).wait_send()
        for u in (0, 3):
            fo_copy(u).wait_send()

    when(L == 0, close0)
    when(L == 1, close1)


def relay(fused, tok, cot, w, gain, bias, mol, key):
    R, D = tok.shape
    V = pl.BlockSpec(memory_space=pltpu.VMEM)
    dma, vm = pltpu.SemaphoreType.DMA, pltpu.VMEM
    scratch = [vm((4,) + sh, dt) for sh, dt in unit_shapes(D)] + [
        vm((D, 3 * D), BF), vm((D, 3 * D), BF), vm((3 * D, D), BF), vm((3 * D, D), BF),
        vm((1, D), F32), vm((1, D), F32), vm((1, D), F32), vm((1, D), F32),
        vm((1, R), I32), vm((1, R), I32), vm((R, R), BF), vm((16, 256), BF), vm((4, T, T), F32),
        vm((4, T, D), BF), vm((4, T, D), BF), vm((2, T, D), BF), vm((4, T, D), BF), vm((4, T, D), BF),
        vm((2, T, D), BF), vm((2, T, D), BF),
        vm((4, 3 * D, T), BF), vm((4, 3 * D, T), BF), vm((4, 3 * D, T), BF), vm((4, 3, T, D), BF),
        vm((3 * D, D), BF), vm((8, D), F32), vm((8, D), F32),
        vm((D, T), F32), vm((T, D), F32), vm((T, D), BF), vm((T, D), BF), vm((D, T), BF),
        vm((3 * D, T), F32), vm((HEADS, T, T), BF),
        dma((3,)), dma((3,)), dma((3,)), dma((2,)), dma((2,)), dma((2,)), dma((2,)), dma((2,)), dma((2,)),
        dma((4,)), dma((4,)), dma((2,)), dma((2,)), dma((4,)), dma((4,)), dma((2,)), dma((2,)),
        dma((4,)), dma((4,)), dma((4, 3)), dma((4, 3)), dma, dma, dma, dma, dma, dma, vm((R, D), BF), vm((R, D), F32), dma((2 + SUB,)),
        vm((R, D), BF), vm((R, D), BF), vm((1, R), I32), vm((1, R), I32), dma((4,)), dma((2,)),
    ]
    if fused:
        CH = 3 * D // (2 * NZ)
        SR = CH // SUB
        scratch += [
            vm((NZ, SUB, SR, D), BF), vm((NZ + 1, SUB, SR, D), BF), vm((HALF, SR, D), BF),
            vm((SUB, SR, D), F32), vm((8, D), F32), vm((NZ - 1, 8, D), F32), vm((8, D), F32),
            vm((1, D // (2 * NZ)), F32), vm((1, D // (2 * NZ)), F32),
            dma((NZ, SUB)), dma((NZ, SUB)), dma((NZ - 1, SUB)), dma((NZ + 1, SUB)),
            dma((HALF,)), dma((HALF,)), dma((NZ,)), dma((NZ,)),
        ]
        outs = [jax.ShapeDtypeStruct((CH, D), F32)] + [jax.ShapeDtypeStruct((1, D // (2 * NZ)), F32)] * 2
    else:
        outs = [jax.ShapeDtypeStruct((3 * D, D), BF), jax.ShapeDtypeStruct((8, D), F32)]
    A = pl.BlockSpec(memory_space=pl.ANY)
    return pl.pallas_call(
        lambda *refs: relay_kernel(fused, *refs),
        out_shape=[jax.ShapeDtypeStruct((R, D), BF), jax.ShapeDtypeStruct((R, D), F32)] + outs,
        in_specs=[A] * 7,
        out_specs=[A] * (2 + len(outs)),
        scratch_shapes=scratch,
        compiler_params=pltpu.CompilerParams(
            collective_id=0, has_side_effects=True, vmem_limit_bytes=64 << 20
        ),
        name="relay",
    )(tok, cot, w, gain, bias, mol, key)


def emit_kernel(*refs):
    n = len(refs) // 3
    sems = refs[-1]
    ins = [pltpu.make_async_copy(refs[i], refs[2 * n + i], sems.at[0, i]) for i in range(n)]
    outs = [pltpu.make_async_copy(refs[2 * n + i], refs[n + i], sems.at[1, i]) for i in range(n)]
    for c in ins:
        c.start()
    for a, b in zip(ins, outs):
        a.wait()
        b.start()
    for c in outs:
        c.wait()


def emit(arrays):
    A = pl.BlockSpec(memory_space=pl.ANY)
    n = len(arrays)
    return pl.pallas_call(
        emit_kernel,
        out_shape=[jax.ShapeDtypeStruct(a.shape, a.dtype) for a in arrays],
        in_specs=[A] * n,
        out_specs=[A] * n,
        scratch_shapes=[pltpu.VMEM(a.shape, a.dtype) for a in arrays] + [pltpu.SemaphoreType.DMA((2, n))],
        name="emit",
    )(*arrays)


def shards(tokens, cotangent, section_weight, norm_gain, norm_bias, mol_ids, key_mask):
    fused = lax.axis_size("dp") == 2 * NZ
    got = relay(fused, tokens, cotangent, section_weight[0], norm_gain, norm_bias, mol_ids, key_mask)
    if fused:
        fo, ig, gw, gg, gb = emit(got)
        return fo, ig, gw.T[None], gg, gb
    fo, ig, gw, gn = got
    e = lax.rem(lax.axis_index("section"), 2)
    gn = lax.dynamic_slice_in_dim(gn, 2 * e, 2, 0)
    gw = lax.psum_scatter(gw, "dp", scatter_dimension=0, tiled=True)
    gn = lax.psum_scatter(gn, "dp", scatter_dimension=1, tiled=True)
    return fo, ig, gw.astype(F32).T[None], gn[0:1], gn[1:2]


def solution(mesh):
    return jax.shard_map(
        shards,
        mesh=mesh,
        in_specs=(
            P(("dp", "section"), None),
            P(("dp", "section"), None),
            P("section", None, None),
            P("section", None),
            P("section", None),
            P(("dp", "section"), None),
            P(("dp", "section"), None),
        ),
        out_specs=(
            P(("dp", "section"), None),
            P(("dp", "section"), None),
            P("section", None, "dp"),
            P("section", "dp"),
            P("section", "dp"),
        ),
        check_vma=False,
    )
```

```python
import jax
import jax.numpy as jnp
from jax import lax
from jax.experimental import pallas as pl
from jax.experimental.pallas import tpu as pltpu
from jax.sharding import PartitionSpec as P

HEADS = 32
HS = 24
EPS = 1e-5
NEG = -1e30
BF = jnp.bfloat16
F32 = jnp.float32
I32 = jnp.int32
MESH = pl.DeviceIdType.MESH
GELU_A = 0.7978845608028654
GELU_B = 0.044715
LOG2E = 1.4426950408889634
T = 128


def dotf(a, b):
    return jnp.dot(a, b, preferred_element_type=F32)


def dot_t(a, b):
    return lax.dot_general(a, b, (((1,), (1,)), ((), ())), preferred_element_type=F32)


def at(i, n):
    return pl.ds(pl.multiple_of(i * n, n), n)


HEAD_WIN = (0,) * 10 + (1,) * 6


def ln_rows(x, g, b):
    c = x - jnp.mean(x, axis=-1, keepdims=True)
    r = lax.rsqrt(jnp.mean(c * c, axis=-1, keepdims=True) + EPS)
    xh = c * r
    return xh, r, (xh * g + b).astype(BF)


def windows(ref, rows, base):
    return [ref[rows, base + 128 * w:base + 128 * w + 256] for w in (0, 1)]


def put_heads(ref, base, j, v):
    ref[base + 48 * j:base + 48 * j + 24, :] = v[0:24, 0:T]
    ref[base + 48 * j + 24:base + 48 * j + 48, :] = v[24:48, T:2 * T]


def two(ref, i, axis):
    return jnp.concatenate([ref[i], ref[i + 1]], axis=axis)


def forward_stages(x, y, wa, wf, lna, lnf, mb, hm, S, ctxT, vec):
    D = x.shape[1]

    def norm_a():
        S["xha"][...], S["ra"][...], S["an"][...] = ln_rows(x[...].astype(F32), lna[0][...], lna[1][...])

    def project():
        S["qkv"][...] = dotf(S["an"][...], wa[...]).astype(BF)

    def flip():
        S["qkvT"][...] = S["qkv"][...].T

    def scores():
        bias = mb[...]
        for g in range(2):
            base = g * 384
            qw = windows(S["qkv"], slice(None), base)
            kw = windows(S["qkv"], slice(None), D + base)
            for h in range(16):
                w = HEAD_WIN[h]
                s = dot_t(kw[w] * hm[h:h + 1, :], qw[w]) * (HS ** -0.5 * LOG2E) + bias
                ex = jnp.exp2(s - jnp.max(s, axis=0, keepdims=True))
                S["pT"][g * 16 + h] = (ex * (1.0 / jnp.sum(ex, axis=0, keepdims=True))).astype(BF)

    def mix_values():
        for g in range(2):
            base = g * 384
            for j in range(8):
                vt = S["qkvT"][2 * D + base + 48 * j:2 * D + base + 48 * j + 48, :]
                put_heads(ctxT, base, j, dotf(vt, two(S["pT"], g * 16 + 2 * j, 1)))

    def mixed():
        S["cfa"][0] = ctxT[...].astype(BF).T
        vec[...] = x[...].astype(F32) + dotf(S["cfa"][0], wf[:, 0:D])

    def norm_f():
        S["xhf"][...], S["rf"][...], S["cfa"][1] = ln_rows(vec[...], lnf[0][...], lnf[1][...])

    def act():
        u = dotf(S["cfa"][1], wf[:, D:2 * D])
        u2 = u * u
        h = 0.5 + 0.5 * jnp.tanh(GELU_A * u * (1.0 + GELU_B * u2))
        a = u * h
        S["cfa"][2] = a.astype(BF)
        S["gp"][...] = h + a * (1.0 - h) * (2 * GELU_A + 6 * GELU_A * GELU_B * u2)

    def branch():
        br = dotf(S["cfa"][2], wf[:, 2 * D:3 * D]).astype(BF).astype(F32)
        y[...] = (vec[...].astype(BF).astype(F32) + br).astype(BF)

    return [norm_a, project, flip, scores, mix_values, mixed, norm_f, act, branch]


def backward_stages(G, gx, waT, wfT, lna, lnf, hm, S, W, glp, gb, gctx, gctxT, gqT, gsT, vec):
    D = G.shape[1]

    def ln_back(gref, xh, r, g, gi, resid, out):
        gn = gref[...]
        x = xh[...]
        gg = gn * g
        m1 = jnp.mean(gg, axis=-1, keepdims=True)
        m2 = jnp.mean(gg * x, axis=-1, keepdims=True)
        out[...] = (r[...] * (gg - m1 - x * m2) + resid[...].astype(F32)).astype(BF)
        glp[gi:gi + 1, :] += jnp.sum(gn * x, axis=0, keepdims=True)
        glp[gi + 1:gi + 2, :] += jnp.sum(gn, axis=0, keepdims=True)

    def g_act():
        W["f"][2 * D:3 * D, :] = G[...].T
        gb[...] = (dotf(G[...], wfT[2 * D:3 * D, :]) * S["gp"][...]).astype(BF)

    def g_norm():
        W["f"][D:2 * D, :] = gb[...].T
        vec[...] = dotf(gb[...], wfT[D:2 * D, :])

    def g_hidden():
        ln_back(vec, S["xhf"], S["rf"], lnf[0][...], 2, G, gb)

    def g_context():
        W["f"][0:D, :] = gb[...].T
        t = dotf(gb[...], wfT[0:D, :]).astype(BF)
        gctx[...] = t
        gctxT[...] = t.T

    def g_scores():
        for g in range(2):
            base = g * 384
            vw = windows(S["qkv"], slice(None), 2 * D + base)
            gw = windows(gctx, slice(None), base)
            for h in range(16):
                w = HEAD_WIN[h]
                gp = dot_t(vw[w] * hm[h:h + 1, :], gw[w])
                p = S["pT"][g * 16 + h].astype(F32)
                d = jnp.sum(p * gp, axis=0, keepdims=True)
                gsT[g * 16 + h] = (p * (gp - d)).astype(BF)

    def g_heads():
        for g in range(2):
            base = g * 384
            for j in range(8):
                i = g * 16 + 2 * j
                at48 = slice(base + 48 * j, base + 48 * j + 48)
                put_heads(gqT, 2 * D + base, j, dot_t(gctxT[at48, :], two(S["pT"], i, 0)))
                put_heads(gqT, D + base, j, dot_t(S["qkvT"][at48, :], two(gsT, i, 0)) * HS ** -0.5)
                k48 = slice(D + base + 48 * j, D + base + 48 * j + 48)
                put_heads(gqT, base, j, dotf(S["qkvT"][k48, :], two(gsT, i, 1)) * HS ** -0.5)

    def g_merge():
        t = gqT[...].astype(BF)
        W["a"][...] = t
        S["qkv"][...] = t.T

    def g_input():
        vec[...] = dotf(S["qkv"][...], waT[...])

    def g_x():
        ln_back(vec, S["xha"], S["ra"], lna[0][...], 0, gb, gx)

    return [g_act, g_norm, g_hidden, g_context, g_scores, g_heads, g_merge, g_input, g_x]


def remote(src, dst, ss, rs, dev):
    return pltpu.make_async_remote_copy(
        src_ref=src, dst_ref=dst, send_sem=ss, recv_sem=rs, device_id=dev, device_id_type=MESH
    )


def when(cond, fn):
    pl.when(cond)(fn)


NZ = 4
SUB = 3
HALF = 1
ORDER = ((3, 2, 1, 0), (3, 0, 2, 1), (0, 3, 1, 2), (0, 1, 2, 3))


def by_place(vals, z):
    r = vals[-1]
    for i in range(len(vals) - 2, -1, -1):
        r = jnp.where(z == i, vals[i], r)
    return r


def rotation(mol, R):
    c0 = jnp.sum((mol == 0).astype(I32), axis=1, keepdims=True)
    c1 = jnp.sum((mol == 1).astype(I32), axis=1, keepdims=True)
    start = jnp.where(c0 == T, 0, jnp.where(c1 == T, c0, c0 + c1))
    i0 = lax.broadcasted_iota(I32, (R, R), 0)
    i1 = lax.broadcasted_iota(I32, (R, R), 1)

    def onehot(a, b):
        t = a + start
        t = jnp.where(t >= R, t - R, t)
        return jnp.where(t == b, 1.0, 0.0).astype(BF)

    return onehot(i0, i1), onehot(i1, i0)


def pair_bias(mol, key, rot, out, mine, R):
    mk = jnp.concatenate([mol, key, jnp.zeros((6, R), I32)], axis=0).astype(F32).astype(BF)
    row = dot_t(mk, rot)
    col = dot_t(rot, mk)
    k0 = lax.broadcasted_iota(I32, (T, T), 0)
    q0 = lax.broadcasted_iota(I32, (T, T), 1)
    for b in range(R // T):
        rs = slice(b * T, b * T + T)
        ok = (col[rs, 0:1] == row[0:1, rs]) & ((col[rs, 1:2] > 0.5) | (k0 == q0))
        out[jnp.where(mine == 0, 3 * b, 1 + b)] = jnp.where(ok, 0.0, NEG)


UNIT = ("xha", "ra", "an", "qkv", "qkvT", "pT", "xhf", "rf", "cfa", "gp")


def unit_shapes(D):
    return (
        ((T, D), F32), ((T, 1), F32), ((T, D), BF), ((T, 3 * D), BF), ((3 * D, T), BF),
        ((HEADS, T, T), BF), ((T, D), F32), ((T, 1), F32), ((3, T, D), BF), ((T, D), F32),
    )


def relay_kernel(fused, tok_hbm, cot_hbm, w, gain, bias, mol_hbm, key_hbm, fo, ig, w_out, *scr):
    R, D = tok_hbm.shape
    norms, scr = scr[:1], scr[1:]
    n = len(UNIT)
    U = {k: r for k, r in zip(UNIT, scr[:n])}
    (
        wa, wf, waT, wfT, lga, lba, lgf, lbf, molo, keyo, rinv, hm, mb, X, G, ex, ys, gx, fob, igb,
        wta, wtf, mw, mr, rb, glp, glr, ctxT, vec, gb, gctx, gctxT, gqT, gsT,
        wl_s, w_s, w_r, l_s, l_r, m_s, m_r, ex_s, ex_r, y_s, y_r, fo_s, fo_r, g_s, g_r, ig_s, ig_r,
        mw_s, mw_r, mr_s, mr_r, x_s, x_r, q_s, q_r, gl_s, gl_r, tok, cot, mol, key, i_s,
    ) = scr[n:n + 66]
    s = lax.axis_index("section")
    e = lax.rem(s, 2)
    L = s // 2
    mate = {"section": s + 1 - 2 * e}
    other = {"section": s + 2 - 4 * L}
    d = lax.axis_index("dp")
    z = d // 2
    y = d - 2 * z
    across = {"dp": d + 1 - 2 * y}

    def on_line(zz):
        return {"dp": zz * 2 + y}

    bar = pltpu.get_barrier_semaphore()
    peers = [mate, other]
    if fused:
        peers += [across] + [on_line(lax.rem(z + t, NZ)) for t in range(1, NZ)]
    for p in peers:
        pl.semaphore_signal(bar, inc=1, device_id=p, device_id_type=MESH)

    own = ((wa, lga, lba), (wf, lgf, lbf))

    def per_core(fn):
        when(e == 0, lambda: fn(0))
        when(e == 1, lambda: fn(1))

    def third(c):
        return (slice(None), pl.ds(c * D, D))

    def w_local(k, j):
        src = (w, gain, bias)[j]
        return pltpu.make_async_copy(src, own[k][j], wl_s.at[j])

    def w_rem(k, j):
        if j < 3:
            return remote(w.at[third(j)], own[k][0].at[third(j)], w_s.at[j], w_r.at[j], mate)
        src = (gain, bias)[j - 3]
        return remote(src, own[k][j - 2], l_s.at[j - 3], l_r.at[j - 3], mate)

    def start_local(k):
        for j in range(3):
            w_local(k, j).start()

    def wait_local(k):
        for j in range(3):
            w_local(k, j).wait()

    inputs = [
        pltpu.make_async_copy(a, b, i_s.at[i])
        for i, (a, b) in enumerate(((mol_hbm, mol), (key_hbm, key), (tok_hbm, tok), (cot_hbm, cot)))
    ]
    for c in inputs:
        c.start()
    per_core(start_local)
    inputs[0].wait()
    inputs[1].wait()
    rot, inv = rotation(mol[...], R)
    inputs[2].wait()
    xu = dotf(rot, tok[...]).astype(BF).reshape(2, T, D)

    def rows0():
        X[0] = xu[0]
        X[3] = xu[1]

    def rows1():
        ex[...] = xu

    when(L == 0, rows0)
    when(L == 1, rows1)

    def unit_forward(u, heads=None, rows=None):
        S = {k: r.at[u] for k, r in U.items()}
        return forward_stages(
            X.at[u], ys.at[u], wa, wf, (lga, lba), (lgf, lbf), mb.at[u], hm, S,
            gqT.at[pl.ds(0, D)] if heads is None else heads, vec if rows is None else rows,
        )

    first = {f.__name__: f for f in unit_forward(0)}

    def own_projection():
        first["norm_a"]()
        first["project"]()

    pl.semaphore_wait(bar, len(peers))

    x_copy = remote(X.at[0], U["an"].at[3], x_s, x_r, mate)
    q_copy = remote(U["qkv"].at[3], U["qkv"].at[0], q_s, q_r, mate)
    mol_copy = remote(mol, molo, m_s.at[0], m_r.at[0], other)
    key_copy = remote(key, keyo, m_s.at[1], m_r.at[1], other)

    def cot_copy(u):
        return remote(ex.at[u // 3], G.at[u], ex_s.at[u // 3], ex_r.at[u // 3], other)

    def tok_copy(u):
        return remote(ex.at[u - 1], X.at[u], ex_s.at[u - 1], ex_r.at[u - 1], other)

    def send_rows(k):
        for j in (3, 4):
            w_rem(k, j).start()

    def send_thirds(k):
        for j in range(3):
            w_rem(k, j).start()

    def send_from(k, c):
        for j in range(c, 3):
            w_rem(k, j).start()

    def wait_rows(k):
        for j in (3, 4):
            w_rem(1 - k, j).wait_recv()

    def wait_third(k, c):
        w_rem(k, c).wait_recv()

    def wait_all(k):
        for c in range(3):
            wait_third(1 - k, c)

    when((L == 0) & (e == 1), x_copy.start)
    per_core(send_rows)
    when((L == 1) & (e == 0), lambda: send_thirds(0))
    when((L == 0) & (e == 0), lambda: w_rem(0, 0).start())
    when(e == 1, lambda: send_thirds(1))
    mol_copy.start()
    key_copy.start()

    def toks():
        tok_copy(1).start()
        tok_copy(2).start()

    when(L == 1, toks)
    rinv[...] = inv
    inputs[3].wait()
    cu = dotf(rot, cot[...]).astype(BF).reshape(2, T, D)

    def cots0():
        ex[...] = cu
        cot_copy(0).start()

    def cots1():
        G[1:3] = cu

    when(L == 0, cots0)
    when(L == 1, cots1)
    i0 = lax.broadcasted_iota(I32, (16, 256), 0)
    i1 = lax.broadcasted_iota(I32, (16, 256), 1)
    lo = HS * i0 - jnp.where(i0 < 10, 0, 128)
    hm[...] = jnp.where((i1 >= lo) & (i1 < lo + HS), 1.0, 0.0).astype(BF)
    glp[...] = jnp.zeros_like(glp)
    pair_bias(mol[...], key[...], rot, mb, L, R)

    def turn_weights():
        @pl.loop(0, 3)
        def _(i):
            cs = at(i, D)
            waT[cs, :] = wa[:, cs].T
            wfT[cs, :] = wf[:, cs].T

    def other_bias():
        mol_copy.wait()
        key_copy.wait()
        rot_o, _ = rotation(molo[...], R)
        pair_bias(molo[...], keyo[...], rot_o, mb, 1 - L, R)

    def ready1():
        other_bias()
        per_core(wait_local)
        per_core(wait_rows)
        per_core(wait_all)
        turn_weights()

    when(L == 1, ready1)

    def mw_copy(k, u):
        return remote((wta, wtf)[k].at[u], mw.at[u], mw_s.at[u], mw_r.at[u], mate)

    def mr_copy(k, u, c):
        src = (U["an"].at[u], U["cfa"].at[u, c])[k]
        return remote(src, mr.at[u, c], mr_s.at[u, c], mr_r.at[u, c], mate)

    def mine(k, u, r, c):
        left = jnp.concatenate([(wta, wtf)[k][u, r, :], mw[u, r, :]], axis=1)
        right = jnp.concatenate([U["an"][u] if k == 0 else U["cfa"][u, c], mr[u, c]], axis=0)
        return left, right

    def all_units(k, r, c):
        parts = [mine(k, u, r, c) for u in range(4)]
        return dotf(
            jnp.concatenate([a for a, _ in parts], axis=1), jnp.concatenate([b for _, b in parts], axis=0)
        )

    def wait_factors(k):
        for u in range(4):
            mw_copy(k, u).wait_recv()
            for c in range(1 if k == 0 else 3):
                if k == 0 and u == 0:
                    when(L == 1, lambda: mr_copy(0, 0, 0).wait_recv())
                else:
                    mr_copy(1, u, c).wait_recv()

    if fused:
        yb, inb, raw, gy, gz, gn, ry_s, ry_r, rz_s, rz_r, rw_s, rw_r, rg_s, rg_r = scr[n + 66:]
        acc = w_out
        CH = 3 * D // (2 * NZ)
        SR = CH // SUB
        dest = [by_place([ORDER[k][i] for k in range(NZ)], z) for i in range(NZ)]
        buddy = z + 1 - 2 * lax.rem(z, 2)

        def rows(zz, yy, q):
            return pl.ds(pl.multiple_of((zz * 2 + yy) * CH + q * SR, 16), SR)

        def y_copy(i, q):
            return remote(rb.at[rows(dest[i], 1 - y, q), :], yb.at[i, q], ry_s.at[i, q], ry_r.at[i, q], across)

        def raw_copy(q):
            return remote(
                rb.at[rows(buddy, 1 - y, q), :], raw.at[q], rw_s.at[q], rw_r.at[q], on_line(buddy)
            )

        def hop(i, q):
            zz = dest[i]
            nz = jnp.where(zz > z, z + 1, z - 1)
            slot = jnp.where((nz == zz) & (z > zz), NZ, zz)
            return remote(yb.at[i, q], inb.at[slot, q], rz_s.at[i, q], rz_r.at[slot, q], on_line(nz))

        def piece(i):
            return pl.ds(pl.multiple_of(dest[i] * (2 * CH), 16), 2 * CH)
    else:
        def piece(i):
            return pl.ds(i * (3 * D // NZ), 3 * D // NZ)

    def finish(k, i):
        n3 = 3 * D // NZ // 3
        if i == 0:
            wait_factors(k)
        if k == 0:
            r = piece(i)
            rb[r, :] = all_units(0, r, 0).astype(BF)
        else:
            for h in range(3):
                blk = (dest[i] if fused else i) * 3 + h
                r = pl.ds(pl.multiple_of(blk * n3, 16), n3)
                rb[r, :] = all_units(1, r, blk * n3 // D).astype(BF)
        if fused and i < NZ - 1:
            def to_buddy():
                for q in range(HALF):
                    raw_copy(q).start()

            def halves():
                for q in range(HALF):
                    y_copy(i, q).start()

            when(dest[i] == buddy, to_buddy)
            when(dest[i] != buddy, halves)
            for q in range(HALF, SUB):
                y_copy(i, q).start()

    def finish_rest(k):
        for i in range(1, NZ):
            finish(k, i)

    def y_copy_x(u):
        return remote(ys.at[u], X.at[u], y_s.at[u], y_r.at[u], other)

    def fo_copy(u):
        return remote(ys.at[u], fob.at[u // 3], fo_s.at[u // 3], fo_r.at[u // 3], other)

    def g_copy(u):
        return remote(gx.at[u], G.at[u], g_s.at[u], g_r.at[u], other)

    def ig_copy(u):
        return remote(gx.at[u], igb.at[u - 1], ig_s.at[u - 1], ig_r.at[u - 1], other)

    def share(u):
        def factors0():
            for c in range(3):
                mr_copy(1, u, c).start()

        when(e == 0, factors0)
        when((e == 1) & ((L == 1) | (u > 0)), lambda: mr_copy(0, u, 0).start())

    def lend():
        wait_local(0)
        x_copy.wait_recv()
        mr[0, 0] = ln_rows(U["an"][3].astype(F32), lga[...], lba[...])[2]
        U["qkv"][3] = dotf(mr[0, 0], wa[...]).astype(BF)
        q_copy.start()
        send_from(0, 1)
        own_projection()

    def borrow():
        wait_local(1)
        first["norm_a"]()
        q_copy.wait_recv()

    def opening():
        when(e == 0, lend)
        per_core(wait_rows)
        when(e == 1, borrow)
        for name in ("flip", "scores", "mix_values"):
            first[name]()
        for c, name in enumerate(("mixed", "act", "branch")):
            when(e == 0, lambda c=c: wait_third(1, c))
            first[name]()
            if name == "mixed":
                first["norm_f"]()
        y_copy_x(0).start()
        share(0)
        other_bias()
        when(e == 0, q_copy.wait_send)
        when(e == 1, x_copy.wait_send)
        when(e == 1, lambda: wait_all(1))

    def after_forward(u):
        share(u)

        def keep():
            fob[u - 1] = ys[u]

        when((L == 1) & ((u == 1) | (u == 2)), keep)

    def forward(u):
        when(L == 1, lambda: y_copy_x(u).wait_recv())
        when((L == 0) & (u < 3), lambda: tok_copy(u).wait_recv())
        for f in unit_forward(u):
            f()
        when(L == 0, lambda: y_copy_x(u).start())
        when((L == 0) & (u == 3), lambda: cot_copy(u).start())
        after_forward(u)

    def unit_backward(u):
        S = {k: r.at[u] for k, r in U.items()}
        return backward_stages(
            G.at[u], gx.at[u], waT, wfT, (lga, lba), (lgf, lbf), hm, S,
            {"a": wta.at[u], "f": wtf.at[u]},
            glp, gb, gctx, gctxT, gqT, gsT, vec,
        )

    def after_backward(u):
        when(L == 1, lambda: g_copy(u).start())
        per_core(lambda k: mw_copy(1 - k, u).start())

    def backward(u):
        when((L == 0) & (u == 0), turn_weights)
        when(L == 1, lambda: cot_copy(u).wait_recv())
        when(L == 0, lambda: g_copy(u).wait_recv())
        for f in unit_backward(u):
            f()
        after_backward(u)
        when((L == 0) & (u > 0), lambda: ig_copy(u).start())

        def keep():
            igb[0] = gx[0]

        when((L == 0) & (u == 0), keep)

    def both_ways(u):
        y_copy_x(u + 1).wait_recv()
        when(u == 0, lambda: cot_copy(0).wait_recv())
        fs, bs = unit_forward(u + 1, ctxT, ig.at[pl.ds(0, T)]), unit_backward(u)
        for i in range(max(len(fs), len(bs))):
            for st in (bs, fs):
                if i < len(st):
                    st[i]()
        after_backward(u)
        after_forward(u + 1)

    gl_copy = remote(glp, glr, gl_s, gl_r, mate)

    def closing():
        g_copy(3).wait_recv()
        for f in unit_backward(3):
            f()
            if f.__name__ == "g_context":
                when(e == 0, lambda: mw_copy(1, 3).start())
            if f.__name__ == "g_merge":
                when(e == 1, lambda: mw_copy(0, 3).start())
                when(e == 1, lambda: finish(1, 0))
        igb[1] = gx[3]

    when(L == 0, opening)

    @pl.loop(0, 7)
    def _(i):
        is_f = jnp.where(L == 0, jnp.where((i >= 1) & (i <= 3), 1, 0), jnp.where(i == 0, 1, 0))
        is_b = jnp.where(L == 0, jnp.where(i >= 4, 1, 0), jnp.where(i == 4, 1, 0))
        when(is_f == 1, lambda: forward(i))
        when((L == 1) & (i >= 1) & (i <= 3), lambda: both_ways(i - 1))
        when(is_b == 1, lambda: backward(jnp.where(L == 0, i - 4, 3)))

    when(L == 0, closing)
    gl_copy.start()
    when(e == 0, lambda: finish(0, 0))
    when((e == 1) & (L == 1), lambda: finish(1, 0))
    gl_copy.wait()
    glr[...] = glp[...] + glr[...]
    if fused:
        gy_copy = remote(glr, gy, rg_s.at[0], rg_r.at[0], across)
        gy_copy.start()
    per_core(finish_rest)

    def send_fo():
        for u in (0, 3):
            fo_copy(u).start()

    when(L == 1, send_fo)

    def bring():
        def bring0():
            for u in (0, 3):
                fo_copy(u).wait_recv()

        def bring1():
            for u in (1, 2):
                ig_copy(u).wait_recv()

        when(L == 0, bring0)
        when(L == 1, bring1)
        fo[...] = dotf(rinv[...], fob[...].reshape(R, D)).astype(BF)
        ig[...] = dotf(rinv[...], igb[...].reshape(R, D))

    if fused:
        def own_y():
            for q in range(SUB):
                if q < HALF:
                    raw_copy(q).wait()
                    r = rows(z, 1 - y, q)
                    rb[r, :] = (rb[r, :].astype(F32) + raw[q].astype(F32)).astype(BF)
                y_copy(NZ - 1, q).start()

        def arrived(slot, q):
            remote(yb.at[0, q], inb.at[slot, q], rz_s.at[0, q], rz_r.at[slot, q], across).wait_recv()

        for i in range(NZ - 1):
            zz = dest[i]
            for q in range(SUB):
                mine = rb.at[rows(zz, y, q), :]

                def combine(i=i, q=q, mine=mine):
                    y_copy(i, q).wait_recv()
                    yb[i, q] = (mine[...].astype(F32) + yb[i, q].astype(F32)).astype(BF)

                def plain(i=i, q=q, mine=mine):
                    yb[i, q] = mine[...]

                def add_in(i=i, q=q, zz=zz):
                    arrived(zz, q)
                    yb[i, q] = (yb[i, q].astype(F32) + inb[zz, q].astype(F32)).astype(BF)

                if q < HALF:
                    when(zz != buddy, combine)
                    when(zz == buddy, plain)
                else:
                    combine()
                when(jnp.where(zz > z, z > 0, z < NZ - 1), add_in)
                hop(i, q).start()
            if i == 0:
                gy_copy.wait()
                gl2 = glr[...] + gy[...]
                gn[...] = gl2
                gz_copies = [
                    remote(gn, gz.at[NZ - t - 1], rg_s.at[t], rg_r.at[NZ - t], on_line(lax.rem(z + t, NZ)))
                    for t in range(1, NZ)
                ]
                for c in gz_copies:
                    c.start()
            if i == NZ - 3:
                own_y()
        bring()
        for c in gz_copies:
            c.wait_send()
        for k in range(NZ - 1):
            remote(gn, gz.at[k], rg_s.at[0], rg_r.at[k + 1], across).wait_recv()
        gl3 = gl2 + gz[0] + gz[1] + gz[2]
        part = D // (2 * NZ)
        for k in range(2 * NZ):
            def own_part(k=k):
                for j in range(2):
                    v = gl3[:, k * part:(k + 1) * part]
                    norms[0][j:j + 1, :] = jnp.where(e == 0, v[j:j + 1, :], v[2 + j:3 + j, :])

            when(d == k, own_part)
        for q in range(SUB):
            acc[q] = rb[rows(z, y, q), :].astype(F32)

            def from_left(q=q):
                arrived(z, q)
                acc[q] += inb[z, q].astype(F32)

            def from_right(q=q):
                arrived(NZ, q)
                acc[q] += inb[NZ, q].astype(F32)

            when(z > 0, from_left)
            when(z < NZ - 1, from_right)
            y_copy(NZ - 1, q).wait_recv()
            acc[q] += yb[NZ - 1, q].astype(F32)
        for i in range(NZ):
            for q in range(SUB):
                if q < HALF and i < NZ - 1:
                    when(dest[i] != buddy, lambda i=i, q=q: y_copy(i, q).wait_send())
                else:
                    y_copy(i, q).wait_send()
                if i < NZ - 1:
                    hop(i, q).wait_send()
    else:
        bring()
        norms[0][...] = glr[...]
        w_out[...] = rb[...]

    def close_weights(k):
        for j in range(5):
            w_rem(k, j).wait_send()

    per_core(close_weights)
    def gave0():
        for u in range(4):
            mw_copy(1, u).wait_send()
            for c in range(3):
                mr_copy(1, u, c).wait_send()

    def gave1():
        for u in range(4):
            mw_copy(0, u).wait_send()
            if u == 0:
                when(L == 1, lambda: mr_copy(0, 0, 0).wait_send())
            else:
                mr_copy(0, u, 0).wait_send()

    when(e == 0, gave0)
    when(e == 1, gave1)
    for u in (1, 2):
        tok_copy(u).wait_send()

    def close0():
        for u in range(4):
            y_copy_x(u).wait_send()
        for u in (1, 2):
            ig_copy(u).wait_send()

    def close1():
        for u in range(4):
            g_copy(u).wait_send()
        for u in (0, 3):
            fo_copy(u).wait_send()

    when(L == 0, close0)
    when(L == 1, close1)


def relay(fused, tok, cot, w, gain, bias, mol, key):
    R, D = tok.shape
    V = pl.BlockSpec(memory_space=pltpu.VMEM)
    dma, vm = pltpu.SemaphoreType.DMA, pltpu.VMEM
    scratch = [vm((4,) + sh, dt) for sh, dt in unit_shapes(D)] + [
        vm((D, 3 * D), BF), vm((D, 3 * D), BF), vm((3 * D, D), BF), vm((3 * D, D), BF),
        vm((1, D), F32), vm((1, D), F32), vm((1, D), F32), vm((1, D), F32),
        vm((1, R), I32), vm((1, R), I32), vm((R, R), BF), vm((16, 256), BF), vm((4, T, T), F32),
        vm((4, T, D), BF), vm((4, T, D), BF), vm((2, T, D), BF), vm((4, T, D), BF), vm((4, T, D), BF),
        vm((2, T, D), BF), vm((2, T, D), BF),
        vm((4, 3 * D, T), BF), vm((4, 3 * D, T), BF), vm((4, 3 * D, T), BF), vm((4, 3, T, D), BF),
        vm((3 * D, D), BF), vm((8, D), F32), vm((8, D), F32),
        vm((D, T), F32), vm((T, D), F32), vm((T, D), BF), vm((T, D), BF), vm((D, T), BF),
        vm((3 * D, T), F32), vm((HEADS, T, T), BF),
        dma((3,)), dma((3,)), dma((3,)), dma((2,)), dma((2,)), dma((2,)), dma((2,)), dma((2,)), dma((2,)),
        dma((4,)), dma((4,)), dma((2,)), dma((2,)), dma((4,)), dma((4,)), dma((2,)), dma((2,)),
        dma((4,)), dma((4,)), dma((4, 3)), dma((4, 3)), dma, dma, dma, dma, dma, dma,
        vm((R, D), BF), vm((R, D), BF), vm((1, R), I32), vm((1, R), I32), dma((4,)),
    ]
    if fused:
        CH = 3 * D // (2 * NZ)
        SR = CH // SUB
        scratch += [
            vm((NZ, SUB, SR, D), BF), vm((NZ + 1, SUB, SR, D), BF), vm((HALF, SR, D), BF),
            vm((8, D), F32), vm((NZ - 1, 8, D), F32), vm((8, D), F32),
            dma((NZ, SUB)), dma((NZ, SUB)), dma((NZ - 1, SUB)), dma((NZ + 1, SUB)),
            dma((HALF,)), dma((HALF,)), dma((NZ,)), dma((NZ,)),
        ]
        outs = [vm((R, D), BF), vm((R, D), F32), vm((SUB, SR, D), F32)] + [vm((2, D // (2 * NZ)), F32)]
    else:
        outs = [
            jax.ShapeDtypeStruct(sh, dt)
            for sh, dt in (((R, D), BF), ((R, D), F32), ((3 * D, D), BF), ((8, D), F32))
        ]
    return pl.pallas_call(
        lambda *refs: relay_kernel(fused, *refs),
        out_shape=outs,
        in_specs=[pl.BlockSpec(memory_space=pl.ANY)] * 7,
        out_specs=[V] * len(outs),
        scratch_shapes=scratch,
        compiler_params=pltpu.CompilerParams(
            collective_id=0, has_side_effects=True, vmem_limit_bytes=(61 if fused else 64) << 20
        ),
        name="relay",
    )(tok, cot, w, gain, bias, mol, key)


def shards(tokens, cotangent, section_weight, norm_gain, norm_bias, mol_ids, key_mask):
    fused = lax.axis_size("dp") == 2 * NZ
    got = relay(fused, tokens, cotangent, section_weight[0], norm_gain, norm_bias, mol_ids, key_mask)
    if fused:
        fo, ig, gw, gn = got
        return fo, ig, gw.reshape(-1, gw.shape[-1]).T[None], gn[0:1], gn[1:2]
    fo, ig, gw, gn = got
    e = lax.rem(lax.axis_index("section"), 2)
    gn = lax.dynamic_slice_in_dim(gn, 2 * e, 2, 0)
    gw = lax.psum_scatter(gw, "dp", scatter_dimension=0, tiled=True)
    gn = lax.psum_scatter(gn, "dp", scatter_dimension=1, tiled=True)
    return fo, ig, gw.astype(F32).T[None], gn[0:1], gn[1:2]


def solution(mesh):
    return jax.shard_map(
        shards,
        mesh=mesh,
        in_specs=(
            P(("dp", "section"), None),
            P(("dp", "section"), None),
            P("section", None, None),
            P("section", None),
            P("section", None),
            P(("dp", "section"), None),
            P(("dp", "section"), None),
        ),
        out_specs=(
            P(("dp", "section"), None),
            P(("dp", "section"), None),
            P("section", None, "dp"),
            P("section", "dp"),
            P("section", "dp"),
        ),
        check_vma=False,
    )
```
